32 devices in a mesh: rep: 2 (over y), seq: 4 (over x, core), head: 4 (over z).
Axes of the slice: x: 2, y: 2, z: 4, core: 2. Of those that a mesh axis runs over, the one named last changes fastest.
Arguments:
- query: bfloat16 [32768, 2048], P(('rep', 'seq', 'head')), parts along dimension 0, may hold values from -6 to 6
- key: bfloat16 [32768, 2048], P(('rep', 'seq', 'head')), parts along dimension 0, may hold values from -6 to 6
- value: bfloat16 [32768, 2048], P(('rep', 'seq', 'head')), parts along dimension 0, may hold values from -6 to 6
- grad_out: bfloat16 [32768, 2048], P(('rep', 'seq', 'head')), parts along dimension 0, may hold values from -6 to 6
- level_weights: bfloat16 [32768, 128], P(('rep', 'seq', 'head')), parts along dimension 0, may hold values from 0.25 to 4
Outputs:
- attended: bfloat16 [32768, 2048], P(('rep', 'seq', 'head')), parts along dimension 0
- grad_query: bfloat16 [32768, 2048], P(('rep', 'seq', 'head')), parts along dimension 0
- grad_key: bfloat16 [32768, 2048], P(('rep', 'seq', 'head')), parts along dimension 0
- grad_value: bfloat16 [32768, 2048], P(('rep', 'seq', 'head')), parts along dimension 0
- grad_weights: bfloat16 [32768, 128], P(('rep', 'seq', 'head')), parts along dimension 0
The draws below stay inside these ranges and needn't reach their ends.
There are 2 independent parts, one for each index of `rep`. The reference program is written for one: setup_inputs(seed, part) draws one part's arguments, and reference() takes and returns one part's arrays. A program takes and returns all parts, laid end to end along the dimension named above; each array names one. Nothing has to cross between parts.
All inputs are finite; a program needn't handle non-finite values.
Results may differ from the reference program's by a relative error of at most 0.0056.
Values may be sent and summed in bfloat16 or wider, within the bound.
A program may use at most 384 MiB of HBM per device.

```python
import math
import jax
import jax.numpy as jnp
from jax import lax

H = 16
DH = 128
C = 128
LEVELS = 8
WIDTH = 2048
NC = 128
TOKENS = 16384


def steps_of(own_key, shape, pieces, low, top_value):
    loudness, own = 1.0, jax.random.fold_in(own_key, 6)
    for dim, shards_of in pieces:
        heights = jnp.exp(jax.random.uniform(jax.random.fold_in(own, dim), (shards_of,), jnp.float32, low / len(pieces), top_value / len(pieces)))
        loudness = loudness * jnp.repeat(heights, shape[dim] // shards_of).reshape([-1 if axis == dim else 1 for axis in range(len(shape))])
    return loudness


def scatter_about(own_key, extent, spread, limit, split=(), kind=jnp.bfloat16):
    loudness = steps_of(own_key, extent, split, -0.22, 0.18) if split else 1.0
    entries = jax.random.normal(own_key, extent, jnp.float32) * spread * loudness
    return jnp.minimum(jnp.maximum(entries, -limit), limit).astype(kind)


def setup_inputs(seed: int = 0, part: int = 0) -> dict:
    key_list = jax.random.split(jax.random.key(seed), 6)
    own_keys = jax.random.split(jax.random.fold_in(key_list[5], part), 6)
    return {
        "query": scatter_about(own_keys[0], (TOKENS, WIDTH), 1.0, 6.0, ((0, 16),)),
        "key": scatter_about(own_keys[1], (TOKENS, WIDTH), 1.0, 6.0, ((0, 16),)),
        "value": scatter_about(own_keys[2], (TOKENS, WIDTH), 1.0, 6.0, ((0, 16),)),
        "grad_out": scatter_about(own_keys[3], (TOKENS, WIDTH), 1.0, 6.0, ((0, 16),)),
        "level_weights": jnp.clip(jnp.exp(math.log(4.0) - 2.7725887 * jax.random.uniform(own_keys[4], (TOKENS, H * LEVELS), jnp.float32) ** steps_of(own_keys[4], (TOKENS, H * LEVELS), ((0, 16),), -0.2, 0.2)), 0.25, 4.0).astype(jnp.bfloat16),
    }


def level_scale(level):
    if level == 0:
        return 1.0 / math.sqrt(DH * C)
    return 1.0 / math.sqrt(DH * C * 2 ** (level - 1))

def bucket_matrix(count, level_bit):
    rows = jnp.arange(count, dtype=jnp.int32)[:, None]
    columns = jnp.arange(count, dtype=jnp.int32)[None, :]
    stride = 2 ** level_bit
    reading = rows // stride % 2 == 1
    inside = columns // stride == rows // (2 * stride) * 2
    return jnp.where(reading & inside, 1.0, 0.0).astype(jnp.float32)

def rounded(values):
    return lax.optimization_barrier(values.astype(jnp.bfloat16)).astype(jnp.float32)

def one_head(inputs):
    query, key, value, grad_out, weights = inputs
    query_full = query.astype(jnp.float32)
    key_full = key.astype(jnp.float32)
    value_full = value.astype(jnp.float32)
    grad_full = grad_out.astype(jnp.float32)
    mask = jnp.tril(jnp.ones((C, C), jnp.float32))
    scores = jnp.einsum('ntd,nsd->nts', query_full, key_full) * level_scale(0) * mask
    first = weights[:, :, 0:1]
    probs = rounded(first * scores)
    attended = jnp.einsum('nts,nsd->ntd', probs, value_full)
    grad_probs = jnp.einsum('nte,nse->nts', grad_full, value_full)
    grad_levels = [lax.optimization_barrier(jnp.sum(scores * grad_probs, axis=-1))]
    grad_scores = rounded(first * grad_probs * level_scale(0) * mask)
    grad_query = jnp.einsum('nts,nsd->ntd', grad_scores, key_full)
    grad_key = jnp.einsum('nts,ntd->nsd', grad_scores, query_full)
    grad_value = jnp.einsum('nts,nte->nse', probs, grad_full)
    states = jnp.einsum('nsd,nse->nde', key_full, value_full)
    adjoint = jnp.zeros((NC, DH, DH), jnp.float32)
    for level in range(1, LEVELS):
        mapping = bucket_matrix(NC, level - 1)
        summed = jnp.einsum('cj,jde->cde', mapping, states, precision=lax.Precision.HIGHEST)
        read_state = rounded(level_scale(level) * summed)
        reads = jnp.einsum('ntd,nde->nte', query_full, read_state)
        weight = weights[:, :, level:level + 1]
        attended = attended + weight * reads
        grad_levels.append(lax.optimization_barrier(jnp.sum(grad_full * reads, axis=-1)))
        grad_query = grad_query + weight * jnp.einsum('nte,nde->ntd', grad_full, read_state)
        weighted = rounded(weight * query_full)
        products = jnp.einsum('ntd,nte->nde', weighted, grad_full)
        adjoint = adjoint + level_scale(level) * jnp.einsum('cj,cde->jde', mapping, products, precision=lax.Precision.HIGHEST)
    adjoint_low = rounded(adjoint)
    grad_key = grad_key + jnp.einsum('nse,nde->nsd', value_full, adjoint_low)
    grad_value = grad_value + jnp.einsum('nsd,nde->nse', key_full, adjoint_low)
    return (attended.astype(jnp.bfloat16), grad_query.astype(jnp.bfloat16), grad_key.astype(jnp.bfloat16), grad_value.astype(jnp.bfloat16), jnp.stack(grad_levels, axis=-1).astype(jnp.bfloat16))

def split_heads(array, width):
    return array.reshape(NC, C, H, width).transpose(2, 0, 1, 3)

def join_heads(array):
    return array.transpose(1, 2, 0, 3).reshape(NC * C, array.shape[0] * array.shape[3])

def reference(query, key, value, grad_out, level_weights):
    inputs = (split_heads(query, DH), split_heads(key, DH), split_heads(value, DH), split_heads(grad_out, DH), split_heads(level_weights, LEVELS).astype(jnp.float32))
    results = lax.map(one_head, inputs)
    return (join_heads(results[0]), join_heads(results[1]), join_heads(results[2]), join_heads(results[3]), join_heads(results[4]))
```

```python
import functools
import math

import jax
import jax.numpy as jnp
from jax import lax
from jax.experimental import pallas as pl
from jax.experimental.pallas import tpu as pltpu
from jax.sharding import PartitionSpec as P

DH = 128
C = 128
LEVELS = 8
VMEM_LIMIT = 60 * 2**20
BF = jnp.bfloat16
F32 = jnp.float32


def level_scale(level):
    if level == 0:
        return 1.0 / math.sqrt(DH * C)
    return 1.0 / math.sqrt(DH * C * 2 ** (level - 1))


def nn(a, b):
    return lax.dot_general(a, b, (((1,), (0,)), ((), ())), preferred_element_type=F32)


def nt(a, b):
    return lax.dot_general(a, b, (((1,), (1,)), ((), ())), preferred_element_type=F32)


def tn(a, b):
    return lax.dot_general(a, b, (((0,), (0,)), ((), ())), preferred_element_type=F32)


def cat(parts, axis):
    return parts[0] if len(parts) == 1 else jnp.concatenate(parts, axis=axis)


def head_weights(w_ref, head):
    width = w_ref.shape[1]
    return pltpu.roll(w_ref[...].astype(F32), lax.rem(width - head * LEVELS, width), 1)


def pick(rows, head, level, width):
    lane = lax.broadcasted_iota(jnp.int32, (rows, width), 1)
    return jnp.where(lane == head * LEVELS + level, 1.0, 0.0).astype(BF)


def sums_kernel(local_bits, q_ref, k_ref, v_ref, g_ref, w_ref, t_ref, *rest):
    p_refs, wr = rest[:-1], rest[-1]
    head = pl.program_id(0)
    wr[...] = head_weights(w_ref, head)
    t_ref[0] = tn(k_ref[...], v_ref[...]).astype(BF)
    q = q_ref[...].astype(F32)
    weighted = [
        (wr[:, local_bits + 1 + j : local_bits + 2 + j] * q).astype(BF) for j in range(len(p_refs))
    ]
    out = tn(g_ref[...], cat(weighted, 1))
    for j, p_ref in enumerate(p_refs):
        p_ref[0] = out[:, j * DH : (j + 1) * DH].astype(BF)


def sums_call(query, key, value, grad_out, weights, heads, local_bits, cross_bits):
    tokens = query.shape[0]
    column = pl.BlockSpec((tokens, DH), lambda h: (0, h))
    square = pl.BlockSpec((1, DH, DH), lambda h: (h, 0, 0))
    outs = [jax.ShapeDtypeStruct((heads, DH, DH), BF)] * (1 + cross_bits)
    return pl.pallas_call(
        functools.partial(sums_kernel, local_bits),
        grid=(heads,),
        in_specs=[column] * 4 + [pl.BlockSpec(weights.shape, lambda h: (0, 0))],
        out_specs=[square] * (1 + cross_bits),
        out_shape=outs,
        scratch_shapes=[pltpu.VMEM(weights.shape, F32)],
        compiler_params=pltpu.CompilerParams(vmem_limit_bytes=VMEM_LIMIT),
        name="sums",
    )(query, key, value, grad_out, weights)


class Exchange:
    def __init__(self, local_bits, cross_bits, head_bits, heads, chunks):
        self.local_bits, self.cross_bits, self.head_bits = local_bits, cross_bits, head_bits
        self.chunks, self.count, self.heads = chunks, heads // chunks, heads
        self.size = 1 << head_bits
        low, high = range(head_bits), range(head_bits, cross_bits)
        self.low, self.high = low, high
        landing = [("R", i) for i in low] + [("PR", j) for j in high]
        landing += [("L", i) for i in low] + [("TL", 0)] + [("PL", j) for j in high]
        landing += [("T", i) for i in high] + [(("P", j), i) for j in high for i in high if i <= j]
        sending = [("TR", 0)] + [("PR", j) for j in high]
        sending += [("L", i) for i in low] + [("TL", 0)] + [("PL", j) for j in high]
        sending += [("T", i) for i in high] + [(("P", j), i) for j in high for i in high if i <= j]
        self.lands = {key: n for n, key in enumerate(landing)}
        self.sends = {key: n for n, key in enumerate(sending)}
        self.last_time = chunks - 1 + self.size + 1 + 2 * (len(high) - 1)

    def scratch(self):
        sems = pltpu.SemaphoreType.DMA((len(self.lands), self.chunks))
        return [
            pltpu.VMEM((len(self.lands), self.heads, DH, DH), BF),
            pltpu.VMEM((len(self.sends), self.heads, DH, DH), BF),
            pltpu.VMEM((self.heads, DH, DH), F32),
            sems,
            sems,
        ]

    def bind(self, sources, states, adjoint, scratch):
        self.total, self.products = sources[0], sources[1:]
        self.states, self.adjoint = states, adjoint
        self.landing, self.sending, self.sum, self.send_sem, self.recv_sem = scratch
        self.z, seq = lax.axis_index("head"), lax.axis_index("seq")
        self.bit = []
        for i in range(self.cross_bits):
            position, stride = self.z, 1 << i
            if i >= self.head_bits:
                position, stride = seq, 1 << (i - self.head_bits)
            self.bit.append((position // stride) % 2)
        self.partner = {
            i: {"seq": seq + (1 - 2 * self.bit[i]) * (1 << (i - self.head_bits))}
            for i in self.high
        }
        self.right, self.left = {"head": self.z + 1}, {"head": self.z - 1}
        self.has_right, self.has_left = self.z < self.size - 1, self.z > 0

    def part(self, chunk):
        return pl.ds(chunk * self.count, self.count)

    def landed(self, key, chunk):
        return self.landing[self.lands[key], self.part(chunk)].astype(F32)

    def store(self, key, chunk, value):
        self.sending[self.sends[key], self.part(chunk)] = value.astype(BF)

    def copy(self, key, chunk, device, source=None):
        slot = self.lands[key]
        if source is None:
            source = self.sending.at[self.sends[key]]
        return pltpu.make_async_remote_copy(
            src_ref=source.at[self.part(chunk)],
            dst_ref=self.landing.at[slot, self.part(chunk)],
            send_sem=self.send_sem.at[slot, chunk],
            recv_sem=self.recv_sem.at[slot, chunk],
            device_id=device,
            device_id_type=pl.DeviceIdType.MESH,
        )

    def transfers(self):
        for i in self.low:
            yield ("R", i), self.right, self.has_right & (((self.z + 1) >> i) % 2 == 1), self.bit[i] == 1
        for j in self.high:
            own = self.bit[j] == 1
            yield ("PR", j), self.right, self.has_right & own, self.has_left & own
        for i in self.low:
            block = self.z % (2 << i)
            yield ("L", i), self.left, block != 0, block != (2 << i) - 1
        yield ("TL", 0), self.left, self.has_left, self.has_right
        for j in self.high:
            own = self.bit[j] == 1
            yield ("PL", j), self.left, self.has_left & own, self.has_right & own
        for i in self.high:
            up, down, always = self.bit[i] == 1, self.bit[i] == 0, self.bit[i] >= 0
            last = i == self.cross_bits - 1
            yield ("T", i), self.partner[i], (down if last else always), (up if last else always)
            yield (("P", i), i), self.partner[i], up, down
            for j in range(i + 1, self.cross_bits):
                own = self.bit[j] == 1
                yield (("P", j), i), self.partner[i], own, own

    def greet(self):
        barrier = pltpu.get_barrier_semaphore()

        def signal(device):
            pl.semaphore_signal(
                barrier, inc=1, device_id=device, device_id_type=pl.DeviceIdType.MESH
            )

        for i in self.high:
            signal(self.partner[i])
        signal({"head": lax.rem(self.z + 1, self.size)})
        signal({"head": lax.rem(self.z + self.size - 1, self.size)})
        pl.semaphore_wait(barrier, len(self.high) + 2)

    def wait(self, chunk, kinds):
        for key, device, _, receives in self.transfers():
            if key in kinds:
                own = self.landing.at[self.lands[key]]
                pl.when(receives)(
                    lambda k=key, d=device, r=own: self.copy(k, chunk, d, r).wait_recv()
                )

    def start(self, chunk, kinds):
        for key, device, sends, _ in self.transfers():
            if key in kinds:
                pl.when(sends)(lambda k=key, d=device: self.copy(k, chunk, d).start())

    def chain(self, key, chunk, own, receives):
        @pl.when(receives)
        def _():
            self.store(key, chunk, own.astype(F32) + self.landed(key, chunk))

        @pl.when(jnp.logical_not(receives))
        def _():
            self.store(key, chunk, own)

    def rightward(self, chunk):
        part = self.part(chunk)
        self.wait(chunk, [("R", i) for i in self.low] + [("PR", j) for j in self.high])
        for i in self.low:
            @pl.when(self.z % (2 << i) == (1 << i) - 1)
            def _(i=i):
                value = self.total[part].astype(F32)
                for k in range(i):
                    value = value + self.landed(("R", k), chunk)
                self.store(("TR", 0), chunk, value)
                self.copy(
                    ("R", i), chunk, self.right, self.sending.at[self.sends["TR", 0]]
                ).start()

            @pl.when((self.bit[i] == 1) & (self.z % (1 << i) != (1 << i) - 1))
            def _(i=i):
                self.copy(
                    ("R", i), chunk, self.right, self.landing.at[self.lands["R", i]]
                ).start()

        for j in self.high:

            @pl.when((self.bit[j] == 1) & self.has_right)
            def _(j=j):
                self.chain(("PR", j), chunk, self.products[j][part], self.has_left)

        self.start(chunk, [("PR", j) for j in self.high])

    def leftward(self, chunk):
        part = self.part(chunk)
        keys = [("L", i) for i in self.low] + [("TL", 0)] + [("PL", j) for j in self.high]
        self.wait(chunk, keys)
        for i in self.low:
            block = self.z % (2 << i)

            @pl.when(self.bit[i] == 1)
            def _(i=i, block=block):
                self.chain(("L", i), chunk, self.products[i][part], block != (2 << i) - 1)
                self.copy(("L", i), chunk, self.left).start()

            @pl.when((self.bit[i] == 0) & (block != 0))
            def _(i=i):
                self.copy(("L", i), chunk, self.left, self.landing.at[self.lands["L", i]]).start()

        @pl.when(self.has_left)
        def _():
            self.chain(("TL", 0), chunk, self.total[part], self.has_right)

        for j in self.high:

            @pl.when((self.bit[j] == 1) & self.has_left)
            def _(j=j):
                self.chain(("PL", j), chunk, self.products[j][part], self.has_right)

        self.start(chunk, [("TL", 0)] + [("PL", j) for j in self.high])

    def add(self, key, chunk, source, receives, first=None):
        @pl.when(receives)
        def _():
            base = self.sending[self.sends[first or key], self.part(chunk)].astype(F32)
            self.store(key, chunk, base + self.landed(source, chunk))

    def read(self, i, chunk, state, term):
        part = self.part(chunk)
        factor = level_scale(self.local_bits + i + 1)

        @pl.when(self.bit[i] == 1)
        def _():
            self.states[i][part] = (factor * self.landed(state, chunk)).astype(BF)

        @pl.when(self.bit[i] == 0)
        def _():
            self.states[i][part] = jnp.zeros((self.count, DH, DH), BF)
            self.sum[part] += factor * self.landed(term, chunk)

    def cross(self, chunk):
        part = self.part(chunk)
        self.sum[part] = jnp.zeros((self.count, DH, DH), F32)
        for i in self.low:
            self.read(i, chunk, ("R", i), ("L", i))
        first = self.head_bits
        value = self.total[part].astype(F32)
        for i in self.low:
            value = value + jnp.where(self.bit[i] == 1, self.landed(("R", i), chunk), 0.0)
        value = value + jnp.where(self.has_right, self.landed(("TL", 0), chunk), 0.0)
        self.store(("T", first), chunk, value)
        for j in self.high:

            @pl.when(self.bit[j] == 1)
            def _(j=j):
                value = self.products[j][part].astype(F32)
                value = value + jnp.where(self.has_left, self.landed(("PR", j), chunk), 0.0)
                value = value + jnp.where(self.has_right, self.landed(("PL", j), chunk), 0.0)
                self.store((("P", j), first), chunk, value)

        self.start(chunk, [("T", first)] + [(("P", j), first) for j in self.high])

    def arrive(self, i, chunk):
        part = self.part(chunk)
        above = range(i + 1, self.cross_bits)
        self.wait(chunk, [("T", i), (("P", i), i)] + [(("P", j), i) for j in above])
        if len(above):
            self.add(("T", i + 1), chunk, ("T", i), self.bit[i] >= 0, ("T", i))
            for j in above:
                self.add((("P", j), i + 1), chunk, (("P", j), i), self.bit[j] == 1, (("P", j), i))
            self.start(chunk, [("T", i + 1)] + [(("P", j), i + 1) for j in above])
        self.read(i, chunk, ("T", i), (("P", i), i))
        if not len(above):
            self.adjoint[part] = self.sum[part].astype(BF)

    def advance(self, time):
        def at(offset, event):
            chunk = time - offset

            @pl.when((chunk >= 0) & (chunk < self.chunks))
            def _():
                event(chunk)

        at(self.z, self.rightward)
        at(self.size - 1 - self.z, self.leftward)
        at(self.size - 1, self.cross)
        for i in self.high:
            at(self.size + 1 + 2 * (i - self.head_bits), functools.partial(self.arrive, i))

    def finish(self, steps):
        def late(time, carry):
            self.advance(time)
            return carry

        if self.last_time >= steps:
            lax.fori_loop(steps, self.last_time + 1, late, 0)

        def body(chunk, carry):
            for key, device, sends, _ in self.transfers():
                source = self.landing.at[self.lands[key]]
                pl.when(sends)(
                    lambda k=key, d=device, r=source: self.copy(k, chunk, d, r).wait_send()
                )
            return carry

        lax.fori_loop(0, self.chunks, body, 0)


def local_kernel(stretches, exchange, *refs):
    cross_bits = exchange.cross_bits
    q_ref, k_ref, v_ref, g_ref, w_ref = refs[:5]
    sources = refs[5 : 6 + cross_bits]
    outs = refs[6 + cross_bits :]
    att_ref, dq_ref, dk_ref, dv_ref, gw_ref = outs[:5]
    states_out = outs[5 : 5 + cross_bits]
    adjoint_out, wr = outs[5 + cross_bits : 7 + cross_bits]
    exchange.bind(sources, states_out, adjoint_out, outs[7 + cross_bits :])
    step = pl.program_id(0)
    head = step
    local_bits = stretches.bit_length() - 1
    width = w_ref.shape[1]

    @pl.when(step == 0)
    def _():
        gw_ref[...] = jnp.zeros_like(gw_ref)

    pl.when(step == 0)(exchange.greet)
    exchange.advance(step)
    wr[...] = head_weights(w_ref, head)

    def rows(ref, n, count=1):
        return ref[n * C : (n + count) * C, :]

    def weighted(n, level):
        return (wr[n * C : (n + 1) * C, level : level + 1] * rows(q_ref, n).astype(F32)).astype(BF)

    sums = {}
    for n in range(stretches - 1):
        sums[0, n] = tn(rows(k_ref, n), rows(v_ref, n))
    for b in range(1, local_bits):
        for m in range(stretches >> b):
            if (b - 1, 2 * m + 1) in sums:
                sums[b, m] = sums[b - 1, 2 * m] + sums[b - 1, 2 * m + 1]
    states, adjoints, wq = {}, {}, {}
    for b in range(local_bits):
        for group in range(stretches >> (b + 1)):
            states[b, group] = (level_scale(b + 1) * sums[b, 2 * group]).astype(BF)
            first = (2 * group + 1) << b
            for n in range(first, first + (1 << b)):
                wq[b, n] = weighted(n, b + 1)
            up = cat([wq[b, n] for n in range(first, first + (1 << b))], 0)
            adjoints[b, group] = level_scale(b + 1) * tn(rows(g_ref, first, 1 << b), up)

    row = lax.broadcasted_iota(jnp.int32, (C, C), 0)
    col = lax.broadcasted_iota(jnp.int32, (C, C), 1)
    mask = jnp.where(col <= row, level_scale(0), 0.0).astype(F32)
    for n in range(stretches):
        q, k, v, g = (rows(ref, n) for ref in (q_ref, k_ref, v_ref, g_ref))
        here = slice(n * C, (n + 1) * C)
        bits = [b for b in range(local_bits) if n >> b & 1]
        read = [states[b, n >> (b + 1)] for b in bits]
        scores = nt(q, k) * mask
        grads = nt(g, v)
        w0 = wr[here, 0:1]
        probs = (w0 * scores).astype(BF)
        gscores = (w0 * (grads * mask)).astype(BF)
        att = nn(cat([probs] + [wq[b, n] for b in bits], 1), cat([v] + read, 0))
        dq = nn(gscores, k)
        marks = [(scores * grads).astype(BF)]
        q32 = q.astype(F32)
        for b, state in zip(bits, read):
            back = nt(g, state)
            dq = dq + wr[here, b + 1 : b + 2] * back
            marks.append((q32 * back).astype(BF))
        picks = [pick(C, head, level, width) for level in [0] + [b + 1 for b in bits]]
        gw_ref[here, :] += nn(cat(marks, 1), cat(picks, 0))
        dk = tn(gscores, q)
        dv = tn(probs, g)
        adjoint = None
        for b in range(local_bits):
            if not n >> b & 1:
                term = adjoints[b, n >> (b + 1)]
                adjoint = term if adjoint is None else adjoint + term
        if adjoint is not None:
            adjoint = adjoint.astype(BF)
            dk = dk + nn(v, adjoint)
            dv = dv + nt(k, adjoint)
        att_ref[here, :] = att.astype(BF)
        dq_ref[here, :] = dq.astype(BF)
        dk_ref[here, :] = dk.astype(BF)
        dv_ref[here, :] = dv.astype(BF)

    @pl.when(step == pl.num_programs(0) - 1)
    def _():
        exchange.finish(exchange.heads)


def local_call(query, key, value, grad_out, weights, sums, head_bits):
    tokens = query.shape[0]
    stretches = tokens // C
    heads = query.shape[1] // DH
    cross_bits = len(sums) - 1
    exchange = Exchange(stretches.bit_length() - 1, cross_bits, head_bits, heads, heads // 2)
    column = pl.BlockSpec((tokens, DH), lambda h: (0, h))
    whole = pl.BlockSpec(weights.shape, lambda h: (0, 0))
    squares = pl.BlockSpec((heads, DH, DH), lambda h: (0, 0, 0))
    shape = jax.ShapeDtypeStruct(query.shape, BF)
    square = jax.ShapeDtypeStruct((heads, DH, DH), BF)
    return pl.pallas_call(
        functools.partial(local_kernel, stretches, exchange),
        grid=(heads,),
        in_specs=[column] * 4 + [whole] + [squares] * (cross_bits + 1),
        out_specs=[column] * 4 + [whole] + [squares] * (cross_bits + 1),
        out_shape=[shape] * 4
        + [jax.ShapeDtypeStruct(weights.shape, F32)]
        + [square] * (cross_bits + 1),
        scratch_shapes=[pltpu.VMEM(weights.shape, F32)] + exchange.scratch(),
        compiler_params=pltpu.CompilerParams(
            vmem_limit_bytes=VMEM_LIMIT, collective_id=0, has_side_effects=True
        ),
        name="local",
    )(query, key, value, grad_out, weights, *sums)


def cross_kernel(local_bits, cross_bits, chunks, *refs):
    q_ref, k_ref, v_ref, g_ref, w_ref = refs[:5]
    att_in, dq_in, dk_in, dv_in = refs[5:9]
    gw_in = refs[9 : 9 + chunks]
    states = refs[9 + chunks : 9 + chunks + cross_bits]
    adjoint = refs[9 + chunks + cross_bits]
    att_ref, dq_ref, dk_ref, dv_ref, gw_ref, acc, wr = refs[10 + chunks + cross_bits :]
    head = pl.program_id(0)
    width = w_ref.shape[1]

    @pl.when(head == 0)
    def _():
        total = gw_in[0][...]
        for other in gw_in[1:]:
            total = total + other[...]
        acc[...] = total

    wr[...] = head_weights(w_ref, head)
    read = cat([state[0] for state in states], 0)
    adj = adjoint[0]
    picks = cat([pick(DH, head, local_bits + 1 + j, width) for j in range(cross_bits)], 0)
    tokens = q_ref.shape[0]
    step = min(2 * C, tokens)
    for start in range(0, tokens, step):
        here = slice(start, start + step)
        q32 = q_ref[here, :].astype(F32)
        columns = [
            wr[here, local_bits + 1 + j : local_bits + 2 + j] for j in range(cross_bits)
        ]
        att = att_in[here, :].astype(F32) + nn(cat([(w * q32).astype(BF) for w in columns], 1), read)
        back = nt(g_ref[here, :], read)
        dq = dq_in[here, :].astype(F32)
        marks = []
        for j, w in enumerate(columns):
            part = back[:, j * DH : (j + 1) * DH]
            dq = dq + w * part
            marks.append((q32 * part).astype(BF))
        acc[here, :] += nn(cat(marks, 1), picks)
        att_ref[here, :] = att.astype(BF)
        dq_ref[here, :] = dq.astype(BF)
        dk_ref[here, :] = (dk_in[here, :].astype(F32) + nn(v_ref[here, :], adj)).astype(BF)
        dv_ref[here, :] = (dv_in[here, :].astype(F32) + nt(k_ref[here, :], adj)).astype(BF)

    @pl.when(head == pl.num_programs(0) - 1)
    def _():
        gw_ref[...] = acc[...].astype(BF)


def cross_call(query, key, value, grad_out, weights, partial, gws, states, adjoint, local_bits):
    tokens = query.shape[0]
    heads = query.shape[1] // DH
    cross_bits = len(states)
    column = pl.BlockSpec((tokens, DH), lambda h: (0, h))
    whole = pl.BlockSpec(weights.shape, lambda h: (0, 0))
    square = pl.BlockSpec((1, DH, DH), lambda h: (h, 0, 0))
    return pl.pallas_call(
        functools.partial(cross_kernel, local_bits, cross_bits, len(gws)),
        grid=(heads,),
        in_specs=[column] * 4
        + [whole]
        + [column] * 4
        + [whole] * len(gws)
        + [square] * (cross_bits + 1),
        out_specs=[column] * 4 + [whole],
        out_shape=[jax.ShapeDtypeStruct(query.shape, BF)] * 4
        + [jax.ShapeDtypeStruct(weights.shape, BF)],
        scratch_shapes=[pltpu.VMEM(weights.shape, F32), pltpu.VMEM(weights.shape, F32)],
        compiler_params=pltpu.CompilerParams(vmem_limit_bytes=VMEM_LIMIT),
        name="cross",
    )(query, key, value, grad_out, weights, *partial, *gws, *states, adjoint)


def general(query, key, value, grad_out, weights):
    tokens = query.shape[0]
    heads = query.shape[1] // DH
    local_bits = (tokens // C).bit_length() - 1
    cross_bits = LEVELS - 1 - local_bits
    head_bits = lax.axis_size("head").bit_length() - 1
    sums = sums_call(query, key, value, grad_out, weights, heads, local_bits, cross_bits)
    outs = local_call(query, key, value, grad_out, weights, sums, head_bits)
    partial, gw = outs[:4], outs[4]
    states, adjoint = outs[5 : 5 + cross_bits], outs[5 + cross_bits]
    return tuple(
        cross_call(
            query, key, value, grad_out, weights, partial, [gw], states, adjoint, local_bits
        )
    )


GRID = 4
T_RIGHT, T_NEXT, T_LEFT, A_RIGHT, A_LEFT, A_LEFT2, P_X, H_CORE, U_CORE, U_X0, U_X1 = range(11)
MESSAGES = 11


class Links:
    def __init__(self, heads, chunks, local_bits):
        self.heads, self.chunks, self.count = heads, chunks, heads // chunks
        self.factors = [level_scale(local_bits + 1 + j) for j in range(4)]
        self.stages = [
            self.x_exchange, self.core_exchange, self.chain1, self.chain2, self.chain3,
            self.across, self.arrive,
        ]

    def scratch(self):
        sems = pltpu.SemaphoreType.DMA((MESSAGES, self.chunks))
        return [
            pltpu.VMEM((5, self.heads, DH, DH), BF),
            pltpu.VMEM((self.heads, DH, DH), F32),
            pltpu.VMEM((MESSAGES, self.heads, DH, DH), BF),
            pltpu.VMEM((MESSAGES, self.heads, DH, DH), BF),
            sems,
            sems,
        ]

    def bind(self, states, adjoint, scratch):
        self.states, self.adjoint = states, adjoint
        self.own, self.extra, self.landing, self.sending, self.send_sem, self.recv_sem = scratch
        self.z, self.seq = lax.axis_index("head"), lax.axis_index("seq")
        self.x, self.c = self.seq // 2, self.seq % 2
        z, x, c = self.z, self.x, self.c
        right, left = {"head": z + 1}, {"head": z - 1}
        core = {"seq": x * 2 + 1 - c}
        both = (x == 0) | (c == 0)
        yes = z >= 0
        self.both = both
        self.table = {
            T_RIGHT: (right, z < 3, z > 0),
            T_NEXT: (right, z == 2, z == 3),
            T_LEFT: (left, (z > 0) & both, (z < 3) & both),
            A_RIGHT: (right, (z < 3) & both, (z > 0) & both),
            A_LEFT: (left, z > 0, z < 3),
            A_LEFT2: (left, z == 3, z == 2),
            P_X: ({"seq": c}, x == 1, x == 0),
            H_CORE: (core, (x == 0) | (c == 1), both),
            U_CORE: (core, (c == 0) & yes, c == 1),
            U_X0: ({"seq": 2}, (x == 0) & (c == 1), (x == 1) & (c == 0)),
            U_X1: ({"seq": 3}, (x == 0) & (c == 1), (x == 1) & (c == 1)),
        }

    def greet(self):
        barrier = pltpu.get_barrier_semaphore()
        other = 1 - self.x
        devices = [
            {"head": (self.z + 1) % GRID},
            {"head": (self.z + GRID - 1) % GRID},
            {"seq": self.x * 2 + 1 - self.c},
            {"seq": other * 2 + self.c},
            {"seq": other * 2 + 1 - self.c},
        ]
        for device in devices:
            pl.semaphore_signal(
                barrier, inc=1, device_id=device, device_id_type=pl.DeviceIdType.MESH
            )
        pl.semaphore_wait(barrier, len(devices))

    def part(self, chunk):
        return pl.ds(chunk * self.count, self.count)

    def copy(self, key, chunk, source):
        part = self.part(chunk)
        return pltpu.make_async_remote_copy(
            src_ref=source.at[part],
            dst_ref=self.landing.at[key, part],
            send_sem=self.send_sem.at[key, chunk],
            recv_sem=self.recv_sem.at[key, chunk],
            device_id=self.table[key][0],
            device_id_type=pl.DeviceIdType.MESH,
        )

    def send(self, key, chunk, source, when):
        pl.when(when)(lambda: self.copy(key, chunk, source).start())

    def emit(self, key, chunk, value):
        self.sending[key, self.part(chunk)] = value.astype(BF)
        self.copy(key, chunk, self.sending.at[key]).start()

    def wait(self, chunk, key, when=True):
        receives = self.table[key][2] & when
        pl.when(receives)(lambda: self.copy(key, chunk, self.landing.at[key]).wait_recv())

    def landed(self, key, chunk):
        return self.landing[key, self.part(chunk)].astype(F32)

    def mine(self, index, chunk):
        return self.own[index, self.part(chunk)].astype(F32)

    def first(self, chunk):
        z, x, c = self.z, self.x, self.c
        total = self.own.at[0]
        self.send(T_RIGHT, chunk, total, z == 0)
        self.send(T_NEXT, chunk, total, z == 2)
        self.send(T_LEFT, chunk, total, (z == 3) & self.both)
        self.send(P_X, chunk, self.own.at[4], x == 1)
        self.send(H_CORE, chunk, self.own.at[3], (x == 1) & (c == 1))

    def x_exchange(self, chunk):
        x, c = self.x, self.c
        self.wait(chunk, P_X)
        self.send(H_CORE, chunk, self.landing.at[P_X], (x == 0) & (c == 0))

        @pl.when((x == 0) & (c == 1))
        def _():
            self.emit(H_CORE, chunk, self.mine(3, chunk) + self.landed(P_X, chunk))

    def core_exchange(self, chunk):
        z = self.z
        part = self.part(chunk)
        self.wait(chunk, H_CORE)

        @pl.when(self.both)
        def _():
            value = self.landed(H_CORE, chunk)
            self.extra[part] = value + jnp.where(self.x == 0, self.landed(P_X, chunk), 0.0)

        @pl.when(jnp.logical_not(self.both))
        def _():
            self.extra[part] = jnp.zeros((self.count, DH, DH), F32)

        @pl.when((z == 0) & self.both)
        def _():
            self.emit(A_RIGHT, chunk, self.extra[part])

        @pl.when(z == 3)
        def _():
            self.emit(A_LEFT2, chunk, self.mine(2, chunk) + self.extra[part])
            self.emit(A_LEFT, chunk, self.mine(1, chunk) + self.extra[part])

    def forward_right(self, chunk):
        part = self.part(chunk)

        @pl.when(self.both)
        def _():
            self.emit(A_RIGHT, chunk, self.extra[part] + self.landed(A_RIGHT, chunk))

    def forward_left(self, chunk):
        pl.when(self.both)(
            lambda: self.emit(T_LEFT, chunk, self.mine(0, chunk) + self.landed(T_LEFT, chunk))
        )

    def chain1(self, chunk):
        z = self.z
        part = self.part(chunk)
        self.wait(chunk, T_RIGHT, z == 1)
        self.wait(chunk, T_LEFT, z == 2)
        self.wait(chunk, A_RIGHT, z == 1)
        self.wait(chunk, A_LEFT, z == 2)
        self.wait(chunk, A_LEFT2)

        @pl.when(z == 1)
        def _():
            self.emit(T_RIGHT, chunk, self.mine(0, chunk) + self.landed(T_RIGHT, chunk))
            self.forward_right(chunk)

        @pl.when(z == 2)
        def _():
            self.forward_left(chunk)
            value = self.mine(2, chunk) + self.extra[part] + self.landed(A_LEFT2, chunk)
            self.emit(A_LEFT, chunk, value)

    def chain2(self, chunk):
        z = self.z
        part = self.part(chunk)
        self.wait(chunk, T_RIGHT, z == 2)
        self.wait(chunk, T_LEFT, z == 1)
        self.wait(chunk, A_RIGHT, z == 2)
        self.wait(chunk, A_LEFT, z == 1)

        @pl.when(z == 2)
        def _():
            self.copy(T_RIGHT, chunk, self.landing.at[T_RIGHT]).start()
            self.forward_right(chunk)

        @pl.when(z == 1)
        def _():
            self.forward_left(chunk)
            value = self.mine(1, chunk) + self.extra[part] + self.landed(A_LEFT, chunk)
            self.emit(A_LEFT, chunk, value)

    def chain3(self, chunk):
        z, c = self.z, self.c
        part = self.part(chunk)
        self.wait(chunk, T_RIGHT, z == 3)
        self.wait(chunk, T_NEXT)
        self.wait(chunk, T_LEFT, z == 0)
        self.wait(chunk, A_RIGHT, z == 3)
        self.wait(chunk, A_LEFT, z == 0)
        value = self.extra[part]
        value = value + jnp.where((z > 0) & self.both, self.landed(A_RIGHT, chunk), 0.0)
        value = value + jnp.where(z < 3, self.landed(A_LEFT, chunk), 0.0)
        self.adjoint[part] = value.astype(BF)

        @pl.when(self.both)
        def _():
            value = self.mine(0, chunk)
            value = value + jnp.where(z > 0, self.landed(T_RIGHT, chunk), 0.0)
            value = value + jnp.where(z == 3, self.landed(T_NEXT, chunk), 0.0)
            value = value + jnp.where(z < 3, self.landed(T_LEFT, chunk), 0.0)
            self.sending[U_CORE, part] = value.astype(BF)

        self.send(U_CORE, chunk, self.sending.at[U_CORE], c == 0)

        def read(level, state):
            self.states[part, level * DH : (level + 1) * DH] = state.astype(BF)

        near = jnp.where(z == 1, self.landed(T_RIGHT, chunk), self.landed(T_NEXT, chunk))
        read(0, jnp.where(z % 2 == 1, self.factors[0] * near, 0.0))
        read(1, jnp.where(z >= 2, self.factors[1] * self.landed(T_RIGHT, chunk), 0.0))

    def across(self, chunk):
        part = self.part(chunk)
        self.wait(chunk, U_CORE)
        state = jnp.where(self.c == 1, self.factors[2] * self.landed(U_CORE, chunk), 0.0)
        self.states[part, 2 * DH : 3 * DH] = state.astype(BF)

        @pl.when((self.x == 0) & (self.c == 1))
        def _():
            value = self.sending[U_CORE, part].astype(F32) + self.landed(U_CORE, chunk)
            self.sending[U_X0, part] = value.astype(BF)
            self.copy(U_X0, chunk, self.sending.at[U_X0]).start()
            self.copy(U_X1, chunk, self.sending.at[U_X0]).start()

    def arrive(self, chunk):
        part = self.part(chunk)
        self.wait(chunk, U_X0)
        self.wait(chunk, U_X1)
        state = jnp.where(self.c == 0, self.landed(U_X0, chunk), self.landed(U_X1, chunk))
        state = jnp.where(self.x == 1, self.factors[3] * state, 0.0)
        self.states[part, 3 * DH : 4 * DH] = state.astype(BF)

    def advance(self, time, pace):
        for offset, stage in enumerate(self.stages):
            late = time - offset
            chunk = late // pace

            @pl.when((late >= 0) & (late % pace == 0) & (chunk < self.chunks))
            def _(stage=stage, chunk=chunk):
                stage(chunk)

    def last(self, pace):
        return (self.chunks - 1) * pace + len(self.stages) - 1

    def drain(self):
        def body(chunk, carry):
            for key, (_, sends, _) in self.table.items():
                pl.when(sends)(
                    lambda k=key: self.copy(k, chunk, self.landing.at[k]).wait_send()
                )
            return carry

        lax.fori_loop(0, self.chunks, body, 0)


def rows_of_weights(w_ref, wt_ref):
    for start in range(0, w_ref.shape[0], C):
        here = slice(start, start + C)
        wt_ref[:, here] = w_ref[here, :].astype(F32).T


def level_rows(wt_ref, head):
    return wt_ref[pl.ds(pl.multiple_of(head * LEVELS, LEVELS), LEVELS), :]


def stage_kernel(stretches, heads, links, *refs):
    q_ref, k_ref, v_ref, g_ref, w_ref = refs[:5]
    att_ref, dq_ref, dk_ref, dv_ref, gw_ref, states_out, adjoint_out = refs[5:12]
    wt, wq = refs[12:14]
    links.bind(states_out, adjoint_out, refs[14:])
    local_bits = stretches.bit_length() - 1
    step = pl.program_id(0)
    head = lax.rem(step, heads)

    @pl.when(step == 0)
    def _():
        rows_of_weights(w_ref, wt)
        links.greet()

    @pl.when(step < heads)
    def _():
        weight = level_rows(wt, head)
        qt32 = q_ref[...].T.astype(F32)
        for j in range(4):
            row = weight[local_bits + 1 + j : local_bits + 2 + j, :]
            wq[j * DH : (j + 1) * DH, :] = (row * qt32).astype(BF)
        out = nt(g_ref[...].T, wq[...])
        for j in range(4):
            links.own[1 + j, head] = (links.factors[j] * out[:, j * DH : (j + 1) * DH]).astype(BF)
        links.own[0, head] = tn(k_ref[...], v_ref[...]).astype(BF)

        @pl.when(head % links.count == links.count - 1)
        def _():
            links.first(head // links.count)

    @pl.when(step >= heads)
    def _():
        links.advance(step - heads, heads // links.chunks)
        local_part(stretches, head, wt, refs[:4], (att_ref, dq_ref, dk_ref, dv_ref, gw_ref))

    @pl.when(step == pl.num_programs(0) - 1)
    def _():
        def late(time, carry):
            links.advance(time, heads // links.chunks)
            return carry

        lax.fori_loop(heads, links.last(heads // links.chunks) + 1, late, 0)
        links.drain()


def local_part(stretches, head, wt, ins, outs):
    q_ref, k_ref, v_ref, g_ref = ins
    att_ref, dq_ref, dk_ref, dv_ref, gw_ref = outs
    local_bits = stretches.bit_length() - 1
    weight = level_rows(wt, head)

    def here(n, count=1):
        return slice(n * C, (n + count) * C)

    qt, kt, vt, gt, qt32 = [], [], [], [], []
    for n in range(stretches):
        qt.append(q_ref[here(n), :].T)
        kt.append(k_ref[here(n), :].T)
        vt.append(v_ref[here(n), :].T)
        gt.append(g_ref[here(n), :].T)
        qt32.append(qt[n].astype(F32))

    sums = {}
    for n in range(stretches - 1):
        sums[0, n] = nn(kt[n], v_ref[here(n), :])
    for b in range(1, local_bits):
        for m in range(stretches >> b):
            if (b - 1, 2 * m + 1) in sums:
                sums[b, m] = sums[b - 1, 2 * m] + sums[b - 1, 2 * m + 1]
    states, flipped, adjoints, wq = {}, {}, {}, {}
    for b in range(local_bits):
        for group in range(stretches >> (b + 1)):
            state = (level_scale(b + 1) * sums[b, 2 * group]).astype(BF)
            states[b, group], flipped[b, group] = state, state.T
            first, count = (2 * group + 1) << b, 1 << b
            for n in range(first, first + count):
                wq[b, n] = (weight[b + 1 : b + 2, here(n)] * qt32[n]).astype(BF)
            across = cat([wq[b, n] for n in range(first, first + count)], 1)
            adjoints[b, group] = level_scale(b + 1) * nn(across, g_ref[here(first, count), :])

    row = lax.broadcasted_iota(jnp.int32, (C, C), 0)
    col = lax.broadcasted_iota(jnp.int32, (C, C), 1)
    mask = jnp.where(row <= col, level_scale(0), 0.0).astype(F32)
    for n in range(stretches):
        q, k, v, g = (ref[here(n), :] for ref in (q_ref, k_ref, v_ref, g_ref))
        bits = [b for b in range(local_bits) if n >> b & 1]
        scores = nn(k, qt[n]) * mask
        grads = nn(v, gt[n])
        w0 = weight[0:1, here(n)]
        probs = (scores * w0).astype(BF)
        gscores = (grads * mask * w0).astype(BF)
        gws = [jnp.sum(scores * grads, axis=0, keepdims=True)]
        left = [vt[n]] + [flipped[b, n >> (b + 1)] for b in bits]
        att = nn(cat(left, 1), cat([probs] + [wq[b, n] for b in bits], 0))
        dq = nn(kt[n], gscores)
        for b in range(local_bits):
            if b in bits:
                back = nn(states[b, n >> (b + 1)], gt[n])
                dq = dq + weight[b + 1 : b + 2, here(n)] * back
                gws.append(jnp.sum(qt32[n] * back, axis=0, keepdims=True))
            else:
                gws.append(jnp.zeros((1, C), F32))
        gws.append(jnp.zeros((LEVELS - 1 - local_bits, C), F32))
        dk = nn(gscores, q)
        dv = nn(probs, g)
        adjoint = None
        for b in range(local_bits):
            if not n >> b & 1:
                term = adjoints[b, n >> (b + 1)]
                adjoint = term if adjoint is None else adjoint + term
        if adjoint is not None:
            adjoint = adjoint.astype(BF)
            dk = dk + nt(v, adjoint)
            dv = dv + nn(k, adjoint)
        att_ref[0, :, here(n)] = att.astype(BF)
        dq_ref[0, :, here(n)] = dq.astype(BF)
        dk_ref[0, here(n), :] = dk.astype(BF)
        dv_ref[0, here(n), :] = dv.astype(BF)
        gw_ref[0, :, here(n)] = jnp.concatenate(gws, 0)


def stage_call(query, key, value, grad_out, weights):
    tokens = query.shape[0]
    stretches, heads = tokens // C, query.shape[1] // DH
    links = Links(heads, heads // 2, stretches.bit_length() - 1)

    def block(*shape):
        return pl.BlockSpec((1,) + shape, lambda s: (jnp.maximum(s - heads, 0), 0, 0))

    column = pl.BlockSpec((tokens, DH), lambda s: (0, lax.rem(s, heads)))
    shapes = [(DH, tokens)] * 2 + [(tokens, DH)] * 2 + [(LEVELS, tokens)]
    types = [BF] * 4 + [F32]
    small = [(heads, 4 * DH, DH), (heads, DH, DH)]
    return pl.pallas_call(
        functools.partial(stage_kernel, stretches, heads, links),
        grid=(2 * heads,),
        in_specs=[column] * 4 + [pl.BlockSpec(weights.shape, lambda s: (0, 0))],
        out_specs=[block(*shape) for shape in shapes]
        + [pl.BlockSpec(shape, lambda s: (0, 0, 0)) for shape in small],
        out_shape=[
            jax.ShapeDtypeStruct((heads,) + shape, kind) for shape, kind in zip(shapes, types)
        ]
        + [jax.ShapeDtypeStruct(shape, BF) for shape in small],
        scratch_shapes=[
            pltpu.VMEM(weights.shape[::-1], F32),
            pltpu.VMEM((4 * DH, tokens), BF),
        ]
        + links.scratch(),
        compiler_params=pltpu.CompilerParams(
            vmem_limit_bytes=VMEM_LIMIT, collective_id=1, has_side_effects=True
        ),
        name="stage",
    )(query, key, value, grad_out, weights)


def merge_kernel(pair, local_bits, *refs):
    q_ref, k_ref, v_ref, g_ref, w_ref = refs[:5]
    att_in, dq_in, dk_in, dv_in, gw_in, states_ref, adjoint_ref = refs[5:12]
    att_ref, dq_ref, dk_ref, dv_ref, gw_ref, wt, gwt = refs[12:]
    step = pl.program_id(0)
    tokens = q_ref.shape[0]

    @pl.when(step == 0)
    def _():
        rows_of_weights(w_ref, wt)

    for i in range(pair):
        head = step * pair + i
        lanes = slice(i * DH, (i + 1) * DH)
        weight = level_rows(wt, head)
        states, adjoint = states_ref[i], adjoint_ref[i]
        flipped = cat([states[j * DH : (j + 1) * DH, :].T for j in range(4)], 1)
        for start in range(0, tokens, 2 * C):
            here = slice(start, start + 2 * C)
            qt32 = q_ref[here, lanes].T.astype(F32)
            levels = [weight[local_bits + 1 + j : local_bits + 2 + j, here] for j in range(4)]
            wq = cat([(row * qt32).astype(BF) for row in levels], 0)
            att = att_in[i, :, here].astype(F32) + nn(flipped, wq)
            back = nn(states, g_ref[here, lanes].T)
            dq = dq_in[i, :, here].astype(F32)
            gws = [gw_in[i, 0 : local_bits + 1, here]]
            for j, row in enumerate(levels):
                part = back[j * DH : (j + 1) * DH, :]
                dq = dq + row * part
                gws.append(jnp.sum(qt32 * part, axis=0, keepdims=True))
            rows = pl.ds(pl.multiple_of(head * LEVELS, LEVELS), LEVELS)
            gwt[rows, here] = jnp.concatenate(gws, 0)
            att_ref[here, lanes] = att.astype(BF).T
            dq_ref[here, lanes] = dq.astype(BF).T
            v, k = v_ref[here, lanes], k_ref[here, lanes]
            dk_ref[here, lanes] = (dk_in[i, here, :].astype(F32) + nn(v, adjoint)).astype(BF)
            dv_ref[here, lanes] = (dv_in[i, here, :].astype(F32) + nt(k, adjoint)).astype(BF)

    @pl.when(step == pl.num_programs(0) - 1)
    def _():
        for start in range(0, tokens, C):
            here = slice(start, start + C)
            gw_ref[here, :] = gwt[:, here].T.astype(BF)


def merge_call(query, key, value, grad_out, weights, outs, local_bits):
    tokens = query.shape[0]
    heads = query.shape[1] // DH
    pair = 2
    column = pl.BlockSpec((tokens, pair * DH), lambda s: (0, s))
    whole = pl.BlockSpec(weights.shape, lambda s: (0, 0))

    def block(array):
        return pl.BlockSpec((pair,) + array.shape[1:], lambda s: (s, 0, 0))

    return pl.pallas_call(
        functools.partial(merge_kernel, pair, local_bits),
        grid=(heads // pair,),
        in_specs=[column] * 4 + [whole] + [block(array) for array in outs],
        out_specs=[column] * 4 + [whole],
        out_shape=[jax.ShapeDtypeStruct(query.shape, BF)] * 4
        + [jax.ShapeDtypeStruct(weights.shape, BF)],
        scratch_shapes=[pltpu.VMEM(weights.shape[::-1], F32)] * 2,
        compiler_params=pltpu.CompilerParams(vmem_limit_bytes=VMEM_LIMIT),
        name="merge",
    )(query, key, value, grad_out, weights, *outs)


def shards(query, key, value, grad_out, weights):
    local_bits = (query.shape[0] // C).bit_length() - 1
    square = lax.axis_size("head") == GRID and lax.axis_size("seq") == GRID
    if not square or local_bits != LEVELS - 5:
        return general(query, key, value, grad_out, weights)
    outs = stage_call(query, key, value, grad_out, weights)
    return tuple(merge_call(query, key, value, grad_out, weights, outs, local_bits))


def solution(mesh):
    spec = P(("rep", "seq", "head"), None)
    return jax.shard_map(
        shards, mesh=mesh, in_specs=(spec,) * 5, out_specs=(spec,) * 5, check_vma=False
    )
```

```python
import functools
import math

import jax
import jax.numpy as jnp
from jax import lax
from jax.experimental import pallas as pl
from jax.experimental.pallas import tpu as pltpu
from jax.sharding import PartitionSpec as P

DH = 128
C = 128
LEVELS = 8
VMEM_LIMIT = 60 * 2**20
BF = jnp.bfloat16
F32 = jnp.float32


def level_scale(level):
    if level == 0:
        return 1.0 / math.sqrt(DH * C)
    return 1.0 / math.sqrt(DH * C * 2 ** (level - 1))


def nn(a, b):
    return lax.dot_general(a, b, (((1,), (0,)), ((), ())), preferred_element_type=F32)


def nt(a, b):
    return lax.dot_general(a, b, (((1,), (1,)), ((), ())), preferred_element_type=F32)


def tn(a, b):
    return lax.dot_general(a, b, (((0,), (0,)), ((), ())), preferred_element_type=F32)


def cat(parts, axis):
    return parts[0] if len(parts) == 1 else jnp.concatenate(parts, axis=axis)


def head_weights(w_ref, head):
    width = w_ref.shape[1]
    return pltpu.roll(w_ref[...].astype(F32), lax.rem(width - head * LEVELS, width), 1)


def pick(rows, head, level, width):
    lane = lax.broadcasted_iota(jnp.int32, (rows, width), 1)
    return jnp.where(lane == head * LEVELS + level, 1.0, 0.0).astype(BF)


def sums_kernel(local_bits, q_ref, k_ref, v_ref, g_ref, w_ref, t_ref, *rest):
    p_refs, wr = rest[:-1], rest[-1]
    head = pl.program_id(0)
    wr[...] = head_weights(w_ref, head)
    t_ref[0] = tn(k_ref[...], v_ref[...]).astype(BF)
    q = q_ref[...].astype(F32)
    weighted = [
        (wr[:, local_bits + 1 + j : local_bits + 2 + j] * q).astype(BF) for j in range(len(p_refs))
    ]
    out = tn(g_ref[...], cat(weighted, 1))
    for j, p_ref in enumerate(p_refs):
        p_ref[0] = out[:, j * DH : (j + 1) * DH].astype(BF)


def sums_call(query, key, value, grad_out, weights, heads, local_bits, cross_bits):
    tokens = query.shape[0]
    column = pl.BlockSpec((tokens, DH), lambda h: (0, h))
    square = pl.BlockSpec((1, DH, DH), lambda h: (h, 0, 0))
    outs = [jax.ShapeDtypeStruct((heads, DH, DH), BF)] * (1 + cross_bits)
    return pl.pallas_call(
        functools.partial(sums_kernel, local_bits),
        grid=(heads,),
        in_specs=[column] * 4 + [pl.BlockSpec(weights.shape, lambda h: (0, 0))],
        out_specs=[square] * (1 + cross_bits),
        out_shape=outs,
        scratch_shapes=[pltpu.VMEM(weights.shape, F32)],
        compiler_params=pltpu.CompilerParams(vmem_limit_bytes=VMEM_LIMIT),
        name="sums",
    )(query, key, value, grad_out, weights)


class Exchange:
    def __init__(self, local_bits, cross_bits, head_bits, heads, chunks):
        self.local_bits, self.cross_bits, self.head_bits = local_bits, cross_bits, head_bits
        self.chunks, self.count, self.heads = chunks, heads // chunks, heads
        self.size = 1 << head_bits
        low, high = range(head_bits), range(head_bits, cross_bits)
        self.low, self.high = low, high
        landing = [("R", i) for i in low] + [("PR", j) for j in high]
        landing += [("L", i) for i in low] + [("TL", 0)] + [("PL", j) for j in high]
        landing += [("T", i) for i in high] + [(("P", j), i) for j in high for i in high if i <= j]
        sending = [("TR", 0)] + [("PR", j) for j in high]
        sending += [("L", i) for i in low] + [("TL", 0)] + [("PL", j) for j in high]
        sending += [("T", i) for i in high] + [(("P", j), i) for j in high for i in high if i <= j]
        self.lands = {key: n for n, key in enumerate(landing)}
        self.sends = {key: n for n, key in enumerate(sending)}
        self.last_time = chunks - 1 + self.size + 1 + 2 * (len(high) - 1)

    def scratch(self):
        sems = pltpu.SemaphoreType.DMA((len(self.lands), self.chunks))
        return [
            pltpu.VMEM((len(self.lands), self.heads, DH, DH), BF),
            pltpu.VMEM((len(self.sends), self.heads, DH, DH), BF),
            pltpu.VMEM((self.heads, DH, DH), F32),
            sems,
            sems,
        ]

    def bind(self, sources, states, adjoint, scratch):
        self.total, self.products = sources[0], sources[1:]
        self.states, self.adjoint = states, adjoint
        self.landing, self.sending, self.sum, self.send_sem, self.recv_sem = scratch
        self.z, seq = lax.axis_index("head"), lax.axis_index("seq")
        self.bit = []
        for i in range(self.cross_bits):
            position, stride = self.z, 1 << i
            if i >= self.head_bits:
                position, stride = seq, 1 << (i - self.head_bits)
            self.bit.append((position // stride) % 2)
        self.partner = {
            i: {"seq": seq + (1 - 2 * self.bit[i]) * (1 << (i - self.head_bits))}
            for i in self.high
        }
        self.right, self.left = {"head": self.z + 1}, {"head": self.z - 1}
        self.has_right, self.has_left = self.z < self.size - 1, self.z > 0

    def part(self, chunk):
        return pl.ds(chunk * self.count, self.count)

    def landed(self, key, chunk):
        return self.landing[self.lands[key], self.part(chunk)].astype(F32)

    def store(self, key, chunk, value):
        self.sending[self.sends[key], self.part(chunk)] = value.astype(BF)

    def copy(self, key, chunk, device, source=None):
        slot = self.lands[key]
        if source is None:
            source = self.sending.at[self.sends[key]]
        return pltpu.make_async_remote_copy(
            src_ref=source.at[self.part(chunk)],
            dst_ref=self.landing.at[slot, self.part(chunk)],
            send_sem=self.send_sem.at[slot, chunk],
            recv_sem=self.recv_sem.at[slot, chunk],
            device_id=device,
            device_id_type=pl.DeviceIdType.MESH,
        )

    def transfers(self):
        for i in self.low:
            yield ("R", i), self.right, self.has_right & (((self.z + 1) >> i) % 2 == 1), self.bit[i] == 1
        for j in self.high:
            own = self.bit[j] == 1
            yield ("PR", j), self.right, self.has_right & own, self.has_left & own
        for i in self.low:
            block = self.z % (2 << i)
            yield ("L", i), self.left, block != 0, block != (2 << i) - 1
        yield ("TL", 0), self.left, self.has_left, self.has_right
        for j in self.high:
            own = self.bit[j] == 1
            yield ("PL", j), self.left, self.has_left & own, self.has_right & own
        for i in self.high:
            up, down, always = self.bit[i] == 1, self.bit[i] == 0, self.bit[i] >= 0
            last = i == self.cross_bits - 1
            yield ("T", i), self.partner[i], (down if last else always), (up if last else always)
            yield (("P", i), i), self.partner[i], up, down
            for j in range(i + 1, self.cross_bits):
                own = self.bit[j] == 1
                yield (("P", j), i), self.partner[i], own, own

    def greet(self):
        barrier = pltpu.get_barrier_semaphore()

        def signal(device):
            pl.semaphore_signal(
                barrier, inc=1, device_id=device, device_id_type=pl.DeviceIdType.MESH
            )

        for i in self.high:
            signal(self.partner[i])
        signal({"head": lax.rem(self.z + 1, self.size)})
        signal({"head": lax.rem(self.z + self.size - 1, self.size)})
        pl.semaphore_wait(barrier, len(self.high) + 2)

    def wait(self, chunk, kinds):
        for key, device, _, receives in self.transfers():
            if key in kinds:
                own = self.landing.at[self.lands[key]]
                pl.when(receives)(
                    lambda k=key, d=device, r=own: self.copy(k, chunk, d, r).wait_recv()
                )

    def start(self, chunk, kinds):
        for key, device, sends, _ in self.transfers():
            if key in kinds:
                pl.when(sends)(lambda k=key, d=device: self.copy(k, chunk, d).start())

    def chain(self, key, chunk, own, receives):
        @pl.when(receives)
        def _():
            self.store(key, chunk, own.astype(F32) + self.landed(key, chunk))

        @pl.when(jnp.logical_not(receives))
        def _():
            self.store(key, chunk, own)

    def rightward(self, chunk):
        part = self.part(chunk)
        self.wait(chunk, [("R", i) for i in self.low] + [("PR", j) for j in self.high])
        for i in self.low:
            @pl.when(self.z % (2 << i) == (1 << i) - 1)
            def _(i=i):
                value = self.total[part].astype(F32)
                for k in range(i):
                    value = value + self.landed(("R", k), chunk)
                self.store(("TR", 0), chunk, value)
                self.copy(
                    ("R", i), chunk, self.right, self.sending.at[self.sends["TR", 0]]
                ).start()

            @pl.when((self.bit[i] == 1) & (self.z % (1 << i) != (1 << i) - 1))
            def _(i=i):
                self.copy(
                    ("R", i), chunk, self.right, self.landing.at[self.lands["R", i]]
                ).start()

        for j in self.high:

            @pl.when((self.bit[j] == 1) & self.has_right)
            def _(j=j):
                self.chain(("PR", j), chunk, self.products[j][part], self.has_left)

        self.start(chunk, [("PR", j) for j in self.high])

    def leftward(self, chunk):
        part = self.part(chunk)
        keys = [("L", i) for i in self.low] + [("TL", 0)] + [("PL", j) for j in self.high]
        self.wait(chunk, keys)
        for i in self.low:
            block = self.z % (2 << i)

            @pl.when(self.bit[i] == 1)
            def _(i=i, block=block):
                self.chain(("L", i), chunk, self.products[i][part], block != (2 << i) - 1)
                self.copy(("L", i), chunk, self.left).start()

            @pl.when((self.bit[i] == 0) & (block != 0))
            def _(i=i):
                self.copy(("L", i), chunk, self.left, self.landing.at[self.lands["L", i]]).start()

        @pl.when(self.has_left)
        def _():
            self.chain(("TL", 0), chunk, self.total[part], self.has_right)

        for j in self.high:

            @pl.when((self.bit[j] == 1) & self.has_left)
            def _(j=j):
                self.chain(("PL", j), chunk, self.products[j][part], self.has_right)

        self.start(chunk, [("TL", 0)] + [("PL", j) for j in self.high])

    def add(self, key, chunk, source, receives, first=None):
        @pl.when(receives)
        def _():
            base = self.sending[self.sends[first or key], self.part(chunk)].astype(F32)
            self.store(key, chunk, base + self.landed(source, chunk))

    def read(self, i, chunk, state, term):
        part = self.part(chunk)
        factor = level_scale(self.local_bits + i + 1)

        @pl.when(self.bit[i] == 1)
        def _():
            self.states[i][part] = (factor * self.landed(state, chunk)).astype(BF)

        @pl.when(self.bit[i] == 0)
        def _():
            self.states[i][part] = jnp.zeros((self.count, DH, DH), BF)
            self.sum[part] += factor * self.landed(term, chunk)

    def cross(self, chunk):
        part = self.part(chunk)
        self.sum[part] = jnp.zeros((self.count, DH, DH), F32)
        for i in self.low:
            self.read(i, chunk, ("R", i), ("L", i))
        first = self.head_bits
        value = self.total[part].astype(F32)
        for i in self.low:
            value = value + jnp.where(self.bit[i] == 1, self.landed(("R", i), chunk), 0.0)
        value = value + jnp.where(self.has_right, self.landed(("TL", 0), chunk), 0.0)
        self.store(("T", first), chunk, value)
        for j in self.high:

            @pl.when(self.bit[j] == 1)
            def _(j=j):
                value = self.products[j][part].astype(F32)
                value = value + jnp.where(self.has_left, self.landed(("PR", j), chunk), 0.0)
                value = value + jnp.where(self.has_right, self.landed(("PL", j), chunk), 0.0)
                self.store((("P", j), first), chunk, value)

        self.start(chunk, [("T", first)] + [(("P", j), first) for j in self.high])

    def arrive(self, i, chunk):
        part = self.part(chunk)
        above = range(i + 1, self.cross_bits)
        self.wait(chunk, [("T", i), (("P", i), i)] + [(("P", j), i) for j in above])
        if len(above):
            self.add(("T", i + 1), chunk, ("T", i), self.bit[i] >= 0, ("T", i))
            for j in above:
                self.add((("P", j), i + 1), chunk, (("P", j), i), self.bit[j] == 1, (("P", j), i))
            self.start(chunk, [("T", i + 1)] + [(("P", j), i + 1) for j in above])
        self.read(i, chunk, ("T", i), (("P", i), i))
        if not len(above):
            self.adjoint[part] = self.sum[part].astype(BF)

    def advance(self, time):
        def at(offset, event):
            chunk = time - offset

            @pl.when((chunk >= 0) & (chunk < self.chunks))
            def _():
                event(chunk)

        at(self.z, self.rightward)
        at(self.size - 1 - self.z, self.leftward)
        at(self.size - 1, self.cross)
        for i in self.high:
            at(self.size + 1 + 2 * (i - self.head_bits), functools.partial(self.arrive, i))

    def finish(self, steps):
        def late(time, carry):
            self.advance(time)
            return carry

        if self.last_time >= steps:
            lax.fori_loop(steps, self.last_time + 1, late, 0)

        def body(chunk, carry):
            for key, device, sends, _ in self.transfers():
                source = self.landing.at[self.lands[key]]
                pl.when(sends)(
                    lambda k=key, d=device, r=source: self.copy(k, chunk, d, r).wait_send()
                )
            return carry

        lax.fori_loop(0, self.chunks, body, 0)


def local_kernel(stretches, exchange, *refs):
    cross_bits = exchange.cross_bits
    q_ref, k_ref, v_ref, g_ref, w_ref = refs[:5]
    sources = refs[5 : 6 + cross_bits]
    outs = refs[6 + cross_bits :]
    att_ref, dq_ref, dk_ref, dv_ref, gw_ref = outs[:5]
    states_out = outs[5 : 5 + cross_bits]
    adjoint_out, wr = outs[5 + cross_bits : 7 + cross_bits]
    exchange.bind(sources, states_out, adjoint_out, outs[7 + cross_bits :])
    step = pl.program_id(0)
    head = step
    local_bits = stretches.bit_length() - 1
    width = w_ref.shape[1]

    @pl.when(step == 0)
    def _():
        gw_ref[...] = jnp.zeros_like(gw_ref)

    pl.when(step == 0)(exchange.greet)
    exchange.advance(step)
    wr[...] = head_weights(w_ref, head)

    def rows(ref, n, count=1):
        return ref[n * C : (n + count) * C, :]

    def weighted(n, level):
        return (wr[n * C : (n + 1) * C, level : level + 1] * rows(q_ref, n).astype(F32)).astype(BF)

    sums = {}
    for n in range(stretches - 1):
        sums[0, n] = tn(rows(k_ref, n), rows(v_ref, n))
    for b in range(1, local_bits):
        for m in range(stretches >> b):
            if (b - 1, 2 * m + 1) in sums:
                sums[b, m] = sums[b - 1, 2 * m] + sums[b - 1, 2 * m + 1]
    states, adjoints, wq = {}, {}, {}
    for b in range(local_bits):
        for group in range(stretches >> (b + 1)):
            states[b, group] = (level_scale(b + 1) * sums[b, 2 * group]).astype(BF)
            first = (2 * group + 1) << b
            for n in range(first, first + (1 << b)):
                wq[b, n] = weighted(n, b + 1)
            up = cat([wq[b, n] for n in range(first, first + (1 << b))], 0)
            adjoints[b, group] = level_scale(b + 1) * tn(rows(g_ref, first, 1 << b), up)

    row = lax.broadcasted_iota(jnp.int32, (C, C), 0)
    col = lax.broadcasted_iota(jnp.int32, (C, C), 1)
    mask = jnp.where(col <= row, level_scale(0), 0.0).astype(F32)
    for n in range(stretches):
        q, k, v, g = (rows(ref, n) for ref in (q_ref, k_ref, v_ref, g_ref))
        here = slice(n * C, (n + 1) * C)
        bits = [b for b in range(local_bits) if n >> b & 1]
        read = [states[b, n >> (b + 1)] for b in bits]
        scores = nt(q, k) * mask
        grads = nt(g, v)
        w0 = wr[here, 0:1]
        probs = (w0 * scores).astype(BF)
        gscores = (w0 * (grads * mask)).astype(BF)
        att = nn(cat([probs] + [wq[b, n] for b in bits], 1), cat([v] + read, 0))
        dq = nn(gscores, k)
        marks = [(scores * grads).astype(BF)]
        q32 = q.astype(F32)
        for b, state in zip(bits, read):
            back = nt(g, state)
            dq = dq + wr[here, b + 1 : b + 2] * back
            marks.append((q32 * back).astype(BF))
        picks = [pick(C, head, level, width) for level in [0] + [b + 1 for b in bits]]
        gw_ref[here, :] += nn(cat(marks, 1), cat(picks, 0))
        dk = tn(gscores, q)
        dv = tn(probs, g)
        adjoint = None
        for b in range(local_bits):
            if not n >> b & 1:
                term = adjoints[b, n >> (b + 1)]
                adjoint = term if adjoint is None else adjoint + term
        if adjoint is not None:
            adjoint = adjoint.astype(BF)
            dk = dk + nn(v, adjoint)
            dv = dv + nt(k, adjoint)
        att_ref[here, :] = att.astype(BF)
        dq_ref[here, :] = dq.astype(BF)
        dk_ref[here, :] = dk.astype(BF)
        dv_ref[here, :] = dv.astype(BF)

    @pl.when(step == pl.num_programs(0) - 1)
    def _():
        exchange.finish(exchange.heads)


def local_call(query, key, value, grad_out, weights, sums, head_bits):
    tokens = query.shape[0]
    stretches = tokens // C
    heads = query.shape[1] // DH
    cross_bits = len(sums) - 1
    exchange = Exchange(stretches.bit_length() - 1, cross_bits, head_bits, heads, heads // 2)
    column = pl.BlockSpec((tokens, DH), lambda h: (0, h))
    whole = pl.BlockSpec(weights.shape, lambda h: (0, 0))
    squares = pl.BlockSpec((heads, DH, DH), lambda h: (0, 0, 0))
    shape = jax.ShapeDtypeStruct(query.shape, BF)
    square = jax.ShapeDtypeStruct((heads, DH, DH), BF)
    return pl.pallas_call(
        functools.partial(local_kernel, stretches, exchange),
        grid=(heads,),
        in_specs=[column] * 4 + [whole] + [squares] * (cross_bits + 1),
        out_specs=[column] * 4 + [whole] + [squares] * (cross_bits + 1),
        out_shape=[shape] * 4
        + [jax.ShapeDtypeStruct(weights.shape, F32)]
        + [square] * (cross_bits + 1),
        scratch_shapes=[pltpu.VMEM(weights.shape, F32)] + exchange.scratch(),
        compiler_params=pltpu.CompilerParams(
            vmem_limit_bytes=VMEM_LIMIT, collective_id=0, has_side_effects=True
        ),
        name="local",
    )(query, key, value, grad_out, weights, *sums)


def cross_kernel(local_bits, cross_bits, chunks, *refs):
    q_ref, k_ref, v_ref, g_ref, w_ref = refs[:5]
    att_in, dq_in, dk_in, dv_in = refs[5:9]
    gw_in = refs[9 : 9 + chunks]
    states = refs[9 + chunks : 9 + chunks + cross_bits]
    adjoint = refs[9 + chunks + cross_bits]
    att_ref, dq_ref, dk_ref, dv_ref, gw_ref, acc, wr = refs[10 + chunks + cross_bits :]
    head = pl.program_id(0)
    width = w_ref.shape[1]

    @pl.when(head == 0)
    def _():
        total = gw_in[0][...]
        for other in gw_in[1:]:
            total = total + other[...]
        acc[...] = total

    wr[...] = head_weights(w_ref, head)
    read = cat([state[0] for state in states], 0)
    adj = adjoint[0]
    picks = cat([pick(DH, head, local_bits + 1 + j, width) for j in range(cross_bits)], 0)
    tokens = q_ref.shape[0]
    step = min(2 * C, tokens)
    for start in range(0, tokens, step):
        here = slice(start, start + step)
        q32 = q_ref[here, :].astype(F32)
        columns = [
            wr[here, local_bits + 1 + j : local_bits + 2 + j] for j in range(cross_bits)
        ]
        att = att_in[here, :].astype(F32) + nn(cat([(w * q32).astype(BF) for w in columns], 1), read)
        back = nt(g_ref[here, :], read)
        dq = dq_in[here, :].astype(F32)
        marks = []
        for j, w in enumerate(columns):
            part = back[:, j * DH : (j + 1) * DH]
            dq = dq + w * part
            marks.append((q32 * part).astype(BF))
        acc[here, :] += nn(cat(marks, 1), picks)
        att_ref[here, :] = att.astype(BF)
        dq_ref[here, :] = dq.astype(BF)
        dk_ref[here, :] = (dk_in[here, :].astype(F32) + nn(v_ref[here, :], adj)).astype(BF)
        dv_ref[here, :] = (dv_in[here, :].astype(F32) + nt(k_ref[here, :], adj)).astype(BF)

    @pl.when(head == pl.num_programs(0) - 1)
    def _():
        gw_ref[...] = acc[...].astype(BF)


def cross_call(query, key, value, grad_out, weights, partial, gws, states, adjoint, local_bits):
    tokens = query.shape[0]
    heads = query.shape[1] // DH
    cross_bits = len(states)
    column = pl.BlockSpec((tokens, DH), lambda h: (0, h))
    whole = pl.BlockSpec(weights.shape, lambda h: (0, 0))
    square = pl.BlockSpec((1, DH, DH), lambda h: (h, 0, 0))
    return pl.pallas_call(
        functools.partial(cross_kernel, local_bits, cross_bits, len(gws)),
        grid=(heads,),
        in_specs=[column] * 4
        + [whole]
        + [column] * 4
        + [whole] * len(gws)
        + [square] * (cross_bits + 1),
        out_specs=[column] * 4 + [whole],
        out_shape=[jax.ShapeDtypeStruct(query.shape, BF)] * 4
        + [jax.ShapeDtypeStruct(weights.shape, BF)],
        scratch_shapes=[pltpu.VMEM(weights.shape, F32), pltpu.VMEM(weights.shape, F32)],
        compiler_params=pltpu.CompilerParams(vmem_limit_bytes=VMEM_LIMIT),
        name="cross",
    )(query, key, value, grad_out, weights, *partial, *gws, *states, adjoint)


def general(query, key, value, grad_out, weights):
    tokens = query.shape[0]
    heads = query.shape[1] // DH
    local_bits = (tokens // C).bit_length() - 1
    cross_bits = LEVELS - 1 - local_bits
    head_bits = lax.axis_size("head").bit_length() - 1
    sums = sums_call(query, key, value, grad_out, weights, heads, local_bits, cross_bits)
    outs = local_call(query, key, value, grad_out, weights, sums, head_bits)
    partial, gw = outs[:4], outs[4]
    states, adjoint = outs[5 : 5 + cross_bits], outs[5 + cross_bits]
    return tuple(
        cross_call(
            query, key, value, grad_out, weights, partial, [gw], states, adjoint, local_bits
        )
    )


GRID = 4
BEGIN, PACE, GAP = 4, 5, 3
T_RIGHT, T_NEXT, T_LEFT, A_RIGHT, A_LEFT, A_LEFT2, P_X, H_CORE, U_CORE, U_X0, U_X1 = range(11)
MESSAGES = 11


class Links:
    def __init__(self, heads, chunks, local_bits):
        self.heads, self.chunks, self.count = heads, chunks, heads // chunks
        self.factors = [level_scale(local_bits + 1 + j) for j in range(4)]
        self.stages = [
            self.x_exchange, self.core_exchange, self.chain1, self.chain2, self.chain3,
            self.across, self.arrive,
        ]

    def scratch(self):
        sems = pltpu.SemaphoreType.DMA((MESSAGES, self.chunks))
        return [
            pltpu.VMEM((5, self.heads, DH, DH), BF),
            pltpu.VMEM((self.heads, DH, DH), F32),
            pltpu.VMEM((MESSAGES, self.heads, DH, DH), BF),
            pltpu.VMEM((MESSAGES, self.heads, DH, DH), BF),
            sems,
            sems,
        ]

    def bind(self, states, adjoint, scratch):
        self.states, self.adjoint = states, adjoint
        self.own, self.extra, self.landing, self.sending, self.send_sem, self.recv_sem = scratch
        self.z, self.seq = lax.axis_index("head"), lax.axis_index("seq")
        self.x, self.c = self.seq // 2, self.seq % 2
        z, x, c = self.z, self.x, self.c
        right, left = {"head": z + 1}, {"head": z - 1}
        core = {"seq": x * 2 + 1 - c}
        both = (x == 0) | (c == 0)
        yes = z >= 0
        self.both = both
        self.table = {
            T_RIGHT: (right, z < 3, z > 0),
            T_NEXT: (right, z == 2, z == 3),
            T_LEFT: (left, (z > 0) & both, (z < 3) & both),
            A_RIGHT: (right, (z < 3) & both, (z > 0) & both),
            A_LEFT: (left, z > 0, z < 3),
            A_LEFT2: (left, z == 3, z == 2),
            P_X: ({"seq": c}, x == 1, x == 0),
            H_CORE: (core, (x == 0) | (c == 1), both),
            U_CORE: (core, (c == 0) & yes, c == 1),
            U_X0: ({"seq": 2}, (x == 0) & (c == 1), (x == 1) & (c == 0)),
            U_X1: ({"seq": 3}, (x == 0) & (c == 1), (x == 1) & (c == 1)),
        }

    def greet(self):
        barrier = pltpu.get_barrier_semaphore()
        other = 1 - self.x
        devices = [
            {"head": (self.z + 1) % GRID},
            {"head": (self.z + GRID - 1) % GRID},
            {"seq": self.x * 2 + 1 - self.c},
            {"seq": other * 2 + self.c},
            {"seq": other * 2 + 1 - self.c},
        ]
        for device in devices:
            pl.semaphore_signal(
                barrier, inc=1, device_id=device, device_id_type=pl.DeviceIdType.MESH
            )
        pl.semaphore_wait(barrier, len(devices))

    def part(self, chunk):
        return pl.ds(chunk * self.count, self.count)

    def copy(self, key, chunk, source):
        part = self.part(chunk)
        return pltpu.make_async_remote_copy(
            src_ref=source.at[part],
            dst_ref=self.landing.at[key, part],
            send_sem=self.send_sem.at[key, chunk],
            recv_sem=self.recv_sem.at[key, chunk],
            device_id=self.table[key][0],
            device_id_type=pl.DeviceIdType.MESH,
        )

    def send(self, key, chunk, source, when):
        pl.when(when)(lambda: self.copy(key, chunk, source).start())

    def emit(self, key, chunk, value):
        self.sending[key, self.part(chunk)] = value.astype(BF)
        self.copy(key, chunk, self.sending.at[key]).start()

    def wait(self, chunk, key, when=True):
        receives = self.table[key][2] & when
        pl.when(receives)(lambda: self.copy(key, chunk, self.landing.at[key]).wait_recv())

    def landed(self, key, chunk):
        return self.landing[key, self.part(chunk)].astype(F32)

    def mine(self, index, chunk):
        return self.own[index, self.part(chunk)].astype(F32)

    def first(self, chunk):
        z, x, c = self.z, self.x, self.c
        total = self.own.at[0]
        self.send(T_RIGHT, chunk, total, z == 0)
        self.send(T_NEXT, chunk, total, z == 2)
        self.send(T_LEFT, chunk, total, (z == 3) & self.both)
        self.send(P_X, chunk, self.own.at[4], x == 1)
        self.send(H_CORE, chunk, self.own.at[3], (x == 1) & (c == 1))

    def x_exchange(self, chunk):
        x, c = self.x, self.c
        self.wait(chunk, P_X)
        self.send(H_CORE, chunk, self.landing.at[P_X], (x == 0) & (c == 0))

        @pl.when((x == 0) & (c == 1))
        def _():
            self.emit(H_CORE, chunk, self.mine(3, chunk) + self.landed(P_X, chunk))

    def core_exchange(self, chunk):
        z = self.z
        part = self.part(chunk)
        self.wait(chunk, H_CORE)

        @pl.when(self.both)
        def _():
            value = self.landed(H_CORE, chunk)
            self.extra[part] = value + jnp.where(self.x == 0, self.landed(P_X, chunk), 0.0)

        @pl.when(jnp.logical_not(self.both))
        def _():
            self.extra[part] = jnp.zeros((self.count, DH, DH), F32)

        @pl.when((z == 0) & self.both)
        def _():
            self.emit(A_RIGHT, chunk, self.extra[part])

        @pl.when(z == 3)
        def _():
            self.emit(A_LEFT2, chunk, self.mine(2, chunk) + self.extra[part])
            self.emit(A_LEFT, chunk, self.mine(1, chunk) + self.extra[part])

    def forward_right(self, chunk):
        part = self.part(chunk)

        @pl.when(self.both)
        def _():
            self.emit(A_RIGHT, chunk, self.extra[part] + self.landed(A_RIGHT, chunk))

    def forward_left(self, chunk):
        pl.when(self.both)(
            lambda: self.emit(T_LEFT, chunk, self.mine(0, chunk) + self.landed(T_LEFT, chunk))
        )

    def chain1(self, chunk):
        z = self.z
        part = self.part(chunk)
        self.wait(chunk, T_RIGHT, z == 1)
        self.wait(chunk, T_LEFT, z == 2)
        self.wait(chunk, A_RIGHT, z == 1)
        self.wait(chunk, A_LEFT, z == 2)
        self.wait(chunk, A_LEFT2)

        @pl.when(z == 1)
        def _():
            self.emit(T_RIGHT, chunk, self.mine(0, chunk) + self.landed(T_RIGHT, chunk))
            self.forward_right(chunk)

        @pl.when(z == 2)
        def _():
            self.forward_left(chunk)
            value = self.mine(2, chunk) + self.extra[part] + self.landed(A_LEFT2, chunk)
            self.emit(A_LEFT, chunk, value)

    def chain2(self, chunk):
        z = self.z
        part = self.part(chunk)
        self.wait(chunk, T_RIGHT, z == 2)
        self.wait(chunk, T_LEFT, z == 1)
        self.wait(chunk, A_RIGHT, z == 2)
        self.wait(chunk, A_LEFT, z == 1)

        @pl.when(z == 2)
        def _():
            self.copy(T_RIGHT, chunk, self.landing.at[T_RIGHT]).start()
            self.forward_right(chunk)

        @pl.when(z == 1)
        def _():
            self.forward_left(chunk)
            value = self.mine(1, chunk) + self.extra[part] + self.landed(A_LEFT, chunk)
            self.emit(A_LEFT, chunk, value)

    def chain3(self, chunk):
        z, c = self.z, self.c
        part = self.part(chunk)
        self.wait(chunk, T_RIGHT, z == 3)
        self.wait(chunk, T_NEXT)
        self.wait(chunk, T_LEFT, z == 0)
        self.wait(chunk, A_RIGHT, z == 3)
        self.wait(chunk, A_LEFT, z == 0)
        value = self.extra[part]
        value = value + jnp.where((z > 0) & self.both, self.landed(A_RIGHT, chunk), 0.0)
        value = value + jnp.where(z < 3, self.landed(A_LEFT, chunk), 0.0)
        self.adjoint[part] = value.astype(BF)

        @pl.when(self.both)
        def _():
            value = self.mine(0, chunk)
            value = value + jnp.where(z > 0, self.landed(T_RIGHT, chunk), 0.0)
            value = value + jnp.where(z == 3, self.landed(T_NEXT, chunk), 0.0)
            value = value + jnp.where(z < 3, self.landed(T_LEFT, chunk), 0.0)
            self.sending[U_CORE, part] = value.astype(BF)

        self.send(U_CORE, chunk, self.sending.at[U_CORE], c == 0)

        def read(level, state):
            self.states[part, level * DH : (level + 1) * DH] = state.astype(BF)

        near = jnp.where(z == 1, self.landed(T_RIGHT, chunk), self.landed(T_NEXT, chunk))
        read(0, jnp.where(z % 2 == 1, self.factors[0] * near, 0.0))
        read(1, jnp.where(z >= 2, self.factors[1] * self.landed(T_RIGHT, chunk), 0.0))

    def across(self, chunk):
        part = self.part(chunk)
        self.wait(chunk, U_CORE)
        state = jnp.where(self.c == 1, self.factors[2] * self.landed(U_CORE, chunk), 0.0)
        self.states[part, 2 * DH : 3 * DH] = state.astype(BF)

        @pl.when((self.x == 0) & (self.c == 1))
        def _():
            value = self.sending[U_CORE, part].astype(F32) + self.landed(U_CORE, chunk)
            self.sending[U_X0, part] = value.astype(BF)
            self.copy(U_X0, chunk, self.sending.at[U_X0]).start()
            self.copy(U_X1, chunk, self.sending.at[U_X0]).start()

    def arrive(self, chunk):
        part = self.part(chunk)
        self.wait(chunk, U_X0)
        self.wait(chunk, U_X1)
        state = jnp.where(self.c == 0, self.landed(U_X0, chunk), self.landed(U_X1, chunk))
        state = jnp.where(self.x == 1, self.factors[3] * state, 0.0)
        self.states[part, 3 * DH : 4 * DH] = state.astype(BF)

    def advance(self, time):
        for index, stage in enumerate(self.stages):
            late = time - BEGIN - index * GAP
            chunk = (2 * late + PACE - 1) // PACE

            @pl.when((late >= 0) & (chunk * PACE // 2 == late) & (chunk < self.chunks))
            def _(stage=stage, chunk=chunk):
                stage(chunk)

    def last(self):
        return BEGIN + (self.chunks - 1) * PACE // 2 + (len(self.stages) - 1) * GAP

    def drain(self):
        def body(chunk, carry):
            for key, (_, sends, _) in self.table.items():
                pl.when(sends)(
                    lambda k=key: self.copy(k, chunk, self.landing.at[k]).wait_send()
                )
            return carry

        lax.fori_loop(0, self.chunks, body, 0)


def rows_of_weights(w_ref, wt_ref):
    for start in range(0, w_ref.shape[0], C):
        here = slice(start, start + C)
        wt_ref[:, here] = w_ref[here, :].astype(F32).T


def level_rows(wt_ref, head):
    return wt_ref[pl.ds(pl.multiple_of(head * LEVELS, LEVELS), LEVELS), :]


def stage_kernel(stretches, heads, links, *refs):
    inputs, w_ref = refs[:4], refs[4]
    outs, states_out, adjoint_out = refs[5:10], refs[10], refs[11]
    natural, turned = refs[12:16], refs[16:20]
    wt, wq, load_sem = refs[20:23]
    links.bind(states_out, adjoint_out, refs[23:])
    step = pl.program_id(0)
    head = lax.rem(step, heads)

    def load(i, h):
        return pltpu.make_async_copy(
            inputs[i].at[:, pl.ds(pl.multiple_of(h * DH, DH), DH)],
            natural[i].at[h],
            load_sem.at[i, h],
        )

    @pl.when(step == 0)
    def _():
        def start(h, carry):
            for i in range(4):
                load(i, h).start()
            return carry

        lax.fori_loop(0, heads, start, 0)
        rows_of_weights(w_ref, wt)
        links.greet()

    links.advance(step)
    weight = level_rows(wt, head)
    here = [ref.at[head] for ref in natural], [ref.at[head] for ref in turned]

    @pl.when(step < heads)
    def _():
        for i in range(4):
            load(i, head).wait()
        sums_part(stretches, head, weight, *here, wq, links)

        @pl.when(head % links.count == links.count - 1)
        def _():
            links.first(head // links.count)

    @pl.when(step >= heads)
    def _():
        local_part(stretches, weight, *here, outs)

    @pl.when(step == pl.num_programs(0) - 1)
    def _():
        def late(time, carry):
            links.advance(time)
            return carry

        lax.fori_loop(2 * heads, links.last() + 1, late, 0)
        links.drain()


def sums_part(stretches, head, weight, natural, turned, wq, links):
    local_bits = stretches.bit_length() - 1
    spans = [slice(start, start + 2 * C) for start in range(0, stretches * C, 2 * C)]
    for here in spans:
        flat = natural[0][here, :].T
        turned[0][:, here] = flat
        for j in range(4):
            row = weight[local_bits + 1 + j : local_bits + 2 + j, here]
            wq[j * DH : (j + 1) * DH, here] = (row * flat.astype(F32)).astype(BF)
        turned[3][:, here] = natural[3][here, :].T
    out = nt(turned[3][...], wq[...])
    for i in (1, 2):
        for here in spans:
            turned[i][:, here] = natural[i][here, :].T
    links.own[0, head] = nn(turned[1][...], natural[2][...]).astype(BF)
    for j in range(4):
        links.own[1 + j, head] = (links.factors[j] * out[:, j * DH : (j + 1) * DH]).astype(BF)


def local_part(stretches, weight, natural, turned, outs):
    q_ref, k_ref, v_ref, g_ref = natural
    qt_ref, kt_ref, vt_ref, gt_ref = turned
    att_ref, dq_ref, dk_ref, dv_ref, gw_ref = outs
    local_bits = stretches.bit_length() - 1

    def here(n, count=1):
        return slice(n * C, (n + count) * C)

    def levels(n):
        return [b for b in range(local_bits) if n >> b & 1]

    sums = {}
    for n in range(stretches - 1):
        sums[0, n] = nn(kt_ref[:, here(n)], v_ref[here(n), :])
    for b in range(1, local_bits):
        for m in range(stretches >> b):
            if (b - 1, 2 * m + 1) in sums:
                sums[b, m] = sums[b - 1, 2 * m] + sums[b - 1, 2 * m + 1]
    states, flipped, adjoints, wq = {}, {}, {}, {}
    for b in range(local_bits):
        for group in range(stretches >> (b + 1)):
            state = (level_scale(b + 1) * sums[b, 2 * group]).astype(BF)
            states[b, group], flipped[b, group] = state, state.T
            first, count = (2 * group + 1) << b, 1 << b
            for n in range(first, first + count):
                row = weight[b + 1 : b + 2, here(n)]
                wq[b, n] = (row * qt_ref[:, here(n)].astype(F32)).astype(BF)
            across = cat([wq[b, n] for n in range(first, first + count)], 1)
            adjoints[b, group] = level_scale(b + 1) * nn(across, g_ref[here(first, count), :])

    row = lax.broadcasted_iota(jnp.int32, (C, C), 0)
    col = lax.broadcasted_iota(jnp.int32, (C, C), 1)
    mask = jnp.where(row <= col, level_scale(0), 0.0).astype(F32)
    ready = {}
    for n in range(stretches):
        bits = levels(n)
        scores = nn(k_ref[here(n), :], qt_ref[:, here(n)]) * mask
        rows = cat([v_ref[here(n), :]] + [states[b, n >> (b + 1)] for b in bits], 0)
        seen = nn(rows, gt_ref[:, here(n)])
        grads = seen[:C]
        w0 = weight[0:1, here(n)]
        gws = {0: jnp.sum(scores * grads, axis=0, keepdims=True)}
        extra = 0.0
        for i, b in enumerate(bits):
            back = seen[C + i * DH : C + (i + 1) * DH]
            extra = extra + weight[b + 1 : b + 2, here(n)] * back
            qt32 = qt_ref[:, here(n)].astype(F32)
            gws[b + 1] = jnp.sum(qt32 * back, axis=0, keepdims=True)
        zero = jnp.zeros((1, C), F32)
        gw_ref[0, :, here(n)] = jnp.concatenate([gws.get(l, zero) for l in range(LEVELS)], 0)
        ready[n] = (scores * w0).astype(BF), (grads * mask * w0).astype(BF), extra
    for n in range(stretches):
        bits = levels(n)
        q, k, v, g = (ref[here(n), :] for ref in natural)
        probs, gscores, extra = ready[n]
        left = [vt_ref[:, here(n)]] + [flipped[b, n >> (b + 1)] for b in bits]
        att = nn(cat(left, 1), cat([probs] + [wq[b, n] for b in bits], 0))
        dq = nn(kt_ref[:, here(n)], gscores) + extra
        terms = [adjoints[b, n >> (b + 1)] for b in range(local_bits) if b not in bits]
        if terms:
            adjoint = sum(terms[1:], terms[0]).astype(BF)
            dk = nn(cat([gscores, v], 1), cat([q, adjoint.T], 0))
            dv = nn(cat([probs, k], 1), cat([g, adjoint], 0))
        else:
            dk, dv = nn(gscores, q), nn(probs, g)
        att_ref[0, :, here(n)] = att.astype(BF)
        dq_ref[0, :, here(n)] = dq.astype(BF)
        dk_ref[0, here(n), :] = dk.astype(BF)
        dv_ref[0, here(n), :] = dv.astype(BF)


def stage_call(query, key, value, grad_out, weights):
    tokens = query.shape[0]
    stretches, heads = tokens // C, query.shape[1] // DH
    links = Links(heads, heads // 2, stretches.bit_length() - 1)

    def block(*shape):
        return pl.BlockSpec((1,) + shape, lambda s: (jnp.maximum(s - heads, 0), 0, 0))

    shapes = [(DH, tokens)] * 2 + [(tokens, DH)] * 2 + [(LEVELS, tokens)]
    types = [BF] * 4 + [F32]
    small = [(heads, 4 * DH, DH), (heads, DH, DH)]
    return pl.pallas_call(
        functools.partial(stage_kernel, stretches, heads, links),
        grid=(2 * heads,),
        in_specs=[pl.BlockSpec(memory_space=pl.ANY)] * 4
        + [pl.BlockSpec(weights.shape, lambda s: (0, 0))],
        out_specs=[block(*shape) for shape in shapes]
        + [pl.BlockSpec(shape, lambda s: (0, 0, 0)) for shape in small],
        out_shape=[
            jax.ShapeDtypeStruct((heads,) + shape, kind) for shape, kind in zip(shapes, types)
        ]
        + [jax.ShapeDtypeStruct(shape, BF) for shape in small],
        scratch_shapes=[pltpu.VMEM((heads, tokens, DH), BF)] * 4
        + [pltpu.VMEM((heads, DH, tokens), BF)] * 4
        + [
            pltpu.VMEM(weights.shape[::-1], F32),
            pltpu.VMEM((4 * DH, tokens), BF),
            pltpu.SemaphoreType.DMA((4, heads)),
        ]
        + links.scratch(),
        compiler_params=pltpu.CompilerParams(
            vmem_limit_bytes=VMEM_LIMIT, collective_id=1, has_side_effects=True
        ),
        name="stage",
    )(query, key, value, grad_out, weights)


def merge_kernel(pair, local_bits, *refs):
    q_ref, k_ref, v_ref, g_ref, w_ref = refs[:5]
    att_in, dq_in, dk_in, dv_in, gw_in, states_ref, adjoint_ref = refs[5:12]
    att_ref, dq_ref, dk_ref, dv_ref, gw_ref, wt, gwt = refs[12:]
    step = pl.program_id(0)
    tokens = q_ref.shape[0]

    @pl.when(step == 0)
    def _():
        rows_of_weights(w_ref, wt)

    for i in range(pair):
        head = step * pair + i
        lanes = slice(i * DH, (i + 1) * DH)
        weight = level_rows(wt, head)
        states, adjoint = states_ref[i], adjoint_ref[i]
        flipped = cat([states[j * DH : (j + 1) * DH, :].T for j in range(4)], 1)
        for start in range(0, tokens, 2 * C):
            here = slice(start, start + 2 * C)
            qt32 = q_ref[here, lanes].T.astype(F32)
            levels = [weight[local_bits + 1 + j : local_bits + 2 + j, here] for j in range(4)]
            wq = cat([(row * qt32).astype(BF) for row in levels], 0)
            att = att_in[i, :, here].astype(F32) + nn(flipped, wq)
            back = nn(states, g_ref[here, lanes].T)
            dq = dq_in[i, :, here].astype(F32)
            gws = [gw_in[i, 0 : local_bits + 1, here]]
            for j, row in enumerate(levels):
                part = back[j * DH : (j + 1) * DH, :]
                dq = dq + row * part
                gws.append(jnp.sum(qt32 * part, axis=0, keepdims=True))
            rows = pl.ds(pl.multiple_of(head * LEVELS, LEVELS), LEVELS)
            gwt[rows, here] = jnp.concatenate(gws, 0)
            att_ref[here, lanes] = att.astype(BF).T
            dq_ref[here, lanes] = dq.astype(BF).T
            v, k = v_ref[here, lanes], k_ref[here, lanes]
            dk_ref[here, lanes] = (dk_in[i, here, :].astype(F32) + nn(v, adjoint)).astype(BF)
            dv_ref[here, lanes] = (dv_in[i, here, :].astype(F32) + nt(k, adjoint)).astype(BF)

    @pl.when(step == pl.num_programs(0) - 1)
    def _():
        for start in range(0, tokens, C):
            here = slice(start, start + C)
            gw_ref[here, :] = gwt[:, here].T.astype(BF)


def merge_call(query, key, value, grad_out, weights, outs, local_bits):
    tokens = query.shape[0]
    heads = query.shape[1] // DH
    pair = 2
    column = pl.BlockSpec((tokens, pair * DH), lambda s: (0, s))
    whole = pl.BlockSpec(weights.shape, lambda s: (0, 0))

    def block(array):
        return pl.BlockSpec((pair,) + array.shape[1:], lambda s: (s, 0, 0))

    return pl.pallas_call(
        functools.partial(merge_kernel, pair, local_bits),
        grid=(heads // pair,),
        in_specs=[column] * 4 + [whole] + [block(array) for array in outs],
        out_specs=[column] * 4 + [whole],
        out_shape=[jax.ShapeDtypeStruct(query.shape, BF)] * 4
        + [jax.ShapeDtypeStruct(weights.shape, BF)],
        scratch_shapes=[pltpu.VMEM(weights.shape[::-1], F32)] * 2,
        compiler_params=pltpu.CompilerParams(vmem_limit_bytes=VMEM_LIMIT),
        name="merge",
    )(query, key, value, grad_out, weights, *outs)


def shards(query, key, value, grad_out, weights):
    local_bits = (query.shape[0] // C).bit_length() - 1
    square = lax.axis_size("head") == GRID and lax.axis_size("seq") == GRID
    if not square or local_bits != LEVELS - 5:
        return general(query, key, value, grad_out, weights)
    outs = stage_call(query, key, value, grad_out, weights)
    return tuple(merge_call(query, key, value, grad_out, weights, outs, local_bits))


def solution(mesh):
    spec = P(("rep", "seq", "head"), None)
    return jax.shard_map(
        shards, mesh=mesh, in_specs=(spec,) * 5, out_specs=(spec,) * 5, check_vma=False
    )
```

```python
import functools
import math

import jax
import jax.numpy as jnp
from jax import lax
from jax.experimental import pallas as pl
from jax.experimental.pallas import tpu as pltpu
from jax.sharding import PartitionSpec as P

DH = 128
C = 128
LEVELS = 8
VMEM_LIMIT = 60 * 2**20
BF = jnp.bfloat16
F32 = jnp.float32


def level_scale(level):
    if level == 0:
        return 1.0 / math.sqrt(DH * C)
    return 1.0 / math.sqrt(DH * C * 2 ** (level - 1))


def nn(a, b):
    return lax.dot_general(a, b, (((1,), (0,)), ((), ())), preferred_element_type=F32)


def nt(a, b):
    return lax.dot_general(a, b, (((1,), (1,)), ((), ())), preferred_element_type=F32)


def tn(a, b):
    return lax.dot_general(a, b, (((0,), (0,)), ((), ())), preferred_element_type=F32)


def cat(parts, axis):
    return parts[0] if len(parts) == 1 else jnp.concatenate(parts, axis=axis)


def head_weights(w_ref, head):
    width = w_ref.shape[1]
    return pltpu.roll(w_ref[...].astype(F32), lax.rem(width - head * LEVELS, width), 1)


def pick(rows, head, level, width):
    lane = lax.broadcasted_iota(jnp.int32, (rows, width), 1)
    return jnp.where(lane == head * LEVELS + level, 1.0, 0.0).astype(BF)


def sums_kernel(local_bits, q_ref, k_ref, v_ref, g_ref, w_ref, t_ref, *rest):
    p_refs, wr = rest[:-1], rest[-1]
    head = pl.program_id(0)
    wr[...] = head_weights(w_ref, head)
    t_ref[0] = tn(k_ref[...], v_ref[...]).astype(BF)
    q = q_ref[...].astype(F32)
    weighted = [
        (wr[:, local_bits + 1 + j : local_bits + 2 + j] * q).astype(BF) for j in range(len(p_refs))
    ]
    out = tn(g_ref[...], cat(weighted, 1))
    for j, p_ref in enumerate(p_refs):
        p_ref[0] = out[:, j * DH : (j + 1) * DH].astype(BF)


def sums_call(query, key, value, grad_out, weights, heads, local_bits, cross_bits):
    tokens = query.shape[0]
    column = pl.BlockSpec((tokens, DH), lambda h: (0, h))
    square = pl.BlockSpec((1, DH, DH), lambda h: (h, 0, 0))
    outs = [jax.ShapeDtypeStruct((heads, DH, DH), BF)] * (1 + cross_bits)
    return pl.pallas_call(
        functools.partial(sums_kernel, local_bits),
        grid=(heads,),
        in_specs=[column] * 4 + [pl.BlockSpec(weights.shape, lambda h: (0, 0))],
        out_specs=[square] * (1 + cross_bits),
        out_shape=outs,
        scratch_shapes=[pltpu.VMEM(weights.shape, F32)],
        compiler_params=pltpu.CompilerParams(vmem_limit_bytes=VMEM_LIMIT),
        name="sums",
    )(query, key, value, grad_out, weights)


class Exchange:
    def __init__(self, local_bits, cross_bits, head_bits, heads, chunks):
        self.local_bits, self.cross_bits, self.head_bits = local_bits, cross_bits, head_bits
        self.chunks, self.count, self.heads = chunks, heads // chunks, heads
        self.size = 1 << head_bits
        low, high = range(head_bits), range(head_bits, cross_bits)
        self.low, self.high = low, high
        landing = [("R", i) for i in low] + [("PR", j) for j in high]
        landing += [("L", i) for i in low] + [("TL", 0)] + [("PL", j) for j in high]
        landing += [("T", i) for i in high] + [(("P", j), i) for j in high for i in high if i <= j]
        sending = [("TR", 0)] + [("PR", j) for j in high]
        sending += [("L", i) for i in low] + [("TL", 0)] + [("PL", j) for j in high]
        sending += [("T", i) for i in high] + [(("P", j), i) for j in high for i in high if i <= j]
        self.lands = {key: n for n, key in enumerate(landing)}
        self.sends = {key: n for n, key in enumerate(sending)}
        self.last_time = chunks - 1 + self.size + 1 + 2 * (len(high) - 1)

    def scratch(self):
        sems = pltpu.SemaphoreType.DMA((len(self.lands), self.chunks))
        return [
            pltpu.VMEM((len(self.lands), self.heads, DH, DH), BF),
            pltpu.VMEM((len(self.sends), self.heads, DH, DH), BF),
            pltpu.VMEM((self.heads, DH, DH), F32),
            sems,
            sems,
        ]

    def bind(self, sources, states, adjoint, scratch):
        self.total, self.products = sources[0], sources[1:]
        self.states, self.adjoint = states, adjoint
        self.landing, self.sending, self.sum, self.send_sem, self.recv_sem = scratch
        self.z, seq = lax.axis_index("head"), lax.axis_index("seq")
        self.bit = []
        for i in range(self.cross_bits):
            position, stride = self.z, 1 << i
            if i >= self.head_bits:
                position, stride = seq, 1 << (i - self.head_bits)
            self.bit.append((position // stride) % 2)
        self.partner = {
            i: {"seq": seq + (1 - 2 * self.bit[i]) * (1 << (i - self.head_bits))}
            for i in self.high
        }
        self.right, self.left = {"head": self.z + 1}, {"head": self.z - 1}
        self.has_right, self.has_left = self.z < self.size - 1, self.z > 0

    def part(self, chunk):
        return pl.ds(chunk * self.count, self.count)

    def landed(self, key, chunk):
        return self.landing[self.lands[key], self.part(chunk)].astype(F32)

    def store(self, key, chunk, value):
        self.sending[self.sends[key], self.part(chunk)] = value.astype(BF)

    def copy(self, key, chunk, device, source=None):
        slot = self.lands[key]
        if source is None:
            source = self.sending.at[self.sends[key]]
        return pltpu.make_async_remote_copy(
            src_ref=source.at[self.part(chunk)],
            dst_ref=self.landing.at[slot, self.part(chunk)],
            send_sem=self.send_sem.at[slot, chunk],
            recv_sem=self.recv_sem.at[slot, chunk],
            device_id=device,
            device_id_type=pl.DeviceIdType.MESH,
        )

    def transfers(self):
        for i in self.low:
            yield ("R", i), self.right, self.has_right & (((self.z + 1) >> i) % 2 == 1), self.bit[i] == 1
        for j in self.high:
            own = self.bit[j] == 1
            yield ("PR", j), self.right, self.has_right & own, self.has_left & own
        for i in self.low:
            block = self.z % (2 << i)
            yield ("L", i), self.left, block != 0, block != (2 << i) - 1
        yield ("TL", 0), self.left, self.has_left, self.has_right
        for j in self.high:
            own = self.bit[j] == 1
            yield ("PL", j), self.left, self.has_left & own, self.has_right & own
        for i in self.high:
            up, down, always = self.bit[i] == 1, self.bit[i] == 0, self.bit[i] >= 0
            last = i == self.cross_bits - 1
            yield ("T", i), self.partner[i], (down if last else always), (up if last else always)
            yield (("P", i), i), self.partner[i], up, down
            for j in range(i + 1, self.cross_bits):
                own = self.bit[j] == 1
                yield (("P", j), i), self.partner[i], own, own

    def greet(self):
        barrier = pltpu.get_barrier_semaphore()

        def signal(device):
            pl.semaphore_signal(
                barrier, inc=1, device_id=device, device_id_type=pl.DeviceIdType.MESH
            )

        for i in self.high:
            signal(self.partner[i])
        signal({"head": lax.rem(self.z + 1, self.size)})
        signal({"head": lax.rem(self.z + self.size - 1, self.size)})
        pl.semaphore_wait(barrier, len(self.high) + 2)

    def wait(self, chunk, kinds):
        for key, device, _, receives in self.transfers():
            if key in kinds:
                own = self.landing.at[self.lands[key]]
                pl.when(receives)(
                    lambda k=key, d=device, r=own: self.copy(k, chunk, d, r).wait_recv()
                )

    def start(self, chunk, kinds):
        for key, device, sends, _ in self.transfers():
            if key in kinds:
                pl.when(sends)(lambda k=key, d=device: self.copy(k, chunk, d).start())

    def chain(self, key, chunk, own, receives):
        @pl.when(receives)
        def _():
            self.store(key, chunk, own.astype(F32) + self.landed(key, chunk))

        @pl.when(jnp.logical_not(receives))
        def _():
            self.store(key, chunk, own)

    def rightward(self, chunk):
        part = self.part(chunk)
        self.wait(chunk, [("R", i) for i in self.low] + [("PR", j) for j in self.high])
        for i in self.low:
            @pl.when(self.z % (2 << i) == (1 << i) - 1)
            def _(i=i):
                value = self.total[part].astype(F32)
                for k in range(i):
                    value = value + self.landed(("R", k), chunk)
                self.store(("TR", 0), chunk, value)
                self.copy(
                    ("R", i), chunk, self.right, self.sending.at[self.sends["TR", 0]]
                ).start()

            @pl.when((self.bit[i] == 1) & (self.z % (1 << i) != (1 << i) - 1))
            def _(i=i):
                self.copy(
                    ("R", i), chunk, self.right, self.landing.at[self.lands["R", i]]
                ).start()

        for j in self.high:

            @pl.when((self.bit[j] == 1) & self.has_right)
            def _(j=j):
                self.chain(("PR", j), chunk, self.products[j][part], self.has_left)

        self.start(chunk, [("PR", j) for j in self.high])

    def leftward(self, chunk):
        part = self.part(chunk)
        keys = [("L", i) for i in self.low] + [("TL", 0)] + [("PL", j) for j in self.high]
        self.wait(chunk, keys)
        for i in self.low:
            block = self.z % (2 << i)

            @pl.when(self.bit[i] == 1)
            def _(i=i, block=block):
                self.chain(("L", i), chunk, self.products[i][part], block != (2 << i) - 1)
                self.copy(("L", i), chunk, self.left).start()

            @pl.when((self.bit[i] == 0) & (block != 0))
            def _(i=i):
                self.copy(("L", i), chunk, self.left, self.landing.at[self.lands["L", i]]).start()

        @pl.when(self.has_left)
        def _():
            self.chain(("TL", 0), chunk, self.total[part], self.has_right)

        for j in self.high:

            @pl.when((self.bit[j] == 1) & self.has_left)
            def _(j=j):
                self.chain(("PL", j), chunk, self.products[j][part], self.has_right)

        self.start(chunk, [("TL", 0)] + [("PL", j) for j in self.high])

    def add(self, key, chunk, source, receives, first=None):
        @pl.when(receives)
        def _():
            base = self.sending[self.sends[first or key], self.part(chunk)].astype(F32)
            self.store(key, chunk, base + self.landed(source, chunk))

    def read(self, i, chunk, state, term):
        part = self.part(chunk)
        factor = level_scale(self.local_bits + i + 1)

        @pl.when(self.bit[i] == 1)
        def _():
            self.states[i][part] = (factor * self.landed(state, chunk)).astype(BF)

        @pl.when(self.bit[i] == 0)
        def _():
            self.states[i][part] = jnp.zeros((self.count, DH, DH), BF)
            self.sum[part] += factor * self.landed(term, chunk)

    def cross(self, chunk):
        part = self.part(chunk)
        self.sum[part] = jnp.zeros((self.count, DH, DH), F32)
        for i in self.low:
            self.read(i, chunk, ("R", i), ("L", i))
        first = self.head_bits
        value = self.total[part].astype(F32)
        for i in self.low:
            value = value + jnp.where(self.bit[i] == 1, self.landed(("R", i), chunk), 0.0)
        value = value + jnp.where(self.has_right, self.landed(("TL", 0), chunk), 0.0)
        self.store(("T", first), chunk, value)
        for j in self.high:

            @pl.when(self.bit[j] == 1)
            def _(j=j):
                value = self.products[j][part].astype(F32)
                value = value + jnp.where(self.has_left, self.landed(("PR", j), chunk), 0.0)
                value = value + jnp.where(self.has_right, self.landed(("PL", j), chunk), 0.0)
                self.store((("P", j), first), chunk, value)

        self.start(chunk, [("T", first)] + [(("P", j), first) for j in self.high])

    def arrive(self, i, chunk):
        part = self.part(chunk)
        above = range(i + 1, self.cross_bits)
        self.wait(chunk, [("T", i), (("P", i), i)] + [(("P", j), i) for j in above])
        if len(above):
            self.add(("T", i + 1), chunk, ("T", i), self.bit[i] >= 0, ("T", i))
            for j in above:
                self.add((("P", j), i + 1), chunk, (("P", j), i), self.bit[j] == 1, (("P", j), i))
            self.start(chunk, [("T", i + 1)] + [(("P", j), i + 1) for j in above])
        self.read(i, chunk, ("T", i), (("P", i), i))
        if not len(above):
            self.adjoint[part] = self.sum[part].astype(BF)

    def advance(self, time):
        def at(offset, event):
            chunk = time - offset

            @pl.when((chunk >= 0) & (chunk < self.chunks))
            def _():
                event(chunk)

        at(self.z, self.rightward)
        at(self.size - 1 - self.z, self.leftward)
        at(self.size - 1, self.cross)
        for i in self.high:
            at(self.size + 1 + 2 * (i - self.head_bits), functools.partial(self.arrive, i))

    def finish(self, steps):
        def late(time, carry):
            self.advance(time)
            return carry

        if self.last_time >= steps:
            lax.fori_loop(steps, self.last_time + 1, late, 0)

        def body(chunk, carry):
            for key, device, sends, _ in self.transfers():
                source = self.landing.at[self.lands[key]]
                pl.when(sends)(
                    lambda k=key, d=device, r=source: self.copy(k, chunk, d, r).wait_send()
                )
            return carry

        lax.fori_loop(0, self.chunks, body, 0)


def local_kernel(stretches, exchange, *refs):
    cross_bits = exchange.cross_bits
    q_ref, k_ref, v_ref, g_ref, w_ref = refs[:5]
    sources = refs[5 : 6 + cross_bits]
    outs = refs[6 + cross_bits :]
    att_ref, dq_ref, dk_ref, dv_ref, gw_ref = outs[:5]
    states_out = outs[5 : 5 + cross_bits]
    adjoint_out, wr = outs[5 + cross_bits : 7 + cross_bits]
    exchange.bind(sources, states_out, adjoint_out, outs[7 + cross_bits :])
    step = pl.program_id(0)
    head = step
    local_bits = stretches.bit_length() - 1
    width = w_ref.shape[1]

    @pl.when(step == 0)
    def _():
        gw_ref[...] = jnp.zeros_like(gw_ref)

    pl.when(step == 0)(exchange.greet)
    exchange.advance(step)
    wr[...] = head_weights(w_ref, head)

    def rows(ref, n, count=1):
        return ref[n * C : (n + count) * C, :]

    def weighted(n, level):
        return (wr[n * C : (n + 1) * C, level : level + 1] * rows(q_ref, n).astype(F32)).astype(BF)

    sums = {}
    for n in range(stretches - 1):
        sums[0, n] = tn(rows(k_ref, n), rows(v_ref, n))
    for b in range(1, local_bits):
        for m in range(stretches >> b):
            if (b - 1, 2 * m + 1) in sums:
                sums[b, m] = sums[b - 1, 2 * m] + sums[b - 1, 2 * m + 1]
    states, adjoints, wq = {}, {}, {}
    for b in range(local_bits):
        for group in range(stretches >> (b + 1)):
            states[b, group] = (level_scale(b + 1) * sums[b, 2 * group]).astype(BF)
            first = (2 * group + 1) << b
            for n in range(first, first + (1 << b)):
                wq[b, n] = weighted(n, b + 1)
            up = cat([wq[b, n] for n in range(first, first + (1 << b))], 0)
            adjoints[b, group] = level_scale(b + 1) * tn(rows(g_ref, first, 1 << b), up)

    row = lax.broadcasted_iota(jnp.int32, (C, C), 0)
    col = lax.broadcasted_iota(jnp.int32, (C, C), 1)
    mask = jnp.where(col <= row, level_scale(0), 0.0).astype(F32)
    for n in range(stretches):
        q, k, v, g = (rows(ref, n) for ref in (q_ref, k_ref, v_ref, g_ref))
        here = slice(n * C, (n + 1) * C)
        bits = [b for b in range(local_bits) if n >> b & 1]
        read = [states[b, n >> (b + 1)] for b in bits]
        scores = nt(q, k) * mask
        grads = nt(g, v)
        w0 = wr[here, 0:1]
        probs = (w0 * scores).astype(BF)
        gscores = (w0 * (grads * mask)).astype(BF)
        att = nn(cat([probs] + [wq[b, n] for b in bits], 1), cat([v] + read, 0))
        dq = nn(gscores, k)
        marks = [(scores * grads).astype(BF)]
        q32 = q.astype(F32)
        for b, state in zip(bits, read):
            back = nt(g, state)
            dq = dq + wr[here, b + 1 : b + 2] * back
            marks.append((q32 * back).astype(BF))
        picks = [pick(C, head, level, width) for level in [0] + [b + 1 for b in bits]]
        gw_ref[here, :] += nn(cat(marks, 1), cat(picks, 0))
        dk = tn(gscores, q)
        dv = tn(probs, g)
        adjoint = None
        for b in range(local_bits):
            if not n >> b & 1:
                term = adjoints[b, n >> (b + 1)]
                adjoint = term if adjoint is None else adjoint + term
        if adjoint is not None:
            adjoint = adjoint.astype(BF)
            dk = dk + nn(v, adjoint)
            dv = dv + nt(k, adjoint)
        att_ref[here, :] = att.astype(BF)
        dq_ref[here, :] = dq.astype(BF)
        dk_ref[here, :] = dk.astype(BF)
        dv_ref[here, :] = dv.astype(BF)

    @pl.when(step == pl.num_programs(0) - 1)
    def _():
        exchange.finish(exchange.heads)


def local_call(query, key, value, grad_out, weights, sums, head_bits):
    tokens = query.shape[0]
    stretches = tokens // C
    heads = query.shape[1] // DH
    cross_bits = len(sums) - 1
    exchange = Exchange(stretches.bit_length() - 1, cross_bits, head_bits, heads, heads // 2)
    column = pl.BlockSpec((tokens, DH), lambda h: (0, h))
    whole = pl.BlockSpec(weights.shape, lambda h: (0, 0))
    squares = pl.BlockSpec((heads, DH, DH), lambda h: (0, 0, 0))
    shape = jax.ShapeDtypeStruct(query.shape, BF)
    square = jax.ShapeDtypeStruct((heads, DH, DH), BF)
    return pl.pallas_call(
        functools.partial(local_kernel, stretches, exchange),
        grid=(heads,),
        in_specs=[column] * 4 + [whole] + [squares] * (cross_bits + 1),
        out_specs=[column] * 4 + [whole] + [squares] * (cross_bits + 1),
        out_shape=[shape] * 4
        + [jax.ShapeDtypeStruct(weights.shape, F32)]
        + [square] * (cross_bits + 1),
        scratch_shapes=[pltpu.VMEM(weights.shape, F32)] + exchange.scratch(),
        compiler_params=pltpu.CompilerParams(
            vmem_limit_bytes=VMEM_LIMIT, collective_id=0, has_side_effects=True
        ),
        name="local",
    )(query, key, value, grad_out, weights, *sums)


def cross_kernel(local_bits, cross_bits, chunks, *refs):
    q_ref, k_ref, v_ref, g_ref, w_ref = refs[:5]
    att_in, dq_in, dk_in, dv_in = refs[5:9]
    gw_in = refs[9 : 9 + chunks]
    states = refs[9 + chunks : 9 + chunks + cross_bits]
    adjoint = refs[9 + chunks + cross_bits]
    att_ref, dq_ref, dk_ref, dv_ref, gw_ref, acc, wr = refs[10 + chunks + cross_bits :]
    head = pl.program_id(0)
    width = w_ref.shape[1]

    @pl.when(head == 0)
    def _():
        total = gw_in[0][...]
        for other in gw_in[1:]:
            total = total + other[...]
        acc[...] = total

    wr[...] = head_weights(w_ref, head)
    read = cat([state[0] for state in states], 0)
    adj = adjoint[0]
    picks = cat([pick(DH, head, local_bits + 1 + j, width) for j in range(cross_bits)], 0)
    tokens = q_ref.shape[0]
    step = min(2 * C, tokens)
    for start in range(0, tokens, step):
        here = slice(start, start + step)
        q32 = q_ref[here, :].astype(F32)
        columns = [
            wr[here, local_bits + 1 + j : local_bits + 2 + j] for j in range(cross_bits)
        ]
        att = att_in[here, :].astype(F32) + nn(cat([(w * q32).astype(BF) for w in columns], 1), read)
        back = nt(g_ref[here, :], read)
        dq = dq_in[here, :].astype(F32)
        marks = []
        for j, w in enumerate(columns):
            part = back[:, j * DH : (j + 1) * DH]
            dq = dq + w * part
            marks.append((q32 * part).astype(BF))
        acc[here, :] += nn(cat(marks, 1), picks)
        att_ref[here, :] = att.astype(BF)
        dq_ref[here, :] = dq.astype(BF)
        dk_ref[here, :] = (dk_in[here, :].astype(F32) + nn(v_ref[here, :], adj)).astype(BF)
        dv_ref[here, :] = (dv_in[here, :].astype(F32) + nt(k_ref[here, :], adj)).astype(BF)

    @pl.when(head == pl.num_programs(0) - 1)
    def _():
        gw_ref[...] = acc[...].astype(BF)


def cross_call(query, key, value, grad_out, weights, partial, gws, states, adjoint, local_bits):
    tokens = query.shape[0]
    heads = query.shape[1] // DH
    cross_bits = len(states)
    column = pl.BlockSpec((tokens, DH), lambda h: (0, h))
    whole = pl.BlockSpec(weights.shape, lambda h: (0, 0))
    square = pl.BlockSpec((1, DH, DH), lambda h: (h, 0, 0))
    return pl.pallas_call(
        functools.partial(cross_kernel, local_bits, cross_bits, len(gws)),
        grid=(heads,),
        in_specs=[column] * 4
        + [whole]
        + [column] * 4
        + [whole] * len(gws)
        + [square] * (cross_bits + 1),
        out_specs=[column] * 4 + [whole],
        out_shape=[jax.ShapeDtypeStruct(query.shape, BF)] * 4
        + [jax.ShapeDtypeStruct(weights.shape, BF)],
        scratch_shapes=[pltpu.VMEM(weights.shape, F32), pltpu.VMEM(weights.shape, F32)],
        compiler_params=pltpu.CompilerParams(vmem_limit_bytes=VMEM_LIMIT),
        name="cross",
    )(query, key, value, grad_out, weights, *partial, *gws, *states, adjoint)


def general(query, key, value, grad_out, weights):
    tokens = query.shape[0]
    heads = query.shape[1] // DH
    local_bits = (tokens // C).bit_length() - 1
    cross_bits = LEVELS - 1 - local_bits
    head_bits = lax.axis_size("head").bit_length() - 1
    sums = sums_call(query, key, value, grad_out, weights, heads, local_bits, cross_bits)
    outs = local_call(query, key, value, grad_out, weights, sums, head_bits)
    partial, gw = outs[:4], outs[4]
    states, adjoint = outs[5 : 5 + cross_bits], outs[5 + cross_bits]
    return tuple(
        cross_call(
            query, key, value, grad_out, weights, partial, [gw], states, adjoint, local_bits
        )
    )


GRID = 4
T_RIGHT, T_NEXT, T_LEFT, A_RIGHT, A_LEFT, A_LEFT2, P_X, H_CORE, U_CORE, U_X0, U_X1 = range(11)
MESSAGES = 11


class Links:
    def __init__(self, heads, chunks, local_bits):
        self.heads, self.chunks, self.count = heads, chunks, heads // chunks
        self.factors = [level_scale(local_bits + 1 + j) for j in range(4)]
        self.stages = [
            (self.totals1, 5, 2),
            (self.totals2, 9, 2),
            (self.totals3, 17, 4),
            (self.across, 20, 4),
            (self.arrive, 24, 4),
            (self.x_exchange, 5, 2),
            (self.core_exchange, 10, 3),
            (self.adjoint1, 15, 3),
            (self.adjoint2, 20, 3),
            (self.adjoint3, 26, 4),
        ]

    def scratch(self):
        return [
            pltpu.VMEM((5, self.heads, DH, DH), BF),
            pltpu.VMEM((self.heads, DH, DH), F32),
            pltpu.VMEM((MESSAGES, self.heads, DH, DH), BF),
            pltpu.VMEM((MESSAGES, self.heads, DH, DH), BF),
            pltpu.SemaphoreType.DMA((MESSAGES,)),
            pltpu.SemaphoreType.DMA((MESSAGES, self.chunks)),
        ]

    def bind(self, states, adjoint, scratch):
        self.states, self.adjoint = states, adjoint
        self.own, self.extra, self.landing, self.sending, self.send_sem, self.recv_sem = scratch
        self.z, self.seq = lax.axis_index("head"), lax.axis_index("seq")
        self.x, self.c = self.seq // 2, self.seq % 2
        z, x, c = self.z, self.x, self.c
        right, left = {"head": z + 1}, {"head": z - 1}
        core = {"seq": x * 2 + 1 - c}
        both = (x == 0) | (c == 0)
        yes = z >= 0
        self.both = both
        self.table = {
            T_RIGHT: (right, z < 3, z > 0),
            T_NEXT: (right, z == 2, z == 3),
            T_LEFT: (left, (z > 0) & both, (z < 3) & both),
            A_RIGHT: (right, (z < 3) & both, (z > 0) & both),
            A_LEFT: (left, z > 0, z < 3),
            A_LEFT2: (left, z == 3, z == 2),
            P_X: ({"seq": c}, x == 1, x == 0),
            H_CORE: (core, (x == 0) | (c == 1), both),
            U_CORE: (core, (c == 0) & yes, c == 1),
            U_X0: ({"seq": 2}, (x == 0) & (c == 1), (x == 1) & (c == 0)),
            U_X1: ({"seq": 3}, (x == 0) & (c == 1), (x == 1) & (c == 1)),
        }

    def greet(self):
        barrier = pltpu.get_barrier_semaphore()
        other = 1 - self.x
        devices = [
            {"head": (self.z + 1) % GRID},
            {"head": (self.z + GRID - 1) % GRID},
            {"seq": self.x * 2 + 1 - self.c},
            {"seq": other * 2 + self.c},
            {"seq": other * 2 + 1 - self.c},
        ]
        for device in devices:
            pl.semaphore_signal(
                barrier, inc=1, device_id=device, device_id_type=pl.DeviceIdType.MESH
            )
        pl.semaphore_wait(barrier, len(devices))

    def part(self, chunk):
        return pl.ds(chunk * self.count, self.count)

    def copy(self, key, chunk, source, part=None):
        part = self.part(chunk) if part is None else part
        return pltpu.make_async_remote_copy(
            src_ref=source.at[part],
            dst_ref=self.landing.at[key, part],
            send_sem=self.send_sem.at[key],
            recv_sem=self.recv_sem.at[key, chunk],
            device_id=self.table[key][0],
            device_id_type=pl.DeviceIdType.MESH,
        )

    def send(self, key, chunk, source, when):
        pl.when(when)(lambda: self.copy(key, chunk, source).start())

    def emit(self, key, chunk, value):
        self.sending[key, self.part(chunk)] = value.astype(BF)
        self.copy(key, chunk, self.sending.at[key]).start()

    def wait(self, chunk, key, when=True):
        receives = self.table[key][2] & when
        pl.when(receives)(lambda: self.copy(key, chunk, self.landing.at[key]).wait_recv())

    def landed(self, key, chunk):
        return self.landing[key, self.part(chunk)].astype(F32)

    def mine(self, index, chunk):
        return self.own[index, self.part(chunk)].astype(F32)

    def first(self, chunk):
        z, x, c = self.z, self.x, self.c
        total = self.own.at[0]
        self.send(T_RIGHT, chunk, total, z == 0)
        self.send(T_NEXT, chunk, total, z == 2)
        self.send(T_LEFT, chunk, total, (z == 3) & self.both)
        self.send(P_X, chunk, self.own.at[4], x == 1)
        self.send(H_CORE, chunk, self.own.at[3], (x == 1) & (c == 1))

    def x_exchange(self, chunk):
        x, c = self.x, self.c
        self.wait(chunk, P_X)
        self.send(H_CORE, chunk, self.landing.at[P_X], (x == 0) & (c == 0))

        @pl.when((x == 0) & (c == 1))
        def _():
            self.emit(H_CORE, chunk, self.mine(3, chunk) + self.landed(P_X, chunk))

    def core_exchange(self, chunk):
        z = self.z
        part = self.part(chunk)
        self.wait(chunk, H_CORE)

        @pl.when(self.both)
        def _():
            value = self.landed(H_CORE, chunk)
            self.extra[part] = value + jnp.where(self.x == 0, self.landed(P_X, chunk), 0.0)

        @pl.when(jnp.logical_not(self.both))
        def _():
            self.extra[part] = jnp.zeros((self.count, DH, DH), F32)

        @pl.when((z == 0) & self.both)
        def _():
            self.emit(A_RIGHT, chunk, self.extra[part])

        @pl.when(z == 3)
        def _():
            self.emit(A_LEFT2, chunk, self.mine(2, chunk) + self.extra[part])

    def forward_right(self, chunk):
        part = self.part(chunk)

        @pl.when(self.both)
        def _():
            self.emit(A_RIGHT, chunk, self.extra[part] + self.landed(A_RIGHT, chunk))

    def forward_left(self, chunk):
        pl.when(self.both)(
            lambda: self.emit(T_LEFT, chunk, self.mine(0, chunk) + self.landed(T_LEFT, chunk))
        )

    def totals1(self, chunk):
        z = self.z
        self.wait(chunk, T_RIGHT, z == 1)
        self.wait(chunk, T_LEFT, z == 2)

        @pl.when(z == 1)
        def _():
            self.emit(T_RIGHT, chunk, self.mine(0, chunk) + self.landed(T_RIGHT, chunk))

        pl.when(z == 2)(lambda: self.forward_left(chunk))

    def totals2(self, chunk):
        z = self.z
        self.wait(chunk, T_RIGHT, z == 2)
        self.wait(chunk, T_LEFT, z == 1)
        self.send(T_RIGHT, chunk, self.landing.at[T_RIGHT], z == 2)
        pl.when(z == 1)(lambda: self.forward_left(chunk))

    def totals3(self, chunk):
        z, c = self.z, self.c
        part = self.part(chunk)
        self.wait(chunk, T_RIGHT, z == 3)
        self.wait(chunk, T_NEXT)
        self.wait(chunk, T_LEFT, z == 0)

        @pl.when(self.both)
        def _():
            value = self.mine(0, chunk)
            value = value + jnp.where(z > 0, self.landed(T_RIGHT, chunk), 0.0)
            value = value + jnp.where(z == 3, self.landed(T_NEXT, chunk), 0.0)
            value = value + jnp.where(z < 3, self.landed(T_LEFT, chunk), 0.0)
            self.sending[U_CORE, part] = value.astype(BF)

        self.send(U_CORE, chunk, self.sending.at[U_CORE], c == 0)

        def read(level, state):
            self.states[part, level * DH : (level + 1) * DH] = state.astype(BF)

        near = jnp.where(z == 1, self.landed(T_RIGHT, chunk), self.landed(T_NEXT, chunk))
        read(0, jnp.where(z % 2 == 1, self.factors[0] * near, 0.0))
        read(1, jnp.where(z >= 2, self.factors[1] * self.landed(T_RIGHT, chunk), 0.0))

    def adjoint1(self, chunk):
        z = self.z
        part = self.part(chunk)
        self.wait(chunk, A_RIGHT, z == 1)
        self.wait(chunk, A_LEFT2)

        @pl.when(z == 3)
        def _():
            self.emit(A_LEFT, chunk, self.mine(1, chunk) + self.extra[part])

        pl.when(z == 1)(lambda: self.forward_right(chunk))

        @pl.when(z == 2)
        def _():
            value = self.mine(2, chunk) + self.extra[part] + self.landed(A_LEFT2, chunk)
            self.emit(A_LEFT, chunk, value)

    def adjoint2(self, chunk):
        z = self.z
        part = self.part(chunk)
        self.wait(chunk, A_RIGHT, z == 2)
        self.wait(chunk, A_LEFT, z == 1)
        pl.when(z == 2)(lambda: self.forward_right(chunk))

        @pl.when(z == 1)
        def _():
            value = self.mine(1, chunk) + self.extra[part] + self.landed(A_LEFT, chunk)
            self.emit(A_LEFT, chunk, value)

    def adjoint3(self, chunk):
        z = self.z
        part = self.part(chunk)
        self.wait(chunk, A_RIGHT, z == 3)
        self.wait(chunk, A_LEFT, z % 2 == 0)
        value = self.extra[part]
        value = value + jnp.where((z > 0) & self.both, self.landed(A_RIGHT, chunk), 0.0)
        value = value + jnp.where(z < 3, self.landed(A_LEFT, chunk), 0.0)
        self.adjoint[part] = value.astype(BF)

    def across(self, chunk):
        part = self.part(chunk)
        self.wait(chunk, U_CORE)
        state = jnp.where(self.c == 1, self.factors[2] * self.landed(U_CORE, chunk), 0.0)
        self.states[part, 2 * DH : 3 * DH] = state.astype(BF)

        @pl.when((self.x == 0) & (self.c == 1))
        def _():
            value = self.sending[U_CORE, part].astype(F32) + self.landed(U_CORE, chunk)
            self.sending[U_X0, part] = value.astype(BF)
            self.copy(U_X0, chunk, self.sending.at[U_X0]).start()
            self.copy(U_X1, chunk, self.sending.at[U_X0]).start()

    def arrive(self, chunk):
        part = self.part(chunk)
        self.wait(chunk, U_X0)
        self.wait(chunk, U_X1)
        state = jnp.where(self.c == 0, self.landed(U_X0, chunk), self.landed(U_X1, chunk))
        state = jnp.where(self.x == 1, self.factors[3] * state, 0.0)
        self.states[part, 3 * DH : 4 * DH] = state.astype(BF)

    def advance(self, time):
        for stage, begin, pace in self.stages:
            late = time - begin
            chunk = jnp.right_shift(late * (8192 // pace + 1), 13)
            last = (self.chunks - 1) * pace

            @pl.when((late >= 0) & (late <= last) & (chunk * pace == late))
            def _(stage=stage, chunk=chunk):
                stage(chunk)

    def last(self):
        return max(begin + (self.chunks - 1) * pace for _, begin, pace in self.stages)

    def drain(self):
        whole = pl.ds(0, self.heads)
        for key, (_, sends, _) in self.table.items():
            pl.when(sends)(
                lambda k=key: self.copy(k, 0, self.landing.at[k], whole).wait_send()
            )


def rows_of_weights(w_ref, wt_ref):
    for start in range(0, w_ref.shape[0], C):
        here = slice(start, start + C)
        wt_ref[:, here] = w_ref[here, :].astype(F32).T


def level_rows(wt_ref, head):
    return wt_ref[pl.ds(pl.multiple_of(head * LEVELS, LEVELS), LEVELS), :]


def stage_kernel(stretches, heads, links, *refs):
    inputs, w_ref = refs[:4], refs[4]
    kept, outs, states_out, adjoint_out = refs[5:9], refs[9:14], refs[14], refs[15]
    natural, turned = refs[16:20], refs[20:24]
    wt, wq, load_sem, keep_sem = refs[24:28]
    links.bind(states_out, adjoint_out, refs[28:])
    keeps = [
        pltpu.make_async_copy(source, target, keep_sem.at[i])
        for i, (source, target) in enumerate(
            zip((turned[0], turned[3], natural[1], natural[2]), kept)
        )
    ]
    step = pl.program_id(0)
    head = lax.rem(step, heads)

    def load(i, h):
        return pltpu.make_async_copy(
            inputs[i].at[:, pl.ds(pl.multiple_of(h * DH, DH), DH)],
            natural[i].at[h],
            load_sem.at[i, h],
        )

    @pl.when(step == 0)
    def _():
        def start(h, carry):
            for i in range(4):
                load(i, h).start()
            return carry

        lax.fori_loop(0, heads, start, 0)
        rows_of_weights(w_ref, wt)
        links.greet()

    weight = level_rows(wt, head)
    here = [ref.at[head] for ref in natural], [ref.at[head] for ref in turned]

    @pl.when(step < heads)
    def _():
        links.advance(step)
        for i in range(4):
            load(i, head).wait()
        sums_part(stretches, head, weight, *here, wq, links)

        @pl.when(head % links.count == links.count - 1)
        def _():
            links.first(head // links.count)

    @pl.when(step >= heads)
    def _():
        @pl.when(step == heads)
        def _():
            for keep in keeps:
                keep.start()

        slot = 2 * step - heads
        links.advance(slot)
        local_part(stretches, weight, *here, outs, lambda: links.advance(slot + 1))

    @pl.when(step == pl.num_programs(0) - 1)
    def _():
        def late(time, carry):
            links.advance(time)
            return carry

        for keep in keeps:
            keep.wait()
        lax.fori_loop(3 * heads, max(3 * heads, links.last() + 1), late, 0)
        links.drain()


def sums_part(stretches, head, weight, natural, turned, wq, links):
    local_bits = stretches.bit_length() - 1
    spans = [slice(start, start + 2 * C) for start in range(0, stretches * C, 2 * C)]
    for here in spans:
        flat = natural[0][here, :].T
        turned[0][:, here] = flat
        for j in range(4):
            row = weight[local_bits + 1 + j : local_bits + 2 + j, here]
            wq[j * DH : (j + 1) * DH, here] = (row * flat.astype(F32)).astype(BF)
        turned[3][:, here] = natural[3][here, :].T
    out = nt(turned[3][...], wq[...])
    for i in (1, 2):
        for here in spans:
            turned[i][:, here] = natural[i][here, :].T
    links.own[0, head] = nn(turned[1][...], natural[2][...]).astype(BF)
    for j in range(4):
        links.own[1 + j, head] = (links.factors[j] * out[:, j * DH : (j + 1) * DH]).astype(BF)


def local_part(stretches, weight, natural, turned, outs, between):
    q_ref, k_ref, v_ref, g_ref = natural
    qt_ref, kt_ref, vt_ref, gt_ref = turned
    att_ref, dq_ref, dk_ref, dv_ref, gw_ref = outs
    local_bits = stretches.bit_length() - 1

    def here(n, count=1):
        return slice(n * C, (n + count) * C)

    def levels(n):
        return [b for b in range(local_bits) if n >> b & 1]

    sums = {}
    for n in range(stretches - 1):
        sums[0, n] = nn(kt_ref[:, here(n)], v_ref[here(n), :])
    for b in range(1, local_bits):
        for m in range(stretches >> b):
            if (b - 1, 2 * m + 1) in sums:
                sums[b, m] = sums[b - 1, 2 * m] + sums[b - 1, 2 * m + 1]
    states, flipped, adjoints, wq = {}, {}, {}, {}
    for b in range(local_bits):
        for group in range(stretches >> (b + 1)):
            state = (level_scale(b + 1) * sums[b, 2 * group]).astype(BF)
            states[b, group], flipped[b, group] = state, state.T
            first, count = (2 * group + 1) << b, 1 << b
            for n in range(first, first + count):
                row = weight[b + 1 : b + 2, here(n)]
                wq[b, n] = (row * qt_ref[:, here(n)].astype(F32)).astype(BF)
            across = cat([wq[b, n] for n in range(first, first + count)], 1)
            adjoints[b, group] = level_scale(b + 1) * nn(across, g_ref[here(first, count), :])

    row = lax.broadcasted_iota(jnp.int32, (C, C), 0)
    col = lax.broadcasted_iota(jnp.int32, (C, C), 1)
    mask = jnp.where(row <= col, level_scale(0), 0.0).astype(F32)
    ready = {}
    for n in range(stretches):
        bits = levels(n)
        scores = nn(k_ref[here(n), :], qt_ref[:, here(n)]) * mask
        rows = cat([v_ref[here(n), :]] + [states[b, n >> (b + 1)] for b in bits], 0)
        seen = nn(rows, gt_ref[:, here(n)])
        grads = seen[:C]
        w0 = weight[0:1, here(n)]
        gws = {0: jnp.sum(scores * grads, axis=0, keepdims=True)}
        extra = 0.0
        for i, b in enumerate(bits):
            back = seen[C + i * DH : C + (i + 1) * DH]
            extra = extra + weight[b + 1 : b + 2, here(n)] * back
            qt32 = qt_ref[:, here(n)].astype(F32)
            gws[b + 1] = jnp.sum(qt32 * back, axis=0, keepdims=True)
        zero = jnp.zeros((1, C), F32)
        gw_ref[0, :, here(n)] = jnp.concatenate([gws.get(l, zero) for l in range(LEVELS)], 0)
        ready[n] = (scores * w0).astype(BF), (grads * mask * w0).astype(BF), extra
    between()
    for n in range(stretches):
        bits = levels(n)
        q, k, v, g = (ref[here(n), :] for ref in natural)
        probs, gscores, extra = ready[n]
        left = [vt_ref[:, here(n)]] + [flipped[b, n >> (b + 1)] for b in bits]
        att = nn(cat(left, 1), cat([probs] + [wq[b, n] for b in bits], 0))
        dq = nn(kt_ref[:, here(n)], gscores) + extra
        terms = [adjoints[b, n >> (b + 1)] for b in range(local_bits) if b not in bits]
        if terms:
            adjoint = sum(terms[1:], terms[0]).astype(BF)
            dk = nn(cat([gscores, v], 1), cat([q, adjoint.T], 0))
            dv = nn(cat([probs, k], 1), cat([g, adjoint], 0))
        else:
            dk, dv = nn(gscores, q), nn(probs, g)
        att_ref[0, :, here(n)] = att.astype(BF)
        dq_ref[0, :, here(n)] = dq.astype(BF)
        dk_ref[0, here(n), :] = dk.astype(BF)
        dv_ref[0, here(n), :] = dv.astype(BF)


def stage_call(query, key, value, grad_out, weights):
    tokens = query.shape[0]
    stretches, heads = tokens // C, query.shape[1] // DH
    links = Links(heads, heads // 2, stretches.bit_length() - 1)

    def block(*shape):
        return pl.BlockSpec((1,) + shape, lambda s: (jnp.maximum(s - heads, 0), 0, 0))

    shapes = [(DH, tokens)] * 2 + [(tokens, DH)] * 2 + [(LEVELS, tokens)]
    types = [BF] * 4 + [F32]
    small = [(heads, 4 * DH, DH), (heads, DH, DH)]
    large = [(heads,) + shape for shape in shapes[:4]]
    return pl.pallas_call(
        functools.partial(stage_kernel, stretches, heads, links),
        grid=(2 * heads,),
        in_specs=[pl.BlockSpec(memory_space=pl.ANY)] * 4
        + [pl.BlockSpec(weights.shape, lambda s: (0, 0))],
        out_specs=[pl.BlockSpec(memory_space=pl.ANY)] * 4
        + [block(*shape) for shape in shapes]
        + [pl.BlockSpec(shape, lambda s: (0, 0, 0)) for shape in small],
        out_shape=[jax.ShapeDtypeStruct(shape, BF) for shape in large]
        + [jax.ShapeDtypeStruct((heads,) + shape, kind) for shape, kind in zip(shapes, types)]
        + [jax.ShapeDtypeStruct(shape, BF) for shape in small],
        scratch_shapes=[pltpu.VMEM((heads, tokens, DH), BF)] * 4
        + [pltpu.VMEM((heads, DH, tokens), BF)] * 4
        + [
            pltpu.VMEM(weights.shape[::-1], F32),
            pltpu.VMEM((4 * DH, tokens), BF),
            pltpu.SemaphoreType.DMA((4, heads)),
            pltpu.SemaphoreType.DMA((4,)),
        ]
        + links.scratch(),
        compiler_params=pltpu.CompilerParams(
            vmem_limit_bytes=VMEM_LIMIT, collective_id=1, has_side_effects=True
        ),
        name="stage",
    )(query, key, value, grad_out, weights)


def merge_kernel(pair, local_bits, *refs):
    near, gw_in, states_ref, adjoint_ref, w_ref = refs[:8], *refs[8:12]
    outs, gw_ref, wt, gwt = refs[12:16], *refs[16:]
    step = pl.program_id(0)

    @pl.when(step == 0)
    def _():
        rows_of_weights(w_ref, wt)

    for i in range(pair):
        head = step * pair + i
        rows = pl.ds(pl.multiple_of(head * LEVELS, LEVELS), LEVELS)
        merge_part(
            local_bits, level_rows(wt, head), [ref.at[i] for ref in near], gw_in[i],
            states_ref[i], adjoint_ref[i], outs, slice(i * DH, (i + 1) * DH), gwt.at[rows],
        )

    @pl.when(step == pl.num_programs(0) - 1)
    def _():
        for start in range(0, w_ref.shape[0], C):
            here = slice(start, start + C)
            gw_ref[here, :] = gwt[:, here].T.astype(BF)


def merge_part(local_bits, weight, near, gw_in, states, adjoint, outs, lanes, gwt):
    qt_ref, gt_ref, k_ref, v_ref, att_in, dq_in, dk_in, dv_in = near
    att_ref, dq_ref, dk_ref, dv_ref = outs
    flipped = cat([states[j * DH : (j + 1) * DH, :].T for j in range(4)], 1)
    back_adjoint = adjoint.T
    for start in range(0, k_ref.shape[0], 2 * C):
        here = slice(start, start + 2 * C)
        qt32 = qt_ref[:, here].astype(F32)
        levels = [weight[local_bits + 1 + j : local_bits + 2 + j, here] for j in range(4)]
        wq = cat([(row * qt32).astype(BF) for row in levels], 0)
        att = att_in[:, here].astype(F32) + nn(flipped, wq)
        back = nn(states, gt_ref[:, here])
        dq = dq_in[:, here].astype(F32)
        gws = [gw_in[0 : local_bits + 1, here]]
        for j, row in enumerate(levels):
            part = back[j * DH : (j + 1) * DH, :]
            dq = dq + row * part
            gws.append(jnp.sum(qt32 * part, axis=0, keepdims=True))
        gwt[:, here] = jnp.concatenate(gws, 0)
        att_ref[here, lanes] = att.astype(BF).T
        dq_ref[here, lanes] = dq.astype(BF).T
        dk = dk_in[here, :].astype(F32) + nn(v_ref[here, :], adjoint)
        dv = dv_in[here, :].astype(F32) + nn(k_ref[here, :], back_adjoint)
        dk_ref[here, lanes] = dk.astype(BF)
        dv_ref[here, lanes] = dv.astype(BF)


def merge_call(weights, outs, local_bits):
    heads, tokens = outs[0].shape[0], weights.shape[0]
    pair = 2
    column = pl.BlockSpec((tokens, pair * DH), lambda s: (0, s))
    whole = pl.BlockSpec(weights.shape, lambda s: (0, 0))

    def block(array):
        return pl.BlockSpec((pair,) + array.shape[1:], lambda s: (s, 0, 0))

    return pl.pallas_call(
        functools.partial(merge_kernel, pair, local_bits),
        grid=(heads // pair,),
        in_specs=[block(array) for array in outs] + [whole],
        out_specs=[column] * 4 + [whole],
        out_shape=[jax.ShapeDtypeStruct((tokens, heads * DH), BF)] * 4
        + [jax.ShapeDtypeStruct(weights.shape, BF)],
        scratch_shapes=[pltpu.VMEM(weights.shape[::-1], F32)] * 2,
        compiler_params=pltpu.CompilerParams(vmem_limit_bytes=VMEM_LIMIT),
        name="merge",
    )(*outs, weights)


def shards(query, key, value, grad_out, weights):
    local_bits = (query.shape[0] // C).bit_length() - 1
    square = lax.axis_size("head") == GRID and lax.axis_size("seq") == GRID
    if not square or local_bits != LEVELS - 5:
        return general(query, key, value, grad_out, weights)
    outs = stage_call(query, key, value, grad_out, weights)
    return tuple(merge_call(weights, outs, local_bits))


def solution(mesh):
    spec = P(("rep", "seq", "head"), None)
    return jax.shard_map(
        shards, mesh=mesh, in_specs=(spec,) * 5, out_specs=(spec,) * 5, check_vma=False
    )
```

```python
import functools
import math

import jax
import jax.numpy as jnp
from jax import lax
from jax.experimental import pallas as pl
from jax.experimental.pallas import tpu as pltpu
from jax.sharding import PartitionSpec as P

DH = 128
C = 128
LEVELS = 8
VMEM_LIMIT = 60 * 2**20
BF = jnp.bfloat16
F32 = jnp.float32


def level_scale(level):
    if level == 0:
        return 1.0 / math.sqrt(DH * C)
    return 1.0 / math.sqrt(DH * C * 2 ** (level - 1))


def nn(a, b):
    return lax.dot_general(a, b, (((1,), (0,)), ((), ())), preferred_element_type=F32)


def nt(a, b):
    return lax.dot_general(a, b, (((1,), (1,)), ((), ())), preferred_element_type=F32)


def tn(a, b):
    return lax.dot_general(a, b, (((0,), (0,)), ((), ())), preferred_element_type=F32)


def cat(parts, axis):
    return parts[0] if len(parts) == 1 else jnp.concatenate(parts, axis=axis)


def head_weights(w_ref, head):
    width = w_ref.shape[1]
    return pltpu.roll(w_ref[...].astype(F32), lax.rem(width - head * LEVELS, width), 1)


def pick(rows, head, level, width):
    lane = lax.broadcasted_iota(jnp.int32, (rows, width), 1)
    return jnp.where(lane == head * LEVELS + level, 1.0, 0.0).astype(BF)


def sums_kernel(local_bits, q_ref, k_ref, v_ref, g_ref, w_ref, t_ref, *rest):
    p_refs, wr = rest[:-1], rest[-1]
    head = pl.program_id(0)
    wr[...] = head_weights(w_ref, head)
    t_ref[0] = tn(k_ref[...], v_ref[...]).astype(BF)
    q = q_ref[...].astype(F32)
    weighted = [
        (wr[:, local_bits + 1 + j : local_bits + 2 + j] * q).astype(BF) for j in range(len(p_refs))
    ]
    out = tn(g_ref[...], cat(weighted, 1))
    for j, p_ref in enumerate(p_refs):
        p_ref[0] = out[:, j * DH : (j + 1) * DH].astype(BF)


def sums_call(query, key, value, grad_out, weights, heads, local_bits, cross_bits):
    tokens = query.shape[0]
    column = pl.BlockSpec((tokens, DH), lambda h: (0, h))
    square = pl.BlockSpec((1, DH, DH), lambda h: (h, 0, 0))
    outs = [jax.ShapeDtypeStruct((heads, DH, DH), BF)] * (1 + cross_bits)
    return pl.pallas_call(
        functools.partial(sums_kernel, local_bits),
        grid=(heads,),
        in_specs=[column] * 4 + [pl.BlockSpec(weights.shape, lambda h: (0, 0))],
        out_specs=[square] * (1 + cross_bits),
        out_shape=outs,
        scratch_shapes=[pltpu.VMEM(weights.shape, F32)],
        compiler_params=pltpu.CompilerParams(vmem_limit_bytes=VMEM_LIMIT),
        name="sums",
    )(query, key, value, grad_out, weights)


class Exchange:
    def __init__(self, local_bits, cross_bits, head_bits, heads, chunks):
        self.local_bits, self.cross_bits, self.head_bits = local_bits, cross_bits, head_bits
        self.chunks, self.count, self.heads = chunks, heads // chunks, heads
        self.size = 1 << head_bits
        low, high = range(head_bits), range(head_bits, cross_bits)
        self.low, self.high = low, high
        landing = [("R", i) for i in low] + [("PR", j) for j in high]
        landing += [("L", i) for i in low] + [("TL", 0)] + [("PL", j) for j in high]
        landing += [("T", i) for i in high] + [(("P", j), i) for j in high for i in high if i <= j]
        sending = [("TR", 0)] + [("PR", j) for j in high]
        sending += [("L", i) for i in low] + [("TL", 0)] + [("PL", j) for j in high]
        sending += [("T", i) for i in high] + [(("P", j), i) for j in high for i in high if i <= j]
        self.lands = {key: n for n, key in enumerate(landing)}
        self.sends = {key: n for n, key in enumerate(sending)}
        self.last_time = chunks - 1 + self.size + 1 + 2 * (len(high) - 1)

    def scratch(self):
        sems = pltpu.SemaphoreType.DMA((len(self.lands), self.chunks))
        return [
            pltpu.VMEM((len(self.lands), self.heads, DH, DH), BF),
            pltpu.VMEM((len(self.sends), self.heads, DH, DH), BF),
            pltpu.VMEM((self.heads, DH, DH), F32),
            sems,
            sems,
        ]

    def bind(self, sources, states, adjoint, scratch):
        self.total, self.products = sources[0], sources[1:]
        self.states, self.adjoint = states, adjoint
        self.landing, self.sending, self.sum, self.send_sem, self.recv_sem = scratch
        self.z, seq = lax.axis_index("head"), lax.axis_index("seq")
        self.bit = []
        for i in range(self.cross_bits):
            position, stride = self.z, 1 << i
            if i >= self.head_bits:
                position, stride = seq, 1 << (i - self.head_bits)
            self.bit.append((position // stride) % 2)
        self.partner = {
            i: {"seq": seq + (1 - 2 * self.bit[i]) * (1 << (i - self.head_bits))}
            for i in self.high
        }
        self.right, self.left = {"head": self.z + 1}, {"head": self.z - 1}
        self.has_right, self.has_left = self.z < self.size - 1, self.z > 0

    def part(self, chunk):
        return pl.ds(chunk * self.count, self.count)

    def landed(self, key, chunk):
        return self.landing[self.lands[key], self.part(chunk)].astype(F32)

    def store(self, key, chunk, value):
        self.sending[self.sends[key], self.part(chunk)] = value.astype(BF)

    def copy(self, key, chunk, device, source=None):
        slot = self.lands[key]
        if source is None:
            source = self.sending.at[self.sends[key]]
        return pltpu.make_async_remote_copy(
            src_ref=source.at[self.part(chunk)],
            dst_ref=self.landing.at[slot, self.part(chunk)],
            send_sem=self.send_sem.at[slot, chunk],
            recv_sem=self.recv_sem.at[slot, chunk],
            device_id=device,
            device_id_type=pl.DeviceIdType.MESH,
        )

    def transfers(self):
        for i in self.low:
            yield ("R", i), self.right, self.has_right & (((self.z + 1) >> i) % 2 == 1), self.bit[i] == 1
        for j in self.high:
            own = self.bit[j] == 1
            yield ("PR", j), self.right, self.has_right & own, self.has_left & own
        for i in self.low:
            block = self.z % (2 << i)
            yield ("L", i), self.left, block != 0, block != (2 << i) - 1
        yield ("TL", 0), self.left, self.has_left, self.has_right
        for j in self.high:
            own = self.bit[j] == 1
            yield ("PL", j), self.left, self.has_left & own, self.has_right & own
        for i in self.high:
            up, down, always = self.bit[i] == 1, self.bit[i] == 0, self.bit[i] >= 0
            last = i == self.cross_bits - 1
            yield ("T", i), self.partner[i], (down if last else always), (up if last else always)
            yield (("P", i), i), self.partner[i], up, down
            for j in range(i + 1, self.cross_bits):
                own = self.bit[j] == 1
                yield (("P", j), i), self.partner[i], own, own

    def greet(self):
        barrier = pltpu.get_barrier_semaphore()

        def signal(device):
            pl.semaphore_signal(
                barrier, inc=1, device_id=device, device_id_type=pl.DeviceIdType.MESH
            )

        for i in self.high:
            signal(self.partner[i])
        signal({"head": lax.rem(self.z + 1, self.size)})
        signal({"head": lax.rem(self.z + self.size - 1, self.size)})
        pl.semaphore_wait(barrier, len(self.high) + 2)

    def wait(self, chunk, kinds):
        for key, device, _, receives in self.transfers():
            if key in kinds:
                own = self.landing.at[self.lands[key]]
                pl.when(receives)(
                    lambda k=key, d=device, r=own: self.copy(k, chunk, d, r).wait_recv()
                )

    def start(self, chunk, kinds):
        for key, device, sends, _ in self.transfers():
            if key in kinds:
                pl.when(sends)(lambda k=key, d=device: self.copy(k, chunk, d).start())

    def chain(self, key, chunk, own, receives):
        @pl.when(receives)
        def _():
            self.store(key, chunk, own.astype(F32) + self.landed(key, chunk))

        @pl.when(jnp.logical_not(receives))
        def _():
            self.store(key, chunk, own)

    def rightward(self, chunk):
        part = self.part(chunk)
        self.wait(chunk, [("R", i) for i in self.low] + [("PR", j) for j in self.high])
        for i in self.low:
            @pl.when(self.z % (2 << i) == (1 << i) - 1)
            def _(i=i):
                value = self.total[part].astype(F32)
                for k in range(i):
                    value = value + self.landed(("R", k), chunk)
                self.store(("TR", 0), chunk, value)
                self.copy(
                    ("R", i), chunk, self.right, self.sending.at[self.sends["TR", 0]]
                ).start()

            @pl.when((self.bit[i] == 1) & (self.z % (1 << i) != (1 << i) - 1))
            def _(i=i):
                self.copy(
                    ("R", i), chunk, self.right, self.landing.at[self.lands["R", i]]
                ).start()

        for j in self.high:

            @pl.when((self.bit[j] == 1) & self.has_right)
            def _(j=j):
                self.chain(("PR", j), chunk, self.products[j][part], self.has_left)

        self.start(chunk, [("PR", j) for j in self.high])

    def leftward(self, chunk):
        part = self.part(chunk)
        keys = [("L", i) for i in self.low] + [("TL", 0)] + [("PL", j) for j in self.high]
        self.wait(chunk, keys)
        for i in self.low:
            block = self.z % (2 << i)

            @pl.when(self.bit[i] == 1)
            def _(i=i, block=block):
                self.chain(("L", i), chunk, self.products[i][part], block != (2 << i) - 1)
                self.copy(("L", i), chunk, self.left).start()

            @pl.when((self.bit[i] == 0) & (block != 0))
            def _(i=i):
                self.copy(("L", i), chunk, self.left, self.landing.at[self.lands["L", i]]).start()

        @pl.when(self.has_left)
        def _():
            self.chain(("TL", 0), chunk, self.total[part], self.has_right)

        for j in self.high:

            @pl.when((self.bit[j] == 1) & self.has_left)
            def _(j=j):
                self.chain(("PL", j), chunk, self.products[j][part], self.has_right)

        self.start(chunk, [("TL", 0)] + [("PL", j) for j in self.high])

    def add(self, key, chunk, source, receives, first=None):
        @pl.when(receives)
        def _():
            base = self.sending[self.sends[first or key], self.part(chunk)].astype(F32)
            self.store(key, chunk, base + self.landed(source, chunk))

    def read(self, i, chunk, state, term):
        part = self.part(chunk)
        factor = level_scale(self.local_bits + i + 1)

        @pl.when(self.bit[i] == 1)
        def _():
            self.states[i][part] = (factor * self.landed(state, chunk)).astype(BF)

        @pl.when(self.bit[i] == 0)
        def _():
            self.states[i][part] = jnp.zeros((self.count, DH, DH), BF)
            self.sum[part] += factor * self.landed(term, chunk)

    def cross(self, chunk):
        part = self.part(chunk)
        self.sum[part] = jnp.zeros((self.count, DH, DH), F32)
        for i in self.low:
            self.read(i, chunk, ("R", i), ("L", i))
        first = self.head_bits
        value = self.total[part].astype(F32)
        for i in self.low:
            value = value + jnp.where(self.bit[i] == 1, self.landed(("R", i), chunk), 0.0)
        value = value + jnp.where(self.has_right, self.landed(("TL", 0), chunk), 0.0)
        self.store(("T", first), chunk, value)
        for j in self.high:

            @pl.when(self.bit[j] == 1)
            def _(j=j):
                value = self.products[j][part].astype(F32)
                value = value + jnp.where(self.has_left, self.landed(("PR", j), chunk), 0.0)
                value = value + jnp.where(self.has_right, self.landed(("PL", j), chunk), 0.0)
                self.store((("P", j), first), chunk, value)

        self.start(chunk, [("T", first)] + [(("P", j), first) for j in self.high])

    def arrive(self, i, chunk):
        part = self.part(chunk)
        above = range(i + 1, self.cross_bits)
        self.wait(chunk, [("T", i), (("P", i), i)] + [(("P", j), i) for j in above])
        if len(above):
            self.add(("T", i + 1), chunk, ("T", i), self.bit[i] >= 0, ("T", i))
            for j in above:
                self.add((("P", j), i + 1), chunk, (("P", j), i), self.bit[j] == 1, (("P", j), i))
            self.start(chunk, [("T", i + 1)] + [(("P", j), i + 1) for j in above])
        self.read(i, chunk, ("T", i), (("P", i), i))
        if not len(above):
            self.adjoint[part] = self.sum[part].astype(BF)

    def advance(self, time):
        def at(offset, event):
            chunk = time - offset

            @pl.when((chunk >= 0) & (chunk < self.chunks))
            def _():
                event(chunk)

        at(self.z, self.rightward)
        at(self.size - 1 - self.z, self.leftward)
        at(self.size - 1, self.cross)
        for i in self.high:
            at(self.size + 1 + 2 * (i - self.head_bits), functools.partial(self.arrive, i))

    def finish(self, steps):
        def late(time, carry):
            self.advance(time)
            return carry

        if self.last_time >= steps:
            lax.fori_loop(steps, self.last_time + 1, late, 0)

        def body(chunk, carry):
            for key, device, sends, _ in self.transfers():
                source = self.landing.at[self.lands[key]]
                pl.when(sends)(
                    lambda k=key, d=device, r=source: self.copy(k, chunk, d, r).wait_send()
                )
            return carry

        lax.fori_loop(0, self.chunks, body, 0)


def local_kernel(stretches, exchange, *refs):
    cross_bits = exchange.cross_bits
    q_ref, k_ref, v_ref, g_ref, w_ref = refs[:5]
    sources = refs[5 : 6 + cross_bits]
    outs = refs[6 + cross_bits :]
    att_ref, dq_ref, dk_ref, dv_ref, gw_ref = outs[:5]
    states_out = outs[5 : 5 + cross_bits]
    adjoint_out, wr = outs[5 + cross_bits : 7 + cross_bits]
    exchange.bind(sources, states_out, adjoint_out, outs[7 + cross_bits :])
    step = pl.program_id(0)
    head = step
    local_bits = stretches.bit_length() - 1
    width = w_ref.shape[1]

    @pl.when(step == 0)
    def _():
        gw_ref[...] = jnp.zeros_like(gw_ref)

    pl.when(step == 0)(exchange.greet)
    exchange.advance(step)
    wr[...] = head_weights(w_ref, head)

    def rows(ref, n, count=1):
        return ref[n * C : (n + count) * C, :]

    def weighted(n, level):
        return (wr[n * C : (n + 1) * C, level : level + 1] * rows(q_ref, n).astype(F32)).astype(BF)

    sums = {}
    for n in range(stretches - 1):
        sums[0, n] = tn(rows(k_ref, n), rows(v_ref, n))
    for b in range(1, local_bits):
        for m in range(stretches >> b):
            if (b - 1, 2 * m + 1) in sums:
                sums[b, m] = sums[b - 1, 2 * m] + sums[b - 1, 2 * m + 1]
    states, adjoints, wq = {}, {}, {}
    for b in range(local_bits):
        for group in range(stretches >> (b + 1)):
            states[b, group] = (level_scale(b + 1) * sums[b, 2 * group]).astype(BF)
            first = (2 * group + 1) << b
            for n in range(first, first + (1 << b)):
                wq[b, n] = weighted(n, b + 1)
            up = cat([wq[b, n] for n in range(first, first + (1 << b))], 0)
            adjoints[b, group] = level_scale(b + 1) * tn(rows(g_ref, first, 1 << b), up)

    row = lax.broadcasted_iota(jnp.int32, (C, C), 0)
    col = lax.broadcasted_iota(jnp.int32, (C, C), 1)
    mask = jnp.where(col <= row, level_scale(0), 0.0).astype(F32)
    for n in range(stretches):
        q, k, v, g = (rows(ref, n) for ref in (q_ref, k_ref, v_ref, g_ref))
        here = slice(n * C, (n + 1) * C)
        bits = [b for b in range(local_bits) if n >> b & 1]
        read = [states[b, n >> (b + 1)] for b in bits]
        scores = nt(q, k) * mask
        grads = nt(g, v)
        w0 = wr[here, 0:1]
        probs = (w0 * scores).astype(BF)
        gscores = (w0 * (grads * mask)).astype(BF)
        att = nn(cat([probs] + [wq[b, n] for b in bits], 1), cat([v] + read, 0))
        dq = nn(gscores, k)
        marks = [(scores * grads).astype(BF)]
        q32 = q.astype(F32)
        for b, state in zip(bits, read):
            back = nt(g, state)
            dq = dq + wr[here, b + 1 : b + 2] * back
            marks.append((q32 * back).astype(BF))
        picks = [pick(C, head, level, width) for level in [0] + [b + 1 for b in bits]]
        gw_ref[here, :] += nn(cat(marks, 1), cat(picks, 0))
        dk = tn(gscores, q)
        dv = tn(probs, g)
        adjoint = None
        for b in range(local_bits):
            if not n >> b & 1:
                term = adjoints[b, n >> (b + 1)]
                adjoint = term if adjoint is None else adjoint + term
        if adjoint is not None:
            adjoint = adjoint.astype(BF)
            dk = dk + nn(v, adjoint)
            dv = dv + nt(k, adjoint)
        att_ref[here, :] = att.astype(BF)
        dq_ref[here, :] = dq.astype(BF)
        dk_ref[here, :] = dk.astype(BF)
        dv_ref[here, :] = dv.astype(BF)

    @pl.when(step == pl.num_programs(0) - 1)
    def _():
        exchange.finish(exchange.heads)


def local_call(query, key, value, grad_out, weights, sums, head_bits):
    tokens = query.shape[0]
    stretches = tokens // C
    heads = query.shape[1] // DH
    cross_bits = len(sums) - 1
    exchange = Exchange(stretches.bit_length() - 1, cross_bits, head_bits, heads, heads // 2)
    column = pl.BlockSpec((tokens, DH), lambda h: (0, h))
    whole = pl.BlockSpec(weights.shape, lambda h: (0, 0))
    squares = pl.BlockSpec((heads, DH, DH), lambda h: (0, 0, 0))
    shape = jax.ShapeDtypeStruct(query.shape, BF)
    square = jax.ShapeDtypeStruct((heads, DH, DH), BF)
    return pl.pallas_call(
        functools.partial(local_kernel, stretches, exchange),
        grid=(heads,),
        in_specs=[column] * 4 + [whole] + [squares] * (cross_bits + 1),
        out_specs=[column] * 4 + [whole] + [squares] * (cross_bits + 1),
        out_shape=[shape] * 4
        + [jax.ShapeDtypeStruct(weights.shape, F32)]
        + [square] * (cross_bits + 1),
        scratch_shapes=[pltpu.VMEM(weights.shape, F32)] + exchange.scratch(),
        compiler_params=pltpu.CompilerParams(
            vmem_limit_bytes=VMEM_LIMIT, collective_id=0, has_side_effects=True
        ),
        name="local",
    )(query, key, value, grad_out, weights, *sums)


def cross_kernel(local_bits, cross_bits, chunks, *refs):
    q_ref, k_ref, v_ref, g_ref, w_ref = refs[:5]
    att_in, dq_in, dk_in, dv_in = refs[5:9]
    gw_in = refs[9 : 9 + chunks]
    states = refs[9 + chunks : 9 + chunks + cross_bits]
    adjoint = refs[9 + chunks + cross_bits]
    att_ref, dq_ref, dk_ref, dv_ref, gw_ref, acc, wr = refs[10 + chunks + cross_bits :]
    head = pl.program_id(0)
    width = w_ref.shape[1]

    @pl.when(head == 0)
    def _():
        total = gw_in[0][...]
        for other in gw_in[1:]:
            total = total + other[...]
        acc[...] = total

    wr[...] = head_weights(w_ref, head)
    read = cat([state[0] for state in states], 0)
    adj = adjoint[0]
    picks = cat([pick(DH, head, local_bits + 1 + j, width) for j in range(cross_bits)], 0)
    tokens = q_ref.shape[0]
    step = min(2 * C, tokens)
    for start in range(0, tokens, step):
        here = slice(start, start + step)
        q32 = q_ref[here, :].astype(F32)
        columns = [
            wr[here, local_bits + 1 + j : local_bits + 2 + j] for j in range(cross_bits)
        ]
        att = att_in[here, :].astype(F32) + nn(cat([(w * q32).astype(BF) for w in columns], 1), read)
        back = nt(g_ref[here, :], read)
        dq = dq_in[here, :].astype(F32)
        marks = []
        for j, w in enumerate(columns):
            part = back[:, j * DH : (j + 1) * DH]
            dq = dq + w * part
            marks.append((q32 * part).astype(BF))
        acc[here, :] += nn(cat(marks, 1), picks)
        att_ref[here, :] = att.astype(BF)
        dq_ref[here, :] = dq.astype(BF)
        dk_ref[here, :] = (dk_in[here, :].astype(F32) + nn(v_ref[here, :], adj)).astype(BF)
        dv_ref[here, :] = (dv_in[here, :].astype(F32) + nt(k_ref[here, :], adj)).astype(BF)

    @pl.when(head == pl.num_programs(0) - 1)
    def _():
        gw_ref[...] = acc[...].astype(BF)


def cross_call(query, key, value, grad_out, weights, partial, gws, states, adjoint, local_bits):
    tokens = query.shape[0]
    heads = query.shape[1] // DH
    cross_bits = len(states)
    column = pl.BlockSpec((tokens, DH), lambda h: (0, h))
    whole = pl.BlockSpec(weights.shape, lambda h: (0, 0))
    square = pl.BlockSpec((1, DH, DH), lambda h: (h, 0, 0))
    return pl.pallas_call(
        functools.partial(cross_kernel, local_bits, cross_bits, len(gws)),
        grid=(heads,),
        in_specs=[column] * 4
        + [whole]
        + [column] * 4
        + [whole] * len(gws)
        + [square] * (cross_bits + 1),
        out_specs=[column] * 4 + [whole],
        out_shape=[jax.ShapeDtypeStruct(query.shape, BF)] * 4
        + [jax.ShapeDtypeStruct(weights.shape, BF)],
        scratch_shapes=[pltpu.VMEM(weights.shape, F32), pltpu.VMEM(weights.shape, F32)],
        compiler_params=pltpu.CompilerParams(vmem_limit_bytes=VMEM_LIMIT),
        name="cross",
    )(query, key, value, grad_out, weights, *partial, *gws, *states, adjoint)


def general(query, key, value, grad_out, weights):
    tokens = query.shape[0]
    heads = query.shape[1] // DH
    local_bits = (tokens // C).bit_length() - 1
    cross_bits = LEVELS - 1 - local_bits
    head_bits = lax.axis_size("head").bit_length() - 1
    sums = sums_call(query, key, value, grad_out, weights, heads, local_bits, cross_bits)
    outs = local_call(query, key, value, grad_out, weights, sums, head_bits)
    partial, gw = outs[:4], outs[4]
    states, adjoint = outs[5 : 5 + cross_bits], outs[5 + cross_bits]
    return tuple(
        cross_call(
            query, key, value, grad_out, weights, partial, [gw], states, adjoint, local_bits
        )
    )


GRID = 4
T_RIGHT, T_NEXT, T_LEFT, A_RIGHT, A_LEFT, A_LEFT2, P_X, H_CORE, U_CORE, U_X0, U_X1 = range(11)
MESSAGES = 11


class Links:
    def __init__(self, heads, chunks, local_bits):
        self.heads, self.chunks, self.count = heads, chunks, heads // chunks
        self.factors = [level_scale(local_bits + 1 + j) for j in range(4)]
        self.stages = [
            (self.totals1, 6, 2),
            (self.totals2, 12, 2),
            (self.totals3, 26, 2),
            (self.across, 30, 2),
            (self.arrive, 34, 2),
            (self.x_exchange, 7, 2),
            (self.core_exchange, 14, 2),
            (self.adjoint1, 20, 2),
            (self.adjoint2, 26, 2),
            (self.adjoint3, 34, 2),
        ]

    def scratch(self):
        return [
            pltpu.VMEM((5, self.heads, DH, DH), BF),
            pltpu.VMEM((self.heads, DH, DH), F32),
            pltpu.VMEM((MESSAGES, self.heads, DH, DH), BF),
            pltpu.VMEM((MESSAGES, self.heads, DH, DH), BF),
            pltpu.SemaphoreType.DMA((MESSAGES,)),
            pltpu.SemaphoreType.DMA((MESSAGES, self.chunks)),
        ]

    def bind(self, states, adjoint, scratch):
        self.states, self.adjoint = states, adjoint
        self.own, self.extra, self.landing, self.sending, self.send_sem, self.recv_sem = scratch
        self.z, self.seq = lax.axis_index("head"), lax.axis_index("seq")
        self.x, self.c = self.seq // 2, self.seq % 2
        z, x, c = self.z, self.x, self.c
        right, left = {"head": z + 1}, {"head": z - 1}
        core = {"seq": x * 2 + 1 - c}
        both = (x == 0) | (c == 0)
        yes = z >= 0
        self.both = both
        self.table = {
            T_RIGHT: (right, z < 3, z > 0),
            T_NEXT: (right, z == 2, z == 3),
            T_LEFT: (left, (z > 0) & both, (z < 3) & both),
            A_RIGHT: (right, (z < 3) & both, (z > 0) & both),
            A_LEFT: (left, z > 0, z < 3),
            A_LEFT2: (left, z == 3, z == 2),
            P_X: ({"seq": c}, x == 1, x == 0),
            H_CORE: (core, (x == 0) | (c == 1), both),
            U_CORE: (core, (c == 0) & yes, c == 1),
            U_X0: ({"seq": 2}, (x == 0) & (c == 1), (x == 1) & (c == 0)),
            U_X1: ({"seq": 3}, (x == 0) & (c == 1), (x == 1) & (c == 1)),
        }

    def greet(self):
        barrier = pltpu.get_barrier_semaphore()
        other = 1 - self.x
        devices = [
            {"head": (self.z + 1) % GRID},
            {"head": (self.z + GRID - 1) % GRID},
            {"seq": self.x * 2 + 1 - self.c},
            {"seq": other * 2 + self.c},
            {"seq": other * 2 + 1 - self.c},
        ]
        for device in devices:
            pl.semaphore_signal(
                barrier, inc=1, device_id=device, device_id_type=pl.DeviceIdType.MESH
            )
        pl.semaphore_wait(barrier, len(devices))

    def part(self, chunk):
        return pl.ds(chunk * self.count, self.count)

    def copy(self, key, chunk, source, part=None):
        part = self.part(chunk) if part is None else part
        return pltpu.make_async_remote_copy(
            src_ref=source.at[part],
            dst_ref=self.landing.at[key, part],
            send_sem=self.send_sem.at[key],
            recv_sem=self.recv_sem.at[key, chunk],
            device_id=self.table[key][0],
            device_id_type=pl.DeviceIdType.MESH,
        )

    def send(self, key, chunk, source, when):
        pl.when(when)(lambda: self.copy(key, chunk, source).start())

    def emit(self, key, chunk, value):
        self.sending[key, self.part(chunk)] = value.astype(BF)
        self.copy(key, chunk, self.sending.at[key]).start()

    def wait(self, chunk, key, when=True):
        receives = self.table[key][2] & when
        pl.when(receives)(lambda: self.copy(key, chunk, self.landing.at[key]).wait_recv())

    def landed(self, key, chunk):
        return self.landing[key, self.part(chunk)].astype(F32)

    def mine(self, index, chunk):
        return self.own[index, self.part(chunk)].astype(F32)

    def first(self, chunk):
        z, x, c = self.z, self.x, self.c
        total = self.own.at[0]
        self.send(T_RIGHT, chunk, total, z == 0)
        self.send(T_NEXT, chunk, total, z == 2)
        self.send(T_LEFT, chunk, total, (z == 3) & self.both)
        self.send(P_X, chunk, self.own.at[4], x == 1)
        self.send(H_CORE, chunk, self.own.at[3], (x == 1) & (c == 1))

    def x_exchange(self, chunk):
        x, c = self.x, self.c
        self.wait(chunk, P_X)
        self.send(H_CORE, chunk, self.landing.at[P_X], (x == 0) & (c == 0))

        @pl.when((x == 0) & (c == 1))
        def _():
            self.emit(H_CORE, chunk, self.mine(3, chunk) + self.landed(P_X, chunk))

    def core_exchange(self, chunk):
        z = self.z
        part = self.part(chunk)
        self.wait(chunk, H_CORE)

        @pl.when(self.both)
        def _():
            value = self.landed(H_CORE, chunk)
            self.extra[part] = value + jnp.where(self.x == 0, self.landed(P_X, chunk), 0.0)

        @pl.when(jnp.logical_not(self.both))
        def _():
            self.extra[part] = jnp.zeros((self.count, DH, DH), F32)

        @pl.when((z == 0) & self.both)
        def _():
            self.emit(A_RIGHT, chunk, self.extra[part])

        @pl.when(z == 3)
        def _():
            self.emit(A_LEFT2, chunk, self.mine(2, chunk) + self.extra[part])

    def forward_right(self, chunk):
        part = self.part(chunk)

        @pl.when(self.both)
        def _():
            self.emit(A_RIGHT, chunk, self.extra[part] + self.landed(A_RIGHT, chunk))

    def forward_left(self, chunk):
        pl.when(self.both)(
            lambda: self.emit(T_LEFT, chunk, self.mine(0, chunk) + self.landed(T_LEFT, chunk))
        )

    def totals1(self, chunk):
        z = self.z
        self.wait(chunk, T_RIGHT, z == 1)
        self.wait(chunk, T_LEFT, z == 2)

        @pl.when(z == 1)
        def _():
            self.emit(T_RIGHT, chunk, self.mine(0, chunk) + self.landed(T_RIGHT, chunk))

        pl.when(z == 2)(lambda: self.forward_left(chunk))

    def totals2(self, chunk):
        z = self.z
        self.wait(chunk, T_RIGHT, z == 2)
        self.wait(chunk, T_LEFT, z == 1)
        self.send(T_RIGHT, chunk, self.landing.at[T_RIGHT], z == 2)
        pl.when(z == 1)(lambda: self.forward_left(chunk))

    def totals3(self, chunk):
        z, c = self.z, self.c
        part = self.part(chunk)
        self.wait(chunk, T_RIGHT, z == 3)
        self.wait(chunk, T_NEXT)
        self.wait(chunk, T_LEFT, z == 0)

        @pl.when(self.both)
        def _():
            value = self.mine(0, chunk)
            value = value + jnp.where(z > 0, self.landed(T_RIGHT, chunk), 0.0)
            value = value + jnp.where(z == 3, self.landed(T_NEXT, chunk), 0.0)
            value = value + jnp.where(z < 3, self.landed(T_LEFT, chunk), 0.0)
            self.sending[U_CORE, part] = value.astype(BF)

        self.send(U_CORE, chunk, self.sending.at[U_CORE], c == 0)

        def read(level, state):
            self.states[part, level * DH : (level + 1) * DH] = state.astype(BF)

        near = jnp.where(z == 1, self.landed(T_RIGHT, chunk), self.landed(T_NEXT, chunk))
        read(0, jnp.where(z % 2 == 1, self.factors[0] * near, 0.0))
        read(1, jnp.where(z >= 2, self.factors[1] * self.landed(T_RIGHT, chunk), 0.0))

    def adjoint1(self, chunk):
        z = self.z
        part = self.part(chunk)
        self.wait(chunk, A_RIGHT, z == 1)
        self.wait(chunk, A_LEFT2)

        @pl.when(z == 3)
        def _():
            self.emit(A_LEFT, chunk, self.mine(1, chunk) + self.extra[part])

        pl.when(z == 1)(lambda: self.forward_right(chunk))

        @pl.when(z == 2)
        def _():
            value = self.mine(2, chunk) + self.extra[part] + self.landed(A_LEFT2, chunk)
            self.emit(A_LEFT, chunk, value)

    def adjoint2(self, chunk):
        z = self.z
        part = self.part(chunk)
        self.wait(chunk, A_RIGHT, z == 2)
        self.wait(chunk, A_LEFT, z == 1)
        pl.when(z == 2)(lambda: self.forward_right(chunk))

        @pl.when(z == 1)
        def _():
            value = self.mine(1, chunk) + self.extra[part] + self.landed(A_LEFT, chunk)
            self.emit(A_LEFT, chunk, value)

    def adjoint3(self, chunk):
        z = self.z
        part = self.part(chunk)
        self.wait(chunk, A_RIGHT, z == 3)
        self.wait(chunk, A_LEFT, z % 2 == 0)
        value = self.extra[part]
        value = value + jnp.where((z > 0) & self.both, self.landed(A_RIGHT, chunk), 0.0)
        value = value + jnp.where(z < 3, self.landed(A_LEFT, chunk), 0.0)
        self.adjoint[part] = value.astype(BF)

    def across(self, chunk):
        part = self.part(chunk)
        self.wait(chunk, U_CORE)
        state = jnp.where(self.c == 1, self.factors[2] * self.landed(U_CORE, chunk), 0.0)
        self.states[part, 2 * DH : 3 * DH] = state.astype(BF)

        @pl.when((self.x == 0) & (self.c == 1))
        def _():
            value = self.sending[U_CORE, part].astype(F32) + self.landed(U_CORE, chunk)
            self.sending[U_X0, part] = value.astype(BF)
            self.copy(U_X0, chunk, self.sending.at[U_X0]).start()
            self.copy(U_X1, chunk, self.sending.at[U_X0]).start()

    def arrive(self, chunk):
        part = self.part(chunk)
        self.wait(chunk, U_X0)
        self.wait(chunk, U_X1)
        state = jnp.where(self.c == 0, self.landed(U_X0, chunk), self.landed(U_X1, chunk))
        state = jnp.where(self.x == 1, self.factors[3] * state, 0.0)
        self.states[part, 3 * DH : 4 * DH] = state.astype(BF)

    def advance(self, time):
        for stage, begin, pace in self.stages:
            late = time - begin
            chunk = jnp.right_shift(late * (8192 // pace + 1), 13)
            last = (self.chunks - 1) * pace

            @pl.when((late >= 0) & (late <= last) & (chunk * pace == late))
            def _(stage=stage, chunk=chunk):
                stage(chunk)

    def last(self):
        return max(begin + (self.chunks - 1) * pace for _, begin, pace in self.stages)

    def drain(self):
        whole = pl.ds(0, self.heads)
        for key, (_, sends, _) in self.table.items():
            pl.when(sends)(
                lambda k=key: self.copy(k, 0, self.landing.at[k], whole).wait_send()
            )


def rows_of_weights(w_ref, wt_ref):
    for start in range(0, w_ref.shape[0], C):
        here = slice(start, start + C)
        wt_ref[:, here] = w_ref[here, :].astype(F32).T


def level_rows(wt_ref, head):
    return wt_ref[pl.ds(pl.multiple_of(head * LEVELS, LEVELS), LEVELS), :]


def stage_kernel(stretches, heads, links, *refs):
    inputs, w_ref = refs[:4], refs[4]
    kept, outs, states_out, adjoint_out = refs[5:9], refs[9:14], refs[14], refs[15]
    natural, turned = refs[16:20], refs[20:24]
    wt, wq, load_sem, keep_sem = refs[24:28]
    links.bind(states_out, adjoint_out, refs[28:])
    keeps = [
        pltpu.make_async_copy(source, target, keep_sem.at[i])
        for i, (source, target) in enumerate(
            zip((turned[0], turned[3], natural[1], natural[2]), kept)
        )
    ]
    step = pl.program_id(0)
    head = lax.rem(step, heads)

    def load(i, h):
        return pltpu.make_async_copy(
            inputs[i].at[:, pl.ds(pl.multiple_of(h * DH, DH), DH)],
            natural[i].at[h],
            load_sem.at[i, h],
        )

    @pl.when(step == 0)
    def _():
        def start(h, carry):
            for i in range(4):
                load(i, h).start()
            return carry

        lax.fori_loop(0, heads, start, 0)
        rows_of_weights(w_ref, wt)
        links.greet()

    weight = level_rows(wt, head)
    here = [ref.at[head] for ref in natural], [ref.at[head] for ref in turned]

    @pl.when(step < heads)
    def _():
        links.advance(step)
        for i in range(4):
            load(i, head).wait()
        sums_part(stretches, head, weight, *here, wq, links)

        @pl.when(head % links.count == links.count - 1)
        def _():
            links.first(head // links.count)

    @pl.when(step >= heads)
    def _():
        @pl.when(step == heads)
        def _():
            for keep in keeps:
                keep.start()

        slot = 2 * step - heads
        links.advance(slot)
        local_part(stretches, weight, *here, outs, lambda: links.advance(slot + 1))

    @pl.when(step == pl.num_programs(0) - 1)
    def _():
        def late(time, carry):
            links.advance(time)
            return carry

        for keep in keeps:
            keep.wait()
        lax.fori_loop(3 * heads, max(3 * heads, links.last() + 1), late, 0)
        links.drain()


def sums_part(stretches, head, weight, natural, turned, wq, links):
    local_bits = stretches.bit_length() - 1
    spans = [slice(start, start + 2 * C) for start in range(0, stretches * C, 2 * C)]
    for here in spans:
        flat = natural[0][here, :].T
        turned[0][:, here] = flat
        for j in range(4):
            row = weight[local_bits + 1 + j : local_bits + 2 + j, here]
            wq[j * DH : (j + 1) * DH, here] = (row * flat.astype(F32)).astype(BF)
        turned[3][:, here] = natural[3][here, :].T
    out = nt(turned[3][...], wq[...])
    for here in spans:
        turned[1][:, here] = natural[1][here, :].T
    links.own[0, head] = nn(turned[1][...], natural[2][...]).astype(BF)
    for j in range(4):
        links.own[1 + j, head] = (links.factors[j] * out[:, j * DH : (j + 1) * DH]).astype(BF)


def local_part(stretches, weight, natural, turned, outs, between):
    q_ref, k_ref, v_ref, g_ref = natural
    qt_ref, kt_ref, vt_ref, gt_ref = turned
    att_ref, dq_ref, dk_ref, dv_ref, gw_ref = outs
    local_bits = stretches.bit_length() - 1

    def here(n, count=1):
        return slice(n * C, (n + count) * C)

    def levels(n):
        return [b for b in range(local_bits) if n >> b & 1]

    sums = {}
    for n in range(stretches - 1):
        sums[0, n] = nn(kt_ref[:, here(n)], v_ref[here(n), :])
    for b in range(1, local_bits):
        for m in range(stretches >> b):
            if (b - 1, 2 * m + 1) in sums:
                sums[b, m] = sums[b - 1, 2 * m] + sums[b - 1, 2 * m + 1]
    states, flipped, adjoints, wq = {}, {}, {}, {}
    for b in range(local_bits):
        for group in range(stretches >> (b + 1)):
            state = (level_scale(b + 1) * sums[b, 2 * group]).astype(BF)
            states[b, group], flipped[b, group] = state, state.T
            first, count = (2 * group + 1) << b, 1 << b
            for n in range(first, first + count):
                row = weight[b + 1 : b + 2, here(n)]
                wq[b, n] = (row * qt_ref[:, here(n)].astype(F32)).astype(BF)
            across = cat([wq[b, n] for n in range(first, first + count)], 1)
            adjoints[b, group] = level_scale(b + 1) * nn(across, g_ref[here(first, count), :])

    row = lax.broadcasted_iota(jnp.int32, (C, C), 0)
    col = lax.broadcasted_iota(jnp.int32, (C, C), 1)
    mask = jnp.where(row <= col, level_scale(0), 0.0).astype(F32)
    ready = {}
    for n in range(stretches):
        bits = levels(n)
        scores = nn(k_ref[here(n), :], qt_ref[:, here(n)]) * mask
        vt_ref[:, here(n)] = v_ref[here(n), :].T
        rows = cat([v_ref[here(n), :]] + [states[b, n >> (b + 1)] for b in bits], 0)
        seen = nn(rows, gt_ref[:, here(n)])
        grads = seen[:C]
        w0 = weight[0:1, here(n)]
        gws = {0: jnp.sum(scores * grads, axis=0, keepdims=True)}
        extra = 0.0
        for i, b in enumerate(bits):
            back = seen[C + i * DH : C + (i + 1) * DH]
            extra = extra + weight[b + 1 : b + 2, here(n)] * back
            qt32 = qt_ref[:, here(n)].astype(F32)
            gws[b + 1] = jnp.sum(qt32 * back, axis=0, keepdims=True)
        zero = jnp.zeros((1, C), F32)
        gw_ref[0, :, here(n)] = jnp.concatenate([gws.get(l, zero) for l in range(LEVELS)], 0)
        ready[n] = (scores * w0).astype(BF), (grads * mask * w0).astype(BF), extra
    between()
    for n in range(stretches):
        bits = levels(n)
        q, k, v, g = (ref[here(n), :] for ref in natural)
        probs, gscores, extra = ready[n]
        left = [vt_ref[:, here(n)]] + [flipped[b, n >> (b + 1)] for b in bits]
        att = nn(cat(left, 1), cat([probs] + [wq[b, n] for b in bits], 0))
        dq = nn(kt_ref[:, here(n)], gscores) + extra
        terms = [adjoints[b, n >> (b + 1)] for b in range(local_bits) if b not in bits]
        if terms:
            adjoint = sum(terms[1:], terms[0]).astype(BF)
            dk = nn(cat([gscores, v], 1), cat([q, adjoint.T], 0))
            dv = nn(cat([probs, k], 1), cat([g, adjoint], 0))
        else:
            dk, dv = nn(gscores, q), nn(probs, g)
        att_ref[0, :, here(n)] = att.astype(BF)
        dq_ref[0, :, here(n)] = dq.astype(BF)
        dk_ref[0, here(n), :] = dk.astype(BF)
        dv_ref[0, here(n), :] = dv.astype(BF)


def stage_call(query, key, value, grad_out, weights):
    tokens = query.shape[0]
    stretches, heads = tokens // C, query.shape[1] // DH
    links = Links(heads, heads // 2, stretches.bit_length() - 1)

    def block(*shape):
        return pl.BlockSpec((1,) + shape, lambda s: (jnp.maximum(s - heads, 0), 0, 0))

    shapes = [(DH, tokens)] * 2 + [(tokens, DH)] * 2 + [(LEVELS, tokens)]
    types = [BF] * 4 + [F32]
    small = [(heads, 4 * DH, DH), (heads, DH, DH)]
    large = [(heads,) + shape for shape in shapes[:4]]
    return pl.pallas_call(
        functools.partial(stage_kernel, stretches, heads, links),
        grid=(2 * heads,),
        in_specs=[pl.BlockSpec(memory_space=pl.ANY)] * 4
        + [pl.BlockSpec(weights.shape, lambda s: (0, 0))],
        out_specs=[pl.BlockSpec(memory_space=pl.ANY)] * 4
        + [block(*shape) for shape in shapes]
        + [pl.BlockSpec(shape, lambda s: (0, 0, 0)) for shape in small],
        out_shape=[jax.ShapeDtypeStruct(shape, BF) for shape in large]
        + [jax.ShapeDtypeStruct((heads,) + shape, kind) for shape, kind in zip(shapes, types)]
        + [jax.ShapeDtypeStruct(shape, BF) for shape in small],
        scratch_shapes=[pltpu.VMEM((heads, tokens, DH), BF)] * 4
        + [pltpu.VMEM((heads, DH, tokens), BF)] * 4
        + [
            pltpu.VMEM(weights.shape[::-1], F32),
            pltpu.VMEM((4 * DH, tokens), BF),
            pltpu.SemaphoreType.DMA((4, heads)),
            pltpu.SemaphoreType.DMA((4,)),
        ]
        + links.scratch(),
        compiler_params=pltpu.CompilerParams(
            vmem_limit_bytes=VMEM_LIMIT, collective_id=1, has_side_effects=True
        ),
        name="stage",
    )(query, key, value, grad_out, weights)


def merge_kernel(pair, local_bits, *refs):
    near, gw_in, states_ref, adjoint_ref, w_ref = refs[:8], *refs[8:12]
    outs, gw_ref, wt, gwt = refs[12:16], *refs[16:]
    step = pl.program_id(0)

    @pl.when(step == 0)
    def _():
        rows_of_weights(w_ref, wt)

    for i in range(pair):
        head = step * pair + i
        rows = pl.ds(pl.multiple_of(head * LEVELS, LEVELS), LEVELS)
        merge_part(
            local_bits, level_rows(wt, head), [ref.at[i] for ref in near], gw_in[i],
            states_ref[i], adjoint_ref[i], outs, slice(i * DH, (i + 1) * DH), gwt.at[rows],
        )

    @pl.when(step == pl.num_programs(0) - 1)
    def _():
        for start in range(0, w_ref.shape[0], C):
            here = slice(start, start + C)
            gw_ref[here, :] = gwt[:, here].T.astype(BF)


def merge_part(local_bits, weight, near, gw_in, states, adjoint, outs, lanes, gwt):
    qt_ref, gt_ref, k_ref, v_ref, att_in, dq_in, dk_in, dv_in = near
    att_ref, dq_ref, dk_ref, dv_ref = outs
    flipped = cat([states[j * DH : (j + 1) * DH, :].T for j in range(4)], 1)
    back_adjoint = adjoint.T
    for start in range(0, k_ref.shape[0], 2 * C):
        here = slice(start, start + 2 * C)
        qt32 = qt_ref[:, here].astype(F32)
        levels = [weight[local_bits + 1 + j : local_bits + 2 + j, here] for j in range(4)]
        wq = cat([(row * qt32).astype(BF) for row in levels], 0)
        att = att_in[:, here].astype(F32) + nn(flipped, wq)
        back = nn(states, gt_ref[:, here])
        dq = dq_in[:, here].astype(F32)
        gws = [gw_in[0 : local_bits + 1, here]]
        for j, row in enumerate(levels):
            part = back[j * DH : (j + 1) * DH, :]
            dq = dq + row * part
            gws.append(jnp.sum(qt32 * part, axis=0, keepdims=True))
        gwt[:, here] = jnp.concatenate(gws, 0)
        att_ref[here, lanes] = att.astype(BF).T
        dq_ref[here, lanes] = dq.astype(BF).T
        dk = dk_in[here, :].astype(F32) + nn(v_ref[here, :], adjoint)
        dv = dv_in[here, :].astype(F32) + nn(k_ref[here, :], back_adjoint)
        dk_ref[here, lanes] = dk.astype(BF)
        dv_ref[here, lanes] = dv.astype(BF)


def merge_call(weights, outs, local_bits):
    heads, tokens = outs[0].shape[0], weights.shape[0]
    pair = 2
    column = pl.BlockSpec((tokens, pair * DH), lambda s: (0, s))
    whole = pl.BlockSpec(weights.shape, lambda s: (0, 0))

    def block(array):
        return pl.BlockSpec((pair,) + array.shape[1:], lambda s: (s, 0, 0))

    return pl.pallas_call(
        functools.partial(merge_kernel, pair, local_bits),
        grid=(heads // pair,),
        in_specs=[block(array) for array in outs] + [whole],
        out_specs=[column] * 4 + [whole],
        out_shape=[jax.ShapeDtypeStruct((tokens, heads * DH), BF)] * 4
        + [jax.ShapeDtypeStruct(weights.shape, BF)],
        scratch_shapes=[pltpu.VMEM(weights.shape[::-1], F32)] * 2,
        compiler_params=pltpu.CompilerParams(vmem_limit_bytes=VMEM_LIMIT),
        name="merge",
    )(*outs, weights)


def shards(query, key, value, grad_out, weights):
    local_bits = (query.shape[0] // C).bit_length() - 1
    square = lax.axis_size("head") == GRID and lax.axis_size("seq") == GRID
    if not square or local_bits != LEVELS - 5:
        return general(query, key, value, grad_out, weights)
    outs = stage_call(query, key, value, grad_out, weights)
    return tuple(merge_call(weights, outs, local_bits))


def solution(mesh):
    spec = P(("rep", "seq", "head"), None)
    return jax.shard_map(
        shards, mesh=mesh, in_specs=(spec,) * 5, out_specs=(spec,) * 5, check_vma=False
    )
```

```python
import functools
import math

import jax
import jax.numpy as jnp
from jax import lax
from jax.experimental import pallas as pl
from jax.experimental.pallas import tpu as pltpu
from jax.sharding import PartitionSpec as P

DH = 128
C = 128
LEVELS = 8
VMEM_LIMIT = 60 * 2**20
BF = jnp.bfloat16
F32 = jnp.float32


def level_scale(level):
    if level == 0:
        return 1.0 / math.sqrt(DH * C)
    return 1.0 / math.sqrt(DH * C * 2 ** (level - 1))


def nn(a, b):
    return lax.dot_general(a, b, (((1,), (0,)), ((), ())), preferred_element_type=F32)


def nt(a, b):
    return lax.dot_general(a, b, (((1,), (1,)), ((), ())), preferred_element_type=F32)


def tn(a, b):
    return lax.dot_general(a, b, (((0,), (0,)), ((), ())), preferred_element_type=F32)


def cat(parts, axis):
    return parts[0] if len(parts) == 1 else jnp.concatenate(parts, axis=axis)


def head_weights(w_ref, head):
    width = w_ref.shape[1]
    return pltpu.roll(w_ref[...].astype(F32), lax.rem(width - head * LEVELS, width), 1)


def pick(rows, head, level, width):
    lane = lax.broadcasted_iota(jnp.int32, (rows, width), 1)
    return jnp.where(lane == head * LEVELS + level, 1.0, 0.0).astype(BF)


def sums_kernel(local_bits, q_ref, k_ref, v_ref, g_ref, w_ref, t_ref, *rest):
    p_refs, wr = rest[:-1], rest[-1]
    head = pl.program_id(0)
    wr[...] = head_weights(w_ref, head)
    t_ref[0] = tn(k_ref[...], v_ref[...]).astype(BF)
    q = q_ref[...].astype(F32)
    weighted = [
        (wr[:, local_bits + 1 + j : local_bits + 2 + j] * q).astype(BF) for j in range(len(p_refs))
    ]
    out = tn(g_ref[...], cat(weighted, 1))
    for j, p_ref in enumerate(p_refs):
        p_ref[0] = out[:, j * DH : (j + 1) * DH].astype(BF)


def sums_call(query, key, value, grad_out, weights, heads, local_bits, cross_bits):
    tokens = query.shape[0]
    column = pl.BlockSpec((tokens, DH), lambda h: (0, h))
    square = pl.BlockSpec((1, DH, DH), lambda h: (h, 0, 0))
    outs = [jax.ShapeDtypeStruct((heads, DH, DH), BF)] * (1 + cross_bits)
    return pl.pallas_call(
        functools.partial(sums_kernel, local_bits),
        grid=(heads,),
        in_specs=[column] * 4 + [pl.BlockSpec(weights.shape, lambda h: (0, 0))],
        out_specs=[square] * (1 + cross_bits),
        out_shape=outs,
        scratch_shapes=[pltpu.VMEM(weights.shape, F32)],
        compiler_params=pltpu.CompilerParams(vmem_limit_bytes=VMEM_LIMIT),
        name="sums",
    )(query, key, value, grad_out, weights)


class Exchange:
    def __init__(self, local_bits, cross_bits, head_bits, heads, chunks):
        self.local_bits, self.cross_bits, self.head_bits = local_bits, cross_bits, head_bits
        self.chunks, self.count, self.heads = chunks, heads // chunks, heads
        self.size = 1 << head_bits
        low, high = range(head_bits), range(head_bits, cross_bits)
        self.low, self.high = low, high
        landing = [("R", i) for i in low] + [("PR", j) for j in high]
        landing += [("L", i) for i in low] + [("TL", 0)] + [("PL", j) for j in high]
        landing += [("T", i) for i in high] + [(("P", j), i) for j in high for i in high if i <= j]
        sending = [("TR", 0)] + [("PR", j) for j in high]
        sending += [("L", i) for i in low] + [("TL", 0)] + [("PL", j) for j in high]
        sending += [("T", i) for i in high] + [(("P", j), i) for j in high for i in high if i <= j]
        self.lands = {key: n for n, key in enumerate(landing)}
        self.sends = {key: n for n, key in enumerate(sending)}
        self.last_time = chunks - 1 + self.size + 1 + 2 * (len(high) - 1)

    def scratch(self):
        sems = pltpu.SemaphoreType.DMA((len(self.lands), self.chunks))
        return [
            pltpu.VMEM((len(self.lands), self.heads, DH, DH), BF),
            pltpu.VMEM((len(self.sends), self.heads, DH, DH), BF),
            pltpu.VMEM((self.heads, DH, DH), F32),
            sems,
            sems,
        ]

    def bind(self, sources, states, adjoint, scratch):
        self.total, self.products = sources[0], sources[1:]
        self.states, self.adjoint = states, adjoint
        self.landing, self.sending, self.sum, self.send_sem, self.recv_sem = scratch
        self.z, seq = lax.axis_index("head"), lax.axis_index("seq")
        self.bit = []
        for i in range(self.cross_bits):
            position, stride = self.z, 1 << i
            if i >= self.head_bits:
                position, stride = seq, 1 << (i - self.head_bits)
            self.bit.append((position // stride) % 2)
        self.partner = {
            i: {"seq": seq + (1 - 2 * self.bit[i]) * (1 << (i - self.head_bits))}
            for i in self.high
        }
        self.right, self.left = {"head": self.z + 1}, {"head": self.z - 1}
        self.has_right, self.has_left = self.z < self.size - 1, self.z > 0

    def part(self, chunk):
        return pl.ds(chunk * self.count, self.count)

    def landed(self, key, chunk):
        return self.landing[self.lands[key], self.part(chunk)].astype(F32)

    def store(self, key, chunk, value):
        self.sending[self.sends[key], self.part(chunk)] = value.astype(BF)

    def copy(self, key, chunk, device, source=None):
        slot = self.lands[key]
        if source is None:
            source = self.sending.at[self.sends[key]]
        return pltpu.make_async_remote_copy(
            src_ref=source.at[self.part(chunk)],
            dst_ref=self.landing.at[slot, self.part(chunk)],
            send_sem=self.send_sem.at[slot, chunk],
            recv_sem=self.recv_sem.at[slot, chunk],
            device_id=device,
            device_id_type=pl.DeviceIdType.MESH,
        )

    def transfers(self):
        for i in self.low:
            yield ("R", i), self.right, self.has_right & (((self.z + 1) >> i) % 2 == 1), self.bit[i] == 1
        for j in self.high:
            own = self.bit[j] == 1
            yield ("PR", j), self.right, self.has_right & own, self.has_left & own
        for i in self.low:
            block = self.z % (2 << i)
            yield ("L", i), self.left, block != 0, block != (2 << i) - 1
        yield ("TL", 0), self.left, self.has_left, self.has_right
        for j in self.high:
            own = self.bit[j] == 1
            yield ("PL", j), self.left, self.has_left & own, self.has_right & own
        for i in self.high:
            up, down, always = self.bit[i] == 1, self.bit[i] == 0, self.bit[i] >= 0
            last = i == self.cross_bits - 1
            yield ("T", i), self.partner[i], (down if last else always), (up if last else always)
            yield (("P", i), i), self.partner[i], up, down
            for j in range(i + 1, self.cross_bits):
                own = self.bit[j] == 1
                yield (("P", j), i), self.partner[i], own, own

    def greet(self):
        barrier = pltpu.get_barrier_semaphore()

        def signal(device):
            pl.semaphore_signal(
                barrier, inc=1, device_id=device, device_id_type=pl.DeviceIdType.MESH
            )

        for i in self.high:
            signal(self.partner[i])
        signal({"head": lax.rem(self.z + 1, self.size)})
        signal({"head": lax.rem(self.z + self.size - 1, self.size)})
        pl.semaphore_wait(barrier, len(self.high) + 2)

    def wait(self, chunk, kinds):
        for key, device, _, receives in self.transfers():
            if key in kinds:
                own = self.landing.at[self.lands[key]]
                pl.when(receives)(
                    lambda k=key, d=device, r=own: self.copy(k, chunk, d, r).wait_recv()
                )

    def start(self, chunk, kinds):
        for key, device, sends, _ in self.transfers():
            if key in kinds:
                pl.when(sends)(lambda k=key, d=device: self.copy(k, chunk, d).start())

    def chain(self, key, chunk, own, receives):
        @pl.when(receives)
        def _():
            self.store(key, chunk, own.astype(F32) + self.landed(key, chunk))

        @pl.when(jnp.logical_not(receives))
        def _():
            self.store(key, chunk, own)

    def rightward(self, chunk):
        part = self.part(chunk)
        self.wait(chunk, [("R", i) for i in self.low] + [("PR", j) for j in self.high])
        for i in self.low:
            @pl.when(self.z % (2 << i) == (1 << i) - 1)
            def _(i=i):
                value = self.total[part].astype(F32)
                for k in range(i):
                    value = value + self.landed(("R", k), chunk)
                self.store(("TR", 0), chunk, value)
                self.copy(
                    ("R", i), chunk, self.right, self.sending.at[self.sends["TR", 0]]
                ).start()

            @pl.when((self.bit[i] == 1) & (self.z % (1 << i) != (1 << i) - 1))
            def _(i=i):
                self.copy(
                    ("R", i), chunk, self.right, self.landing.at[self.lands["R", i]]
                ).start()

        for j in self.high:

            @pl.when((self.bit[j] == 1) & self.has_right)
            def _(j=j):
                self.chain(("PR", j), chunk, self.products[j][part], self.has_left)

        self.start(chunk, [("PR", j) for j in self.high])

    def leftward(self, chunk):
        part = self.part(chunk)
        keys = [("L", i) for i in self.low] + [("TL", 0)] + [("PL", j) for j in self.high]
        self.wait(chunk, keys)
        for i in self.low:
            block = self.z % (2 << i)

            @pl.when(self.bit[i] == 1)
            def _(i=i, block=block):
                self.chain(("L", i), chunk, self.products[i][part], block != (2 << i) - 1)
                self.copy(("L", i), chunk, self.left).start()

            @pl.when((self.bit[i] == 0) & (block != 0))
            def _(i=i):
                self.copy(("L", i), chunk, self.left, self.landing.at[self.lands["L", i]]).start()

        @pl.when(self.has_left)
        def _():
            self.chain(("TL", 0), chunk, self.total[part], self.has_right)

        for j in self.high:

            @pl.when((self.bit[j] == 1) & self.has_left)
            def _(j=j):
                self.chain(("PL", j), chunk, self.products[j][part], self.has_right)

        self.start(chunk, [("TL", 0)] + [("PL", j) for j in self.high])

    def add(self, key, chunk, source, receives, first=None):
        @pl.when(receives)
        def _():
            base = self.sending[self.sends[first or key], self.part(chunk)].astype(F32)
            self.store(key, chunk, base + self.landed(source, chunk))

    def read(self, i, chunk, state, term):
        part = self.part(chunk)
        factor = level_scale(self.local_bits + i + 1)

        @pl.when(self.bit[i] == 1)
        def _():
            self.states[i][part] = (factor * self.landed(state, chunk)).astype(BF)

        @pl.when(self.bit[i] == 0)
        def _():
            self.states[i][part] = jnp.zeros((self.count, DH, DH), BF)
            self.sum[part] += factor * self.landed(term, chunk)

    def cross(self, chunk):
        part = self.part(chunk)
        self.sum[part] = jnp.zeros((self.count, DH, DH), F32)
        for i in self.low:
            self.read(i, chunk, ("R", i), ("L", i))
        first = self.head_bits
        value = self.total[part].astype(F32)
        for i in self.low:
            value = value + jnp.where(self.bit[i] == 1, self.landed(("R", i), chunk), 0.0)
        value = value + jnp.where(self.has_right, self.landed(("TL", 0), chunk), 0.0)
        self.store(("T", first), chunk, value)
        for j in self.high:

            @pl.when(self.bit[j] == 1)
            def _(j=j):
                value = self.products[j][part].astype(F32)
                value = value + jnp.where(self.has_left, self.landed(("PR", j), chunk), 0.0)
                value = value + jnp.where(self.has_right, self.landed(("PL", j), chunk), 0.0)
                self.store((("P", j), first), chunk, value)

        self.start(chunk, [("T", first)] + [(("P", j), first) for j in self.high])

    def arrive(self, i, chunk):
        part = self.part(chunk)
        above = range(i + 1, self.cross_bits)
        self.wait(chunk, [("T", i), (("P", i), i)] + [(("P", j), i) for j in above])
        if len(above):
            self.add(("T", i + 1), chunk, ("T", i), self.bit[i] >= 0, ("T", i))
            for j in above:
                self.add((("P", j), i + 1), chunk, (("P", j), i), self.bit[j] == 1, (("P", j), i))
            self.start(chunk, [("T", i + 1)] + [(("P", j), i + 1) for j in above])
        self.read(i, chunk, ("T", i), (("P", i), i))
        if not len(above):
            self.adjoint[part] = self.sum[part].astype(BF)

    def advance(self, time):
        def at(offset, event):
            chunk = time - offset

            @pl.when((chunk >= 0) & (chunk < self.chunks))
            def _():
                event(chunk)

        at(self.z, self.rightward)
        at(self.size - 1 - self.z, self.leftward)
        at(self.size - 1, self.cross)
        for i in self.high:
            at(self.size + 1 + 2 * (i - self.head_bits), functools.partial(self.arrive, i))

    def finish(self, steps):
        def late(time, carry):
            self.advance(time)
            return carry

        if self.last_time >= steps:
            lax.fori_loop(steps, self.last_time + 1, late, 0)

        def body(chunk, carry):
            for key, device, sends, _ in self.transfers():
                source = self.landing.at[self.lands[key]]
                pl.when(sends)(
                    lambda k=key, d=device, r=source: self.copy(k, chunk, d, r).wait_send()
                )
            return carry

        lax.fori_loop(0, self.chunks, body, 0)


def local_kernel(stretches, exchange, *refs):
    cross_bits = exchange.cross_bits
    q_ref, k_ref, v_ref, g_ref, w_ref = refs[:5]
    sources = refs[5 : 6 + cross_bits]
    outs = refs[6 + cross_bits :]
    att_ref, dq_ref, dk_ref, dv_ref, gw_ref = outs[:5]
    states_out = outs[5 : 5 + cross_bits]
    adjoint_out, wr = outs[5 + cross_bits : 7 + cross_bits]
    exchange.bind(sources, states_out, adjoint_out, outs[7 + cross_bits :])
    step = pl.program_id(0)
    head = step
    local_bits = stretches.bit_length() - 1
    width = w_ref.shape[1]

    @pl.when(step == 0)
    def _():
        gw_ref[...] = jnp.zeros_like(gw_ref)

    pl.when(step == 0)(exchange.greet)
    exchange.advance(step)
    wr[...] = head_weights(w_ref, head)

    def rows(ref, n, count=1):
        return ref[n * C : (n + count) * C, :]

    def weighted(n, level):
        return (wr[n * C : (n + 1) * C, level : level + 1] * rows(q_ref, n).astype(F32)).astype(BF)

    sums = {}
    for n in range(stretches - 1):
        sums[0, n] = tn(rows(k_ref, n), rows(v_ref, n))
    for b in range(1, local_bits):
        for m in range(stretches >> b):
            if (b - 1, 2 * m + 1) in sums:
                sums[b, m] = sums[b - 1, 2 * m] + sums[b - 1, 2 * m + 1]
    states, adjoints, wq = {}, {}, {}
    for b in range(local_bits):
        for group in range(stretches >> (b + 1)):
            states[b, group] = (level_scale(b + 1) * sums[b, 2 * group]).astype(BF)
            first = (2 * group + 1) << b
            for n in range(first, first + (1 << b)):
                wq[b, n] = weighted(n, b + 1)
            up = cat([wq[b, n] for n in range(first, first + (1 << b))], 0)
            adjoints[b, group] = level_scale(b + 1) * tn(rows(g_ref, first, 1 << b), up)

    row = lax.broadcasted_iota(jnp.int32, (C, C), 0)
    col = lax.broadcasted_iota(jnp.int32, (C, C), 1)
    mask = jnp.where(col <= row, level_scale(0), 0.0).astype(F32)
    for n in range(stretches):
        q, k, v, g = (rows(ref, n) for ref in (q_ref, k_ref, v_ref, g_ref))
        here = slice(n * C, (n + 1) * C)
        bits = [b for b in range(local_bits) if n >> b & 1]
        read = [states[b, n >> (b + 1)] for b in bits]
        scores = nt(q, k) * mask
        grads = nt(g, v)
        w0 = wr[here, 0:1]
        probs = (w0 * scores).astype(BF)
        gscores = (w0 * (grads * mask)).astype(BF)
        att = nn(cat([probs] + [wq[b, n] for b in bits], 1), cat([v] + read, 0))
        dq = nn(gscores, k)
        marks = [(scores * grads).astype(BF)]
        q32 = q.astype(F32)
        for b, state in zip(bits, read):
            back = nt(g, state)
            dq = dq + wr[here, b + 1 : b + 2] * back
            marks.append((q32 * back).astype(BF))
        picks = [pick(C, head, level, width) for level in [0] + [b + 1 for b in bits]]
        gw_ref[here, :] += nn(cat(marks, 1), cat(picks, 0))
        dk = tn(gscores, q)
        dv = tn(probs, g)
        adjoint = None
        for b in range(local_bits):
            if not n >> b & 1:
                term = adjoints[b, n >> (b + 1)]
                adjoint = term if adjoint is None else adjoint + term
        if adjoint is not None:
            adjoint = adjoint.astype(BF)
            dk = dk + nn(v, adjoint)
            dv = dv + nt(k, adjoint)
        att_ref[here, :] = att.astype(BF)
        dq_ref[here, :] = dq.astype(BF)
        dk_ref[here, :] = dk.astype(BF)
        dv_ref[here, :] = dv.astype(BF)

    @pl.when(step == pl.num_programs(0) - 1)
    def _():
        exchange.finish(exchange.heads)


def local_call(query, key, value, grad_out, weights, sums, head_bits):
    tokens = query.shape[0]
    stretches = tokens // C
    heads = query.shape[1] // DH
    cross_bits = len(sums) - 1
    exchange = Exchange(stretches.bit_length() - 1, cross_bits, head_bits, heads, heads // 2)
    column = pl.BlockSpec((tokens, DH), lambda h: (0, h))
    whole = pl.BlockSpec(weights.shape, lambda h: (0, 0))
    squares = pl.BlockSpec((heads, DH, DH), lambda h: (0, 0, 0))
    shape = jax.ShapeDtypeStruct(query.shape, BF)
    square = jax.ShapeDtypeStruct((heads, DH, DH), BF)
    return pl.pallas_call(
        functools.partial(local_kernel, stretches, exchange),
        grid=(heads,),
        in_specs=[column] * 4 + [whole] + [squares] * (cross_bits + 1),
        out_specs=[column] * 4 + [whole] + [squares] * (cross_bits + 1),
        out_shape=[shape] * 4
        + [jax.ShapeDtypeStruct(weights.shape, F32)]
        + [square] * (cross_bits + 1),
        scratch_shapes=[pltpu.VMEM(weights.shape, F32)] + exchange.scratch(),
        compiler_params=pltpu.CompilerParams(
            vmem_limit_bytes=VMEM_LIMIT, collective_id=0, has_side_effects=True
        ),
        name="local",
    )(query, key, value, grad_out, weights, *sums)


def cross_kernel(local_bits, cross_bits, chunks, *refs):
    q_ref, k_ref, v_ref, g_ref, w_ref = refs[:5]
    att_in, dq_in, dk_in, dv_in = refs[5:9]
    gw_in = refs[9 : 9 + chunks]
    states = refs[9 + chunks : 9 + chunks + cross_bits]
    adjoint = refs[9 + chunks + cross_bits]
    att_ref, dq_ref, dk_ref, dv_ref, gw_ref, acc, wr = refs[10 + chunks + cross_bits :]
    head = pl.program_id(0)
    width = w_ref.shape[1]

    @pl.when(head == 0)
    def _():
        total = gw_in[0][...]
        for other in gw_in[1:]:
            total = total + other[...]
        acc[...] = total

    wr[...] = head_weights(w_ref, head)
    read = cat([state[0] for state in states], 0)
    adj = adjoint[0]
    picks = cat([pick(DH, head, local_bits + 1 + j, width) for j in range(cross_bits)], 0)
    tokens = q_ref.shape[0]
    step = min(2 * C, tokens)
    for start in range(0, tokens, step):
        here = slice(start, start + step)
        q32 = q_ref[here, :].astype(F32)
        columns = [
            wr[here, local_bits + 1 + j : local_bits + 2 + j] for j in range(cross_bits)
        ]
        att = att_in[here, :].astype(F32) + nn(cat([(w * q32).astype(BF) for w in columns], 1), read)
        back = nt(g_ref[here, :], read)
        dq = dq_in[here, :].astype(F32)
        marks = []
        for j, w in enumerate(columns):
            part = back[:, j * DH : (j + 1) * DH]
            dq = dq + w * part
            marks.append((q32 * part).astype(BF))
        acc[here, :] += nn(cat(marks, 1), picks)
        att_ref[here, :] = att.astype(BF)
        dq_ref[here, :] = dq.astype(BF)
        dk_ref[here, :] = (dk_in[here, :].astype(F32) + nn(v_ref[here, :], adj)).astype(BF)
        dv_ref[here, :] = (dv_in[here, :].astype(F32) + nt(k_ref[here, :], adj)).astype(BF)

    @pl.when(head == pl.num_programs(0) - 1)
    def _():
        gw_ref[...] = acc[...].astype(BF)


def cross_call(query, key, value, grad_out, weights, partial, gws, states, adjoint, local_bits):
    tokens = query.shape[0]
    heads = query.shape[1] // DH
    cross_bits = len(states)
    column = pl.BlockSpec((tokens, DH), lambda h: (0, h))
    whole = pl.BlockSpec(weights.shape, lambda h: (0, 0))
    square = pl.BlockSpec((1, DH, DH), lambda h: (h, 0, 0))
    return pl.pallas_call(
        functools.partial(cross_kernel, local_bits, cross_bits, len(gws)),
        grid=(heads,),
        in_specs=[column] * 4
        + [whole]
        + [column] * 4
        + [whole] * len(gws)
        + [square] * (cross_bits + 1),
        out_specs=[column] * 4 + [whole],
        out_shape=[jax.ShapeDtypeStruct(query.shape, BF)] * 4
        + [jax.ShapeDtypeStruct(weights.shape, BF)],
        scratch_shapes=[pltpu.VMEM(weights.shape, F32), pltpu.VMEM(weights.shape, F32)],
        compiler_params=pltpu.CompilerParams(vmem_limit_bytes=VMEM_LIMIT),
        name="cross",
    )(query, key, value, grad_out, weights, *partial, *gws, *states, adjoint)


def general(query, key, value, grad_out, weights):
    tokens = query.shape[0]
    heads = query.shape[1] // DH
    local_bits = (tokens // C).bit_length() - 1
    cross_bits = LEVELS - 1 - local_bits
    head_bits = lax.axis_size("head").bit_length() - 1
    sums = sums_call(query, key, value, grad_out, weights, heads, local_bits, cross_bits)
    outs = local_call(query, key, value, grad_out, weights, sums, head_bits)
    partial, gw = outs[:4], outs[4]
    states, adjoint = outs[5 : 5 + cross_bits], outs[5 + cross_bits]
    return tuple(
        cross_call(
            query, key, value, grad_out, weights, partial, [gw], states, adjoint, local_bits
        )
    )


GRID = 4
T_RIGHT, T_NEXT, T_LEFT, A_RIGHT, A_LEFT, A_LEFT2, P_X, H_CORE, U_CORE, U_X0, U_X1 = range(11)
MESSAGES = 11


class Links:
    def __init__(self, heads, chunks, local_bits):
        self.heads, self.chunks, self.count = heads, chunks, heads // chunks
        self.factors = [level_scale(local_bits + 1 + j) for j in range(4)]
        self.stages = [
            (self.totals1, 6, 2),
            (self.totals2, 12, 2),
            (self.totals3, 26, 2),
            (self.across, 30, 2),
            (self.arrive, 34, 2),
            (self.x_exchange, 7, 2),
            (self.core_exchange, 14, 2),
            (self.adjoint1, 20, 2),
            (self.adjoint2, 26, 2),
            (self.adjoint3, 34, 2),
        ]

    def scratch(self):
        return [
            pltpu.VMEM((5, self.heads, DH, DH), BF),
            pltpu.VMEM((self.heads, DH, DH), F32),
            pltpu.VMEM((MESSAGES, self.heads, DH, DH), BF),
            pltpu.VMEM((MESSAGES, self.heads, DH, DH), BF),
            pltpu.SemaphoreType.DMA((MESSAGES,)),
            pltpu.SemaphoreType.DMA((MESSAGES, self.chunks)),
        ]

    def bind(self, states, adjoint, scratch):
        self.states, self.adjoint = states, adjoint
        self.own, self.extra, self.landing, self.sending, self.send_sem, self.recv_sem = scratch
        self.z, self.seq = lax.axis_index("head"), lax.axis_index("seq")
        self.x, self.c = self.seq // 2, self.seq % 2
        z, x, c = self.z, self.x, self.c
        right, left = {"head": z + 1}, {"head": z - 1}
        core = {"seq": x * 2 + 1 - c}
        both = (x == 0) | (c == 0)
        yes = z >= 0
        self.both = both
        self.table = {
            T_RIGHT: (right, z < 3, z > 0),
            T_NEXT: (right, z == 2, z == 3),
            T_LEFT: (left, (z > 0) & both, (z < 3) & both),
            A_RIGHT: (right, (z < 3) & both, (z > 0) & both),
            A_LEFT: (left, z > 0, z < 3),
            A_LEFT2: (left, z == 3, z == 2),
            P_X: ({"seq": c}, x == 1, x == 0),
            H_CORE: (core, (x == 0) | (c == 1), both),
            U_CORE: (core, (c == 0) & yes, c == 1),
            U_X0: ({"seq": 2}, (x == 0) & (c == 1), (x == 1) & (c == 0)),
            U_X1: ({"seq": 3}, (x == 0) & (c == 1), (x == 1) & (c == 1)),
        }

    def greet(self):
        barrier = pltpu.get_barrier_semaphore()
        other = 1 - self.x
        devices = [
            {"head": (self.z + 1) % GRID},
            {"head": (self.z + GRID - 1) % GRID},
            {"seq": self.x * 2 + 1 - self.c},
            {"seq": other * 2 + self.c},
            {"seq": other * 2 + 1 - self.c},
        ]
        for device in devices:
            pl.semaphore_signal(
                barrier, inc=1, device_id=device, device_id_type=pl.DeviceIdType.MESH
            )
        pl.semaphore_wait(barrier, len(devices))

    def part(self, chunk):
        return pl.ds(chunk * self.count, self.count)

    def copy(self, key, chunk, source, part=None):
        part = self.part(chunk) if part is None else part
        return pltpu.make_async_remote_copy(
            src_ref=source.at[part],
            dst_ref=self.landing.at[key, part],
            send_sem=self.send_sem.at[key],
            recv_sem=self.recv_sem.at[key, chunk],
            device_id=self.table[key][0],
            device_id_type=pl.DeviceIdType.MESH,
        )

    def send(self, key, chunk, source, when):
        pl.when(when)(lambda: self.copy(key, chunk, source).start())

    def emit(self, key, chunk, value):
        self.sending[key, self.part(chunk)] = value.astype(BF)
        self.copy(key, chunk, self.sending.at[key]).start()

    def wait(self, chunk, key, when=True):
        receives = self.table[key][2] & when
        pl.when(receives)(lambda: self.copy(key, chunk, self.landing.at[key]).wait_recv())

    def landed(self, key, chunk):
        return self.landing[key, self.part(chunk)].astype(F32)

    def mine(self, index, chunk):
        return self.own[index, self.part(chunk)].astype(F32)

    def first(self, chunk):
        z, x, c = self.z, self.x, self.c
        total = self.own.at[0]
        self.send(T_RIGHT, chunk, total, z == 0)
        self.send(T_NEXT, chunk, total, z == 2)
        self.send(T_LEFT, chunk, total, (z == 3) & self.both)
        self.send(P_X, chunk, self.own.at[4], x == 1)
        self.send(H_CORE, chunk, self.own.at[3], (x == 1) & (c == 1))

    def x_exchange(self, chunk):
        x, c = self.x, self.c
        self.wait(chunk, P_X)
        self.send(H_CORE, chunk, self.landing.at[P_X], (x == 0) & (c == 0))

        @pl.when((x == 0) & (c == 1))
        def _():
            self.emit(H_CORE, chunk, self.mine(3, chunk) + self.landed(P_X, chunk))

    def core_exchange(self, chunk):
        z = self.z
        part = self.part(chunk)
        self.wait(chunk, H_CORE)

        @pl.when(self.both)
        def _():
            value = self.landed(H_CORE, chunk)
            self.extra[part] = value + jnp.where(self.x == 0, self.landed(P_X, chunk), 0.0)

        @pl.when(jnp.logical_not(self.both))
        def _():
            self.extra[part] = jnp.zeros((self.count, DH, DH), F32)

        @pl.when((z == 0) & self.both)
        def _():
            self.emit(A_RIGHT, chunk, self.extra[part])

        @pl.when(z == 3)
        def _():
            self.emit(A_LEFT2, chunk, self.mine(2, chunk) + self.extra[part])

    def forward_right(self, chunk):
        part = self.part(chunk)

        @pl.when(self.both)
        def _():
            self.emit(A_RIGHT, chunk, self.extra[part] + self.landed(A_RIGHT, chunk))

    def forward_left(self, chunk):
        pl.when(self.both)(
            lambda: self.emit(T_LEFT, chunk, self.mine(0, chunk) + self.landed(T_LEFT, chunk))
        )

    def totals1(self, chunk):
        z = self.z
        self.wait(chunk, T_RIGHT, z == 1)
        self.wait(chunk, T_LEFT, z == 2)

        @pl.when(z == 1)
        def _():
            self.emit(T_RIGHT, chunk, self.mine(0, chunk) + self.landed(T_RIGHT, chunk))

        pl.when(z == 2)(lambda: self.forward_left(chunk))

    def totals2(self, chunk):
        z = self.z
        self.wait(chunk, T_RIGHT, z == 2)
        self.wait(chunk, T_LEFT, z == 1)
        self.send(T_RIGHT, chunk, self.landing.at[T_RIGHT], z == 2)
        pl.when(z == 1)(lambda: self.forward_left(chunk))

    def totals3(self, chunk):
        z, c = self.z, self.c
        part = self.part(chunk)
        self.wait(chunk, T_RIGHT, z == 3)
        self.wait(chunk, T_NEXT)
        self.wait(chunk, T_LEFT, z == 0)

        @pl.when(self.both)
        def _():
            value = self.mine(0, chunk)
            value = value + jnp.where(z > 0, self.landed(T_RIGHT, chunk), 0.0)
            value = value + jnp.where(z == 3, self.landed(T_NEXT, chunk), 0.0)
            value = value + jnp.where(z < 3, self.landed(T_LEFT, chunk), 0.0)
            self.sending[U_CORE, part] = value.astype(BF)

        self.send(U_CORE, chunk, self.sending.at[U_CORE], c == 0)

        def read(level, state):
            self.states[part, level * DH : (level + 1) * DH] = state.astype(BF)

        near = jnp.where(z == 1, self.landed(T_RIGHT, chunk), self.landed(T_NEXT, chunk))
        read(0, jnp.where(z % 2 == 1, self.factors[0] * near, 0.0))
        read(1, jnp.where(z >= 2, self.factors[1] * self.landed(T_RIGHT, chunk), 0.0))

    def adjoint1(self, chunk):
        z = self.z
        part = self.part(chunk)
        self.wait(chunk, A_RIGHT, z == 1)
        self.wait(chunk, A_LEFT2)

        @pl.when(z == 3)
        def _():
            self.emit(A_LEFT, chunk, self.mine(1, chunk) + self.extra[part])

        pl.when(z == 1)(lambda: self.forward_right(chunk))

        @pl.when(z == 2)
        def _():
            value = self.mine(2, chunk) + self.extra[part] + self.landed(A_LEFT2, chunk)
            self.emit(A_LEFT, chunk, value)

    def adjoint2(self, chunk):
        z = self.z
        part = self.part(chunk)
        self.wait(chunk, A_RIGHT, z == 2)
        self.wait(chunk, A_LEFT, z == 1)
        pl.when(z == 2)(lambda: self.forward_right(chunk))

        @pl.when(z == 1)
        def _():
            value = self.mine(1, chunk) + self.extra[part] + self.landed(A_LEFT, chunk)
            self.emit(A_LEFT, chunk, value)

    def adjoint3(self, chunk):
        z = self.z
        part = self.part(chunk)
        self.wait(chunk, A_RIGHT, z == 3)
        self.wait(chunk, A_LEFT, z % 2 == 0)
        value = self.extra[part]
        value = value + jnp.where((z > 0) & self.both, self.landed(A_RIGHT, chunk), 0.0)
        value = value + jnp.where(z < 3, self.landed(A_LEFT, chunk), 0.0)
        self.adjoint[part] = value.astype(BF)

    def across(self, chunk):
        part = self.part(chunk)
        self.wait(chunk, U_CORE)
        state = jnp.where(self.c == 1, self.factors[2] * self.landed(U_CORE, chunk), 0.0)
        self.states[part, 2 * DH : 3 * DH] = state.astype(BF)

        @pl.when((self.x == 0) & (self.c == 1))
        def _():
            value = self.sending[U_CORE, part].astype(F32) + self.landed(U_CORE, chunk)
            self.sending[U_X0, part] = value.astype(BF)
            self.copy(U_X0, chunk, self.sending.at[U_X0]).start()
            self.copy(U_X1, chunk, self.sending.at[U_X0]).start()

    def arrive(self, chunk):
        part = self.part(chunk)
        self.wait(chunk, U_X0)
        self.wait(chunk, U_X1)
        state = jnp.where(self.c == 0, self.landed(U_X0, chunk), self.landed(U_X1, chunk))
        state = jnp.where(self.x == 1, self.factors[3] * state, 0.0)
        self.states[part, 3 * DH : 4 * DH] = state.astype(BF)

    def advance(self, time):
        for stage, begin, pace in self.stages:
            late = time - begin
            chunk = jnp.right_shift(late * (8192 // pace + 1), 13)
            last = (self.chunks - 1) * pace

            @pl.when((late >= 0) & (late <= last) & (chunk * pace == late))
            def _(stage=stage, chunk=chunk):
                stage(chunk)

    def last(self):
        return max(begin + (self.chunks - 1) * pace for _, begin, pace in self.stages)

    def drain(self):
        whole = pl.ds(0, self.heads)
        for key, (_, sends, _) in self.table.items():
            pl.when(sends)(
                lambda k=key: self.copy(k, 0, self.landing.at[k], whole).wait_send()
            )


def rows_of_weights(w_ref, wt_ref):
    for start in range(0, w_ref.shape[0], C):
        here = slice(start, start + C)
        wt_ref[:, here] = w_ref[here, :].astype(F32).T


def level_rows(wt_ref, head):
    return wt_ref[pl.ds(pl.multiple_of(head * LEVELS, LEVELS), LEVELS), :]


def stage_kernel(stretches, heads, links, *refs):
    inputs, w_ref = refs[:4], refs[4]
    kept, outs, states_out, adjoint_out = refs[5:9], refs[9:14], refs[14], refs[15]
    natural, turned = refs[16:20], refs[20:24]
    wt, wq, load_sem, keep_sem = refs[24:28]
    links.bind(states_out, adjoint_out, refs[28:])
    keeps = [
        pltpu.make_async_copy(source, target, keep_sem.at[i])
        for i, (source, target) in enumerate(
            zip((turned[0], turned[3], natural[1], natural[2]), kept)
        )
    ]
    step = pl.program_id(0)
    head = lax.rem(step, heads)

    def load(i, h):
        return pltpu.make_async_copy(
            inputs[i].at[:, pl.ds(pl.multiple_of(h * DH, DH), DH)],
            natural[i].at[h],
            load_sem.at[i, h],
        )

    @pl.when(step == 0)
    def _():
        def start(h, carry):
            for i in range(4):
                load(i, h).start()
            return carry

        lax.fori_loop(0, heads, start, 0)
        rows_of_weights(w_ref, wt)
        links.greet()

    weight = level_rows(wt, head)
    here = [ref.at[head] for ref in natural], [ref.at[head] for ref in turned]

    @pl.when(step < heads)
    def _():
        links.advance(step)
        for i in range(4):
            load(i, head).wait()
        sums_part(stretches, head, weight, *here, wq, links)

        @pl.when(head % links.count == links.count - 1)
        def _():
            links.first(head // links.count)

    @pl.when(step >= heads)
    def _():
        @pl.when(step == heads)
        def _():
            for keep in keeps:
                keep.start()

        slot = 2 * step - heads
        links.advance(slot)
        local_part(stretches, weight, *here, outs, lambda: links.advance(slot + 1))

    @pl.when(step == pl.num_programs(0) - 1)
    def _():
        def late(time, carry):
            links.advance(time)
            return carry

        for keep in keeps:
            keep.wait()
        lax.fori_loop(3 * heads, max(3 * heads, links.last() + 1), late, 0)
        links.drain()


def sums_part(stretches, head, weight, natural, turned, wq, links):
    local_bits = stretches.bit_length() - 1
    spans = [slice(start, start + 2 * C) for start in range(0, stretches * C, 2 * C)]
    for here in spans:
        flat = natural[0][here, :].T
        turned[0][:, here] = flat
        for j in range(4):
            row = weight[local_bits + 1 + j : local_bits + 2 + j, here]
            wq[j * DH : (j + 1) * DH, here] = (row * flat.astype(F32)).astype(BF)
        turned[3][:, here] = natural[3][here, :].T
    out = nt(turned[3][...], wq[...])
    for here in spans:
        turned[1][:, here] = natural[1][here, :].T
    links.own[0, head] = nn(turned[1][...], natural[2][...]).astype(BF)
    for j in range(4):
        links.own[1 + j, head] = (links.factors[j] * out[:, j * DH : (j + 1) * DH]).astype(BF)


def local_part(stretches, weight, natural, turned, outs, between):
    q_ref, k_ref, v_ref, g_ref = natural
    qt_ref, kt_ref, vt_ref, gt_ref = turned
    att_ref, dq_ref, dk_ref, dv_ref, gw_ref = outs
    local_bits = stretches.bit_length() - 1

    def here(n, count=1):
        return slice(n * C, (n + count) * C)

    def levels(n):
        return [b for b in range(local_bits) if n >> b & 1]

    sums = {}
    for n in range(stretches - 1):
        sums[0, n] = nn(kt_ref[:, here(n)], v_ref[here(n), :])
    for b in range(1, local_bits):
        for m in range(stretches >> b):
            if (b - 1, 2 * m + 1) in sums:
                sums[b, m] = sums[b - 1, 2 * m] + sums[b - 1, 2 * m + 1]
    states, flipped, adjoints, wq = {}, {}, {}, {}
    for b in range(local_bits):
        for group in range(stretches >> (b + 1)):
            state = (level_scale(b + 1) * sums[b, 2 * group]).astype(BF)
            states[b, group], flipped[b, group] = state, state.T
            first, count = (2 * group + 1) << b, 1 << b
            for n in range(first, first + count):
                row = weight[b + 1 : b + 2, here(n)]
                wq[b, n] = (row * qt_ref[:, here(n)].astype(F32)).astype(BF)
            across = cat([wq[b, n] for n in range(first, first + count)], 1)
            adjoints[b, group] = level_scale(b + 1) * nn(across, g_ref[here(first, count), :])

    row = lax.broadcasted_iota(jnp.int32, (C, C), 0)
    col = lax.broadcasted_iota(jnp.int32, (C, C), 1)
    mask = jnp.where(row <= col, level_scale(0), 0.0).astype(F32)
    ready = {}
    for n in range(stretches):
        bits = levels(n)
        scores = nn(k_ref[here(n), :], qt_ref[:, here(n)]) * mask
        vt_ref[:, here(n)] = v_ref[here(n), :].T
        rows = cat([v_ref[here(n), :]] + [states[b, n >> (b + 1)] for b in bits], 0)
        seen = nn(rows, gt_ref[:, here(n)])
        grads = seen[:C]
        w0 = weight[0:1, here(n)]
        gws = {0: jnp.sum(scores * grads, axis=0, keepdims=True)}
        extra = 0.0
        for i, b in enumerate(bits):
            back = seen[C + i * DH : C + (i + 1) * DH]
            extra = extra + weight[b + 1 : b + 2, here(n)] * back
            qt32 = qt_ref[:, here(n)].astype(F32)
            gws[b + 1] = jnp.sum(qt32 * back, axis=0, keepdims=True)
        zero = jnp.zeros((1, C), F32)
        gw_ref[0, :, here(n)] = jnp.concatenate([gws.get(l, zero) for l in range(LEVELS)], 0)
        ready[n] = (scores * w0).astype(BF), (grads * mask * w0).astype(BF), extra
    between()
    for n in range(stretches):
        bits = levels(n)
        q, k, v, g = (ref[here(n), :] for ref in natural)
        probs, gscores, extra = ready[n]
        left = [vt_ref[:, here(n)]] + [flipped[b, n >> (b + 1)] for b in bits]
        att = nn(cat(left, 1), cat([probs] + [wq[b, n] for b in bits], 0))
        dq = nn(kt_ref[:, here(n)], gscores) + extra
        terms = [adjoints[b, n >> (b + 1)] for b in range(local_bits) if b not in bits]
        if terms:
            adjoint = sum(terms[1:], terms[0]).astype(BF)
            dk = nn(cat([gscores, v], 1), cat([q, adjoint.T], 0))
            dv = nn(cat([probs, k], 1), cat([g, adjoint], 0))
        else:
            dk, dv = nn(gscores, q), nn(probs, g)
        att_ref[0, :, here(n)] = att.astype(BF)
        dq_ref[0, :, here(n)] = dq.astype(BF)
        dk_ref[0, here(n), :] = dk.astype(BF)
        dv_ref[0, here(n), :] = dv.astype(BF)


def stage_call(query, key, value, grad_out, weights):
    tokens = query.shape[0]
    stretches, heads = tokens // C, query.shape[1] // DH
    links = Links(heads, heads // 2, stretches.bit_length() - 1)

    def block(*shape):
        return pl.BlockSpec((1,) + shape, lambda s: (jnp.maximum(s - heads, 0), 0, 0))

    shapes = [(DH, tokens)] * 2 + [(tokens, DH)] * 2 + [(LEVELS, tokens)]
    types = [BF] * 4 + [F32]
    small = [(heads, 4 * DH, DH), (heads, DH, DH)]
    large = [(heads,) + shape for shape in shapes[:4]]
    return pl.pallas_call(
        functools.partial(stage_kernel, stretches, heads, links),
        grid=(2 * heads,),
        in_specs=[pl.BlockSpec(memory_space=pl.ANY)] * 4
        + [pl.BlockSpec(weights.shape, lambda s: (0, 0))],
        out_specs=[pl.BlockSpec(memory_space=pl.ANY)] * 4
        + [block(*shape) for shape in shapes]
        + [pl.BlockSpec(shape, lambda s: (0, 0, 0)) for shape in small],
        out_shape=[jax.ShapeDtypeStruct(shape, BF) for shape in large]
        + [jax.ShapeDtypeStruct((heads,) + shape, kind) for shape, kind in zip(shapes, types)]
        + [jax.ShapeDtypeStruct(shape, BF) for shape in small],
        scratch_shapes=[pltpu.VMEM((heads, tokens, DH), BF)] * 4
        + [pltpu.VMEM((heads, DH, tokens), BF)] * 4
        + [
            pltpu.VMEM(weights.shape[::-1], F32),
            pltpu.VMEM((4 * DH, tokens), BF),
            pltpu.SemaphoreType.DMA((4, heads)),
            pltpu.SemaphoreType.DMA((4,)),
        ]
        + links.scratch(),
        compiler_params=pltpu.CompilerParams(
            vmem_limit_bytes=VMEM_LIMIT, collective_id=1, has_side_effects=True
        ),
        name="stage",
    )(query, key, value, grad_out, weights)


def merge_kernel(pair, local_bits, *refs):
    near, gw_in, states_ref, adjoint_ref, w_ref = refs[:8], *refs[8:12]
    outs, gw_ref, wt, gwt = refs[12:16], *refs[16:]
    step = pl.program_id(0)

    @pl.when(step == 0)
    def _():
        rows_of_weights(w_ref, wt)

    for i in range(pair):
        head = step * pair + i
        rows = pl.ds(pl.multiple_of(head * LEVELS, LEVELS), LEVELS)
        merge_part(
            local_bits, level_rows(wt, head), [ref.at[i] for ref in near], gw_in[i],
            states_ref[i], adjoint_ref[i], outs, slice(i * DH, (i + 1) * DH), gwt.at[rows],
        )

    @pl.when(step == pl.num_programs(0) - 1)
    def _():
        for start in range(0, w_ref.shape[0], C):
            here = slice(start, start + C)
            gw_ref[here, :] = gwt[:, here].T.astype(BF)


def merge_part(local_bits, weight, near, gw_in, states, adjoint, outs, lanes, gwt):
    qt_ref, gt_ref, k_ref, v_ref, att_in, dq_in, dk_in, dv_in = near
    att_ref, dq_ref, dk_ref, dv_ref = outs
    flipped = cat([states[j * DH : (j + 1) * DH, :].T for j in range(4)], 1)
    back_adjoint = adjoint.T
    for start in range(0, k_ref.shape[0], 2 * C):
        here = slice(start, start + 2 * C)
        qt32 = qt_ref[:, here].astype(F32)
        levels = [weight[local_bits + 1 + j : local_bits + 2 + j, here] for j in range(4)]
        wq = cat([(row * qt32).astype(BF) for row in levels], 0)
        att = att_in[:, here].astype(F32) + nn(flipped, wq)
        back = nn(states, gt_ref[:, here])
        dq = dq_in[:, here].astype(F32)
        gws = [gw_in[0 : local_bits + 1, here]]
        for j, row in enumerate(levels):
            part = back[j * DH : (j + 1) * DH, :]
            dq = dq + row * part
            gws.append(jnp.sum(qt32 * part, axis=0, keepdims=True))
        gwt[:, here] = jnp.concatenate(gws, 0)
        att_ref[here, lanes] = att.astype(BF).T
        dq_ref[here, lanes] = dq.astype(BF).T
        dk = dk_in[here, :].astype(F32) + nn(v_ref[here, :], adjoint)
        dv = dv_in[here, :].astype(F32) + nn(k_ref[here, :], back_adjoint)
        dk_ref[here, lanes] = dk.astype(BF)
        dv_ref[here, lanes] = dv.astype(BF)


def merge_call(weights, outs, local_bits):
    heads, tokens = outs[0].shape[0], weights.shape[0]
    pair = 4
    column = pl.BlockSpec((tokens, pair * DH), lambda s: (0, s))
    whole = pl.BlockSpec(weights.shape, lambda s: (0, 0))

    def block(array):
        return pl.BlockSpec((pair,) + array.shape[1:], lambda s: (s, 0, 0))

    return pl.pallas_call(
        functools.partial(merge_kernel, pair, local_bits),
        grid=(heads // pair,),
        in_specs=[block(array) for array in outs] + [whole],
        out_specs=[column] * 4 + [whole],
        out_shape=[jax.ShapeDtypeStruct((tokens, heads * DH), BF)] * 4
        + [jax.ShapeDtypeStruct(weights.shape, BF)],
        scratch_shapes=[pltpu.VMEM(weights.shape[::-1], F32)] * 2,
        compiler_params=pltpu.CompilerParams(vmem_limit_bytes=VMEM_LIMIT),
        name="merge",
    )(*outs, weights)


def shards(query, key, value, grad_out, weights):
    local_bits = (query.shape[0] // C).bit_length() - 1
    square = lax.axis_size("head") == GRID and lax.axis_size("seq") == GRID
    if not square or local_bits != LEVELS - 5:
        return general(query, key, value, grad_out, weights)
    outs = stage_call(query, key, value, grad_out, weights)
    return tuple(merge_call(weights, outs, local_bits))


def solution(mesh):
    spec = P(("rep", "seq", "head"), None)
    return jax.shard_map(
        shards, mesh=mesh, in_specs=(spec,) * 5, out_specs=(spec,) * 5, check_vma=False
    )
```

```python
import functools
import math

import jax
import jax.numpy as jnp
from jax import lax
from jax.experimental import pallas as pl
from jax.experimental.pallas import tpu as pltpu
from jax.sharding import PartitionSpec as P

DH = 128
C = 128
LEVELS = 8
VMEM_LIMIT = 60 * 2**20
BF = jnp.bfloat16
F32 = jnp.float32


def level_scale(level):
    if level == 0:
        return 1.0 / math.sqrt(DH * C)
    return 1.0 / math.sqrt(DH * C * 2 ** (level - 1))


def nn(a, b):
    return lax.dot_general(a, b, (((1,), (0,)), ((), ())), preferred_element_type=F32)


def nt(a, b):
    return lax.dot_general(a, b, (((1,), (1,)), ((), ())), preferred_element_type=F32)


def tn(a, b):
    return lax.dot_general(a, b, (((0,), (0,)), ((), ())), preferred_element_type=F32)


def cat(parts, axis):
    return parts[0] if len(parts) == 1 else jnp.concatenate(parts, axis=axis)


def head_weights(w_ref, head):
    width = w_ref.shape[1]
    return pltpu.roll(w_ref[...].astype(F32), lax.rem(width - head * LEVELS, width), 1)


def pick(rows, head, level, width):
    lane = lax.broadcasted_iota(jnp.int32, (rows, width), 1)
    return jnp.where(lane == head * LEVELS + level, 1.0, 0.0).astype(BF)


def sums_kernel(local_bits, q_ref, k_ref, v_ref, g_ref, w_ref, t_ref, *rest):
    p_refs, wr = rest[:-1], rest[-1]
    head = pl.program_id(0)
    wr[...] = head_weights(w_ref, head)
    t_ref[0] = tn(k_ref[...], v_ref[...]).astype(BF)
    q = q_ref[...].astype(F32)
    weighted = [
        (wr[:, local_bits + 1 + j : local_bits + 2 + j] * q).astype(BF) for j in range(len(p_refs))
    ]
    out = tn(g_ref[...], cat(weighted, 1))
    for j, p_ref in enumerate(p_refs):
        p_ref[0] = out[:, j * DH : (j + 1) * DH].astype(BF)


def sums_call(query, key, value, grad_out, weights, heads, local_bits, cross_bits):
    tokens = query.shape[0]
    column = pl.BlockSpec((tokens, DH), lambda h: (0, h))
    square = pl.BlockSpec((1, DH, DH), lambda h: (h, 0, 0))
    outs = [jax.ShapeDtypeStruct((heads, DH, DH), BF)] * (1 + cross_bits)
    return pl.pallas_call(
        functools.partial(sums_kernel, local_bits),
        grid=(heads,),
        in_specs=[column] * 4 + [pl.BlockSpec(weights.shape, lambda h: (0, 0))],
        out_specs=[square] * (1 + cross_bits),
        out_shape=outs,
        scratch_shapes=[pltpu.VMEM(weights.shape, F32)],
        compiler_params=pltpu.CompilerParams(vmem_limit_bytes=VMEM_LIMIT),
        name="sums",
    )(query, key, value, grad_out, weights)


class Exchange:
    def __init__(self, local_bits, cross_bits, head_bits, heads, chunks):
        self.local_bits, self.cross_bits, self.head_bits = local_bits, cross_bits, head_bits
        self.chunks, self.count, self.heads = chunks, heads // chunks, heads
        self.size = 1 << head_bits
        low, high = range(head_bits), range(head_bits, cross_bits)
        self.low, self.high = low, high
        landing = [("R", i) for i in low] + [("PR", j) for j in high]
        landing += [("L", i) for i in low] + [("TL", 0)] + [("PL", j) for j in high]
        landing += [("T", i) for i in high] + [(("P", j), i) for j in high for i in high if i <= j]
        sending = [("TR", 0)] + [("PR", j) for j in high]
        sending += [("L", i) for i in low] + [("TL", 0)] + [("PL", j) for j in high]
        sending += [("T", i) for i in high] + [(("P", j), i) for j in high for i in high if i <= j]
        self.lands = {key: n for n, key in enumerate(landing)}
        self.sends = {key: n for n, key in enumerate(sending)}
        self.last_time = chunks - 1 + self.size + 1 + 2 * (len(high) - 1)

    def scratch(self):
        sems = pltpu.SemaphoreType.DMA((len(self.lands), self.chunks))
        return [
            pltpu.VMEM((len(self.lands), self.heads, DH, DH), BF),
            pltpu.VMEM((len(self.sends), self.heads, DH, DH), BF),
            pltpu.VMEM((self.heads, DH, DH), F32),
            sems,
            sems,
        ]

    def bind(self, sources, states, adjoint, scratch):
        self.total, self.products = sources[0], sources[1:]
        self.states, self.adjoint = states, adjoint
        self.landing, self.sending, self.sum, self.send_sem, self.recv_sem = scratch
        self.z, seq = lax.axis_index("head"), lax.axis_index("seq")
        self.bit = []
        for i in range(self.cross_bits):
            position, stride = self.z, 1 << i
            if i >= self.head_bits:
                position, stride = seq, 1 << (i - self.head_bits)
            self.bit.append((position // stride) % 2)
        self.partner = {
            i: {"seq": seq + (1 - 2 * self.bit[i]) * (1 << (i - self.head_bits))}
            for i in self.high
        }
        self.right, self.left = {"head": self.z + 1}, {"head": self.z - 1}
        self.has_right, self.has_left = self.z < self.size - 1, self.z > 0

    def part(self, chunk):
        return pl.ds(chunk * self.count, self.count)

    def landed(self, key, chunk):
        return self.landing[self.lands[key], self.part(chunk)].astype(F32)

    def store(self, key, chunk, value):
        self.sending[self.sends[key], self.part(chunk)] = value.astype(BF)

    def copy(self, key, chunk, device, source=None):
        slot = self.lands[key]
        if source is None:
            source = self.sending.at[self.sends[key]]
        return pltpu.make_async_remote_copy(
            src_ref=source.at[self.part(chunk)],
            dst_ref=self.landing.at[slot, self.part(chunk)],
            send_sem=self.send_sem.at[slot, chunk],
            recv_sem=self.recv_sem.at[slot, chunk],
            device_id=device,
            device_id_type=pl.DeviceIdType.MESH,
        )

    def transfers(self):
        for i in self.low:
            yield ("R", i), self.right, self.has_right & (((self.z + 1) >> i) % 2 == 1), self.bit[i] == 1
        for j in self.high:
            own = self.bit[j] == 1
            yield ("PR", j), self.right, self.has_right & own, self.has_left & own
        for i in self.low:
            block = self.z % (2 << i)
            yield ("L", i), self.left, block != 0, block != (2 << i) - 1
        yield ("TL", 0), self.left, self.has_left, self.has_right
        for j in self.high:
            own = self.bit[j] == 1
            yield ("PL", j), self.left, self.has_left & own, self.has_right & own
        for i in self.high:
            up, down, always = self.bit[i] == 1, self.bit[i] == 0, self.bit[i] >= 0
            last = i == self.cross_bits - 1
            yield ("T", i), self.partner[i], (down if last else always), (up if last else always)
            yield (("P", i), i), self.partner[i], up, down
            for j in range(i + 1, self.cross_bits):
                own = self.bit[j] == 1
                yield (("P", j), i), self.partner[i], own, own

    def greet(self):
        barrier = pltpu.get_barrier_semaphore()

        def signal(device):
            pl.semaphore_signal(
                barrier, inc=1, device_id=device, device_id_type=pl.DeviceIdType.MESH
            )

        for i in self.high:
            signal(self.partner[i])
        signal({"head": lax.rem(self.z + 1, self.size)})
        signal({"head": lax.rem(self.z + self.size - 1, self.size)})
        pl.semaphore_wait(barrier, len(self.high) + 2)

    def wait(self, chunk, kinds):
        for key, device, _, receives in self.transfers():
            if key in kinds:
                own = self.landing.at[self.lands[key]]
                pl.when(receives)(
                    lambda k=key, d=device, r=own: self.copy(k, chunk, d, r).wait_recv()
                )

    def start(self, chunk, kinds):
        for key, device, sends, _ in self.transfers():
            if key in kinds:
                pl.when(sends)(lambda k=key, d=device: self.copy(k, chunk, d).start())

    def chain(self, key, chunk, own, receives):
        @pl.when(receives)
        def _():
            self.store(key, chunk, own.astype(F32) + self.landed(key, chunk))

        @pl.when(jnp.logical_not(receives))
        def _():
            self.store(key, chunk, own)

    def rightward(self, chunk):
        part = self.part(chunk)
        self.wait(chunk, [("R", i) for i in self.low] + [("PR", j) for j in self.high])
        for i in self.low:
            @pl.when(self.z % (2 << i) == (1 << i) - 1)
            def _(i=i):
                value = self.total[part].astype(F32)
                for k in range(i):
                    value = value + self.landed(("R", k), chunk)
                self.store(("TR", 0), chunk, value)
                self.copy(
                    ("R", i), chunk, self.right, self.sending.at[self.sends["TR", 0]]
                ).start()

            @pl.when((self.bit[i] == 1) & (self.z % (1 << i) != (1 << i) - 1))
            def _(i=i):
                self.copy(
                    ("R", i), chunk, self.right, self.landing.at[self.lands["R", i]]
                ).start()

        for j in self.high:

            @pl.when((self.bit[j] == 1) & self.has_right)
            def _(j=j):
                self.chain(("PR", j), chunk, self.products[j][part], self.has_left)

        self.start(chunk, [("PR", j) for j in self.high])

    def leftward(self, chunk):
        part = self.part(chunk)
        keys = [("L", i) for i in self.low] + [("TL", 0)] + [("PL", j) for j in self.high]
        self.wait(chunk, keys)
        for i in self.low:
            block = self.z % (2 << i)

            @pl.when(self.bit[i] == 1)
            def _(i=i, block=block):
                self.chain(("L", i), chunk, self.products[i][part], block != (2 << i) - 1)
                self.copy(("L", i), chunk, self.left).start()

            @pl.when((self.bit[i] == 0) & (block != 0))
            def _(i=i):
                self.copy(("L", i), chunk, self.left, self.landing.at[self.lands["L", i]]).start()

        @pl.when(self.has_left)
        def _():
            self.chain(("TL", 0), chunk, self.total[part], self.has_right)

        for j in self.high:

            @pl.when((self.bit[j] == 1) & self.has_left)
            def _(j=j):
                self.chain(("PL", j), chunk, self.products[j][part], self.has_right)

        self.start(chunk, [("TL", 0)] + [("PL", j) for j in self.high])

    def add(self, key, chunk, source, receives, first=None):
        @pl.when(receives)
        def _():
            base = self.sending[self.sends[first or key], self.part(chunk)].astype(F32)
            self.store(key, chunk, base + self.landed(source, chunk))

    def read(self, i, chunk, state, term):
        part = self.part(chunk)
        factor = level_scale(self.local_bits + i + 1)

        @pl.when(self.bit[i] == 1)
        def _():
            self.states[i][part] = (factor * self.landed(state, chunk)).astype(BF)

        @pl.when(self.bit[i] == 0)
        def _():
            self.states[i][part] = jnp.zeros((self.count, DH, DH), BF)
            self.sum[part] += factor * self.landed(term, chunk)

    def cross(self, chunk):
        part = self.part(chunk)
        self.sum[part] = jnp.zeros((self.count, DH, DH), F32)
        for i in self.low:
            self.read(i, chunk, ("R", i), ("L", i))
        first = self.head_bits
        value = self.total[part].astype(F32)
        for i in self.low:
            value = value + jnp.where(self.bit[i] == 1, self.landed(("R", i), chunk), 0.0)
        value = value + jnp.where(self.has_right, self.landed(("TL", 0), chunk), 0.0)
        self.store(("T", first), chunk, value)
        for j in self.high:

            @pl.when(self.bit[j] == 1)
            def _(j=j):
                value = self.products[j][part].astype(F32)
                value = value + jnp.where(self.has_left, self.landed(("PR", j), chunk), 0.0)
                value = value + jnp.where(self.has_right, self.landed(("PL", j), chunk), 0.0)
                self.store((("P", j), first), chunk, value)

        self.start(chunk, [("T", first)] + [(("P", j), first) for j in self.high])

    def arrive(self, i, chunk):
        part = self.part(chunk)
        above = range(i + 1, self.cross_bits)
        self.wait(chunk, [("T", i), (("P", i), i)] + [(("P", j), i) for j in above])
        if len(above):
            self.add(("T", i + 1), chunk, ("T", i), self.bit[i] >= 0, ("T", i))
            for j in above:
                self.add((("P", j), i + 1), chunk, (("P", j), i), self.bit[j] == 1, (("P", j), i))
            self.start(chunk, [("T", i + 1)] + [(("P", j), i + 1) for j in above])
        self.read(i, chunk, ("T", i), (("P", i), i))
        if not len(above):
            self.adjoint[part] = self.sum[part].astype(BF)

    def advance(self, time):
        def at(offset, event):
            chunk = time - offset

            @pl.when((chunk >= 0) & (chunk < self.chunks))
            def _():
                event(chunk)

        at(self.z, self.rightward)
        at(self.size - 1 - self.z, self.leftward)
        at(self.size - 1, self.cross)
        for i in self.high:
            at(self.size + 1 + 2 * (i - self.head_bits), functools.partial(self.arrive, i))

    def finish(self, steps):
        def late(time, carry):
            self.advance(time)
            return carry

        if self.last_time >= steps:
            lax.fori_loop(steps, self.last_time + 1, late, 0)

        def body(chunk, carry):
            for key, device, sends, _ in self.transfers():
                source = self.landing.at[self.lands[key]]
                pl.when(sends)(
                    lambda k=key, d=device, r=source: self.copy(k, chunk, d, r).wait_send()
                )
            return carry

        lax.fori_loop(0, self.chunks, body, 0)


def local_kernel(stretches, exchange, *refs):
    cross_bits = exchange.cross_bits
    q_ref, k_ref, v_ref, g_ref, w_ref = refs[:5]
    sources = refs[5 : 6 + cross_bits]
    outs = refs[6 + cross_bits :]
    att_ref, dq_ref, dk_ref, dv_ref, gw_ref = outs[:5]
    states_out = outs[5 : 5 + cross_bits]
    adjoint_out, wr = outs[5 + cross_bits : 7 + cross_bits]
    exchange.bind(sources, states_out, adjoint_out, outs[7 + cross_bits :])
    step = pl.program_id(0)
    head = step
    local_bits = stretches.bit_length() - 1
    width = w_ref.shape[1]

    @pl.when(step == 0)
    def _():
        gw_ref[...] = jnp.zeros_like(gw_ref)

    pl.when(step == 0)(exchange.greet)
    exchange.advance(step)
    wr[...] = head_weights(w_ref, head)

    def rows(ref, n, count=1):
        return ref[n * C : (n + count) * C, :]

    def weighted(n, level):
        return (wr[n * C : (n + 1) * C, level : level + 1] * rows(q_ref, n).astype(F32)).astype(BF)

    sums = {}
    for n in range(stretches - 1):
        sums[0, n] = tn(rows(k_ref, n), rows(v_ref, n))
    for b in range(1, local_bits):
        for m in range(stretches >> b):
            if (b - 1, 2 * m + 1) in sums:
                sums[b, m] = sums[b - 1, 2 * m] + sums[b - 1, 2 * m + 1]
    states, adjoints, wq = {}, {}, {}
    for b in range(local_bits):
        for group in range(stretches >> (b + 1)):
            states[b, group] = (level_scale(b + 1) * sums[b, 2 * group]).astype(BF)
            first = (2 * group + 1) << b
            for n in range(first, first + (1 << b)):
                wq[b, n] = weighted(n, b + 1)
            up = cat([wq[b, n] for n in range(first, first + (1 << b))], 0)
            adjoints[b, group] = level_scale(b + 1) * tn(rows(g_ref, first, 1 << b), up)

    row = lax.broadcasted_iota(jnp.int32, (C, C), 0)
    col = lax.broadcasted_iota(jnp.int32, (C, C), 1)
    mask = jnp.where(col <= row, level_scale(0), 0.0).astype(F32)
    for n in range(stretches):
        q, k, v, g = (rows(ref, n) for ref in (q_ref, k_ref, v_ref, g_ref))
        here = slice(n * C, (n + 1) * C)
        bits = [b for b in range(local_bits) if n >> b & 1]
        read = [states[b, n >> (b + 1)] for b in bits]
        scores = nt(q, k) * mask
        grads = nt(g, v)
        w0 = wr[here, 0:1]
        probs = (w0 * scores).astype(BF)
        gscores = (w0 * (grads * mask)).astype(BF)
        att = nn(cat([probs] + [wq[b, n] for b in bits], 1), cat([v] + read, 0))
        dq = nn(gscores, k)
        marks = [(scores * grads).astype(BF)]
        q32 = q.astype(F32)
        for b, state in zip(bits, read):
            back = nt(g, state)
            dq = dq + wr[here, b + 1 : b + 2] * back
            marks.append((q32 * back).astype(BF))
        picks = [pick(C, head, level, width) for level in [0] + [b + 1 for b in bits]]
        gw_ref[here, :] += nn(cat(marks, 1), cat(picks, 0))
        dk = tn(gscores, q)
        dv = tn(probs, g)
        adjoint = None
        for b in range(local_bits):
            if not n >> b & 1:
                term = adjoints[b, n >> (b + 1)]
                adjoint = term if adjoint is None else adjoint + term
        if adjoint is not None:
            adjoint = adjoint.astype(BF)
            dk = dk + nn(v, adjoint)
            dv = dv + nt(k, adjoint)
        att_ref[here, :] = att.astype(BF)
        dq_ref[here, :] = dq.astype(BF)
        dk_ref[here, :] = dk.astype(BF)
        dv_ref[here, :] = dv.astype(BF)

    @pl.when(step == pl.num_programs(0) - 1)
    def _():
        exchange.finish(exchange.heads)


def local_call(query, key, value, grad_out, weights, sums, head_bits):
    tokens = query.shape[0]
    stretches = tokens // C
    heads = query.shape[1] // DH
    cross_bits = len(sums) - 1
    exchange = Exchange(stretches.bit_length() - 1, cross_bits, head_bits, heads, heads // 2)
    column = pl.BlockSpec((tokens, DH), lambda h: (0, h))
    whole = pl.BlockSpec(weights.shape, lambda h: (0, 0))
    squares = pl.BlockSpec((heads, DH, DH), lambda h: (0, 0, 0))
    shape = jax.ShapeDtypeStruct(query.shape, BF)
    square = jax.ShapeDtypeStruct((heads, DH, DH), BF)
    return pl.pallas_call(
        functools.partial(local_kernel, stretches, exchange),
        grid=(heads,),
        in_specs=[column] * 4 + [whole] + [squares] * (cross_bits + 1),
        out_specs=[column] * 4 + [whole] + [squares] * (cross_bits + 1),
        out_shape=[shape] * 4
        + [jax.ShapeDtypeStruct(weights.shape, F32)]
        + [square] * (cross_bits + 1),
        scratch_shapes=[pltpu.VMEM(weights.shape, F32)] + exchange.scratch(),
        compiler_params=pltpu.CompilerParams(
            vmem_limit_bytes=VMEM_LIMIT, collective_id=0, has_side_effects=True
        ),
        name="local",
    )(query, key, value, grad_out, weights, *sums)


def cross_kernel(local_bits, cross_bits, chunks, *refs):
    q_ref, k_ref, v_ref, g_ref, w_ref = refs[:5]
    att_in, dq_in, dk_in, dv_in = refs[5:9]
    gw_in = refs[9 : 9 + chunks]
    states = refs[9 + chunks : 9 + chunks + cross_bits]
    adjoint = refs[9 + chunks + cross_bits]
    att_ref, dq_ref, dk_ref, dv_ref, gw_ref, acc, wr = refs[10 + chunks + cross_bits :]
    head = pl.program_id(0)
    width = w_ref.shape[1]

    @pl.when(head == 0)
    def _():
        total = gw_in[0][...]
        for other in gw_in[1:]:
            total = total + other[...]
        acc[...] = total

    wr[...] = head_weights(w_ref, head)
    read = cat([state[0] for state in states], 0)
    adj = adjoint[0]
    picks = cat([pick(DH, head, local_bits + 1 + j, width) for j in range(cross_bits)], 0)
    tokens = q_ref.shape[0]
    step = min(2 * C, tokens)
    for start in range(0, tokens, step):
        here = slice(start, start + step)
        q32 = q_ref[here, :].astype(F32)
        columns = [
            wr[here, local_bits + 1 + j : local_bits + 2 + j] for j in range(cross_bits)
        ]
        att = att_in[here, :].astype(F32) + nn(cat([(w * q32).astype(BF) for w in columns], 1), read)
        back = nt(g_ref[here, :], read)
        dq = dq_in[here, :].astype(F32)
        marks = []
        for j, w in enumerate(columns):
            part = back[:, j * DH : (j + 1) * DH]
            dq = dq + w * part
            marks.append((q32 * part).astype(BF))
        acc[here, :] += nn(cat(marks, 1), picks)
        att_ref[here, :] = att.astype(BF)
        dq_ref[here, :] = dq.astype(BF)
        dk_ref[here, :] = (dk_in[here, :].astype(F32) + nn(v_ref[here, :], adj)).astype(BF)
        dv_ref[here, :] = (dv_in[here, :].astype(F32) + nt(k_ref[here, :], adj)).astype(BF)

    @pl.when(head == pl.num_programs(0) - 1)
    def _():
        gw_ref[...] = acc[...].astype(BF)


def cross_call(query, key, value, grad_out, weights, partial, gws, states, adjoint, local_bits):
    tokens = query.shape[0]
    heads = query.shape[1] // DH
    cross_bits = len(states)
    column = pl.BlockSpec((tokens, DH), lambda h: (0, h))
    whole = pl.BlockSpec(weights.shape, lambda h: (0, 0))
    square = pl.BlockSpec((1, DH, DH), lambda h: (h, 0, 0))
    return pl.pallas_call(
        functools.partial(cross_kernel, local_bits, cross_bits, len(gws)),
        grid=(heads,),
        in_specs=[column] * 4
        + [whole]
        + [column] * 4
        + [whole] * len(gws)
        + [square] * (cross_bits + 1),
        out_specs=[column] * 4 + [whole],
        out_shape=[jax.ShapeDtypeStruct(query.shape, BF)] * 4
        + [jax.ShapeDtypeStruct(weights.shape, BF)],
        scratch_shapes=[pltpu.VMEM(weights.shape, F32), pltpu.VMEM(weights.shape, F32)],
        compiler_params=pltpu.CompilerParams(vmem_limit_bytes=VMEM_LIMIT),
        name="cross",
    )(query, key, value, grad_out, weights, *partial, *gws, *states, adjoint)


def general(query, key, value, grad_out, weights):
    tokens = query.shape[0]
    heads = query.shape[1] // DH
    local_bits = (tokens // C).bit_length() - 1
    cross_bits = LEVELS - 1 - local_bits
    head_bits = lax.axis_size("head").bit_length() - 1
    sums = sums_call(query, key, value, grad_out, weights, heads, local_bits, cross_bits)
    outs = local_call(query, key, value, grad_out, weights, sums, head_bits)
    partial, gw = outs[:4], outs[4]
    states, adjoint = outs[5 : 5 + cross_bits], outs[5 + cross_bits]
    return tuple(
        cross_call(
            query, key, value, grad_out, weights, partial, [gw], states, adjoint, local_bits
        )
    )


GRID = 4
T_RIGHT, T_NEXT, T_LEFT, A_RIGHT, A_LEFT, A_LEFT2, P_X, H_CORE, U_CORE, U_X0, U_X1 = range(11)
MESSAGES = 11


class Links:
    def __init__(self, heads, chunks, local_bits):
        self.heads, self.chunks, self.count = heads, chunks, heads // chunks
        self.factors = [level_scale(local_bits + 1 + j) for j in range(4)]
        self.stages = [
            (self.totals1, 6, 2),
            (self.totals2, 12, 2),
            (self.totals3, 26, 2),
            (self.across, 30, 2),
            (self.arrive, 34, 2),
            (self.x_exchange, 7, 2),
            (self.core_exchange, 14, 2),
            (self.adjoint1, 20, 2),
            (self.adjoint2, 26, 2),
            (self.adjoint3, 34, 2),
        ]

    def scratch(self):
        return [
            pltpu.VMEM((5, self.heads, DH, DH), BF),
            pltpu.VMEM((self.heads, DH, DH), F32),
            pltpu.VMEM((MESSAGES, self.heads, DH, DH), BF),
            pltpu.VMEM((MESSAGES, self.heads, DH, DH), BF),
            pltpu.SemaphoreType.DMA((MESSAGES,)),
            pltpu.SemaphoreType.DMA((MESSAGES, self.chunks)),
        ]

    def bind(self, states, adjoint, scratch):
        self.states, self.adjoint = states, adjoint
        self.own, self.extra, self.landing, self.sending, self.send_sem, self.recv_sem = scratch
        self.z, self.seq = lax.axis_index("head"), lax.axis_index("seq")
        self.x, self.c = self.seq // 2, self.seq % 2
        z, x, c = self.z, self.x, self.c
        right, left = {"head": z + 1}, {"head": z - 1}
        core = {"seq": x * 2 + 1 - c}
        both = (x == 0) | (c == 0)
        yes = z >= 0
        self.both = both
        self.table = {
            T_RIGHT: (right, z < 3, z > 0),
            T_NEXT: (right, z == 2, z == 3),
            T_LEFT: (left, (z > 0) & both, (z < 3) & both),
            A_RIGHT: (right, (z < 3) & both, (z > 0) & both),
            A_LEFT: (left, z > 0, z < 3),
            A_LEFT2: (left, z == 3, z == 2),
            P_X: ({"seq": c}, x == 1, x == 0),
            H_CORE: (core, (x == 0) | (c == 1), both),
            U_CORE: (core, (c == 0) & yes, c == 1),
            U_X0: ({"seq": 2}, (x == 0) & (c == 1), (x == 1) & (c == 0)),
            U_X1: ({"seq": 3}, (x == 0) & (c == 1), (x == 1) & (c == 1)),
        }

    def greet(self):
        barrier = pltpu.get_barrier_semaphore()
        other = 1 - self.x
        devices = [
            {"head": (self.z + 1) % GRID},
            {"head": (self.z + GRID - 1) % GRID},
            {"seq": self.x * 2 + 1 - self.c},
            {"seq": other * 2 + self.c},
            {"seq": other * 2 + 1 - self.c},
        ]
        for device in devices:
            pl.semaphore_signal(
                barrier, inc=1, device_id=device, device_id_type=pl.DeviceIdType.MESH
            )
        pl.semaphore_wait(barrier, len(devices))

    def part(self, chunk):
        return pl.ds(chunk * self.count, self.count)

    def copy(self, key, chunk, source, part=None):
        part = self.part(chunk) if part is None else part
        return pltpu.make_async_remote_copy(
            src_ref=source.at[part],
            dst_ref=self.landing.at[key, part],
            send_sem=self.send_sem.at[key],
            recv_sem=self.recv_sem.at[key, chunk],
            device_id=self.table[key][0],
            device_id_type=pl.DeviceIdType.MESH,
        )

    def send(self, key, chunk, source, when):
        pl.when(when)(lambda: self.copy(key, chunk, source).start())

    def emit(self, key, chunk, value):
        self.sending[key, self.part(chunk)] = value.astype(BF)
        self.copy(key, chunk, self.sending.at[key]).start()

    def wait(self, chunk, key, when=True):
        receives = self.table[key][2] & when
        pl.when(receives)(lambda: self.copy(key, chunk, self.landing.at[key]).wait_recv())

    def landed(self, key, chunk):
        return self.landing[key, self.part(chunk)].astype(F32)

    def mine(self, index, chunk):
        return self.own[index, self.part(chunk)].astype(F32)

    def first(self, chunk):
        z, x, c = self.z, self.x, self.c
        total = self.own.at[0]
        self.send(T_RIGHT, chunk, total, z == 0)
        self.send(T_NEXT, chunk, total, z == 2)
        self.send(T_LEFT, chunk, total, (z == 3) & self.both)
        self.send(P_X, chunk, self.own.at[4], x == 1)
        self.send(H_CORE, chunk, self.own.at[3], (x == 1) & (c == 1))

    def x_exchange(self, chunk):
        x, c = self.x, self.c
        self.wait(chunk, P_X)
        self.send(H_CORE, chunk, self.landing.at[P_X], (x == 0) & (c == 0))

        @pl.when((x == 0) & (c == 1))
        def _():
            self.emit(H_CORE, chunk, self.mine(3, chunk) + self.landed(P_X, chunk))

    def core_exchange(self, chunk):
        z = self.z
        part = self.part(chunk)
        self.wait(chunk, H_CORE)

        @pl.when(self.both)
        def _():
            value = self.landed(H_CORE, chunk)
            self.extra[part] = value + jnp.where(self.x == 0, self.landed(P_X, chunk), 0.0)

        @pl.when(jnp.logical_not(self.both))
        def _():
            self.extra[part] = jnp.zeros((self.count, DH, DH), F32)

        @pl.when((z == 0) & self.both)
        def _():
            self.emit(A_RIGHT, chunk, self.extra[part])

        @pl.when(z == 3)
        def _():
            self.emit(A_LEFT2, chunk, self.mine(2, chunk) + self.extra[part])

    def forward_right(self, chunk):
        part = self.part(chunk)

        @pl.when(self.both)
        def _():
            self.emit(A_RIGHT, chunk, self.extra[part] + self.landed(A_RIGHT, chunk))

    def forward_left(self, chunk):
        pl.when(self.both)(
            lambda: self.emit(T_LEFT, chunk, self.mine(0, chunk) + self.landed(T_LEFT, chunk))
        )

    def totals1(self, chunk):
        z = self.z
        self.wait(chunk, T_RIGHT, z == 1)
        self.wait(chunk, T_LEFT, z == 2)

        @pl.when(z == 1)
        def _():
            self.emit(T_RIGHT, chunk, self.mine(0, chunk) + self.landed(T_RIGHT, chunk))

        pl.when(z == 2)(lambda: self.forward_left(chunk))

    def totals2(self, chunk):
        z = self.z
        self.wait(chunk, T_RIGHT, z == 2)
        self.wait(chunk, T_LEFT, z == 1)
        self.send(T_RIGHT, chunk, self.landing.at[T_RIGHT], z == 2)
        pl.when(z == 1)(lambda: self.forward_left(chunk))

    def totals3(self, chunk):
        z, c = self.z, self.c
        part = self.part(chunk)
        self.wait(chunk, T_RIGHT, z == 3)
        self.wait(chunk, T_NEXT)
        self.wait(chunk, T_LEFT, z == 0)

        @pl.when(self.both)
        def _():
            value = self.mine(0, chunk)
            value = value + jnp.where(z > 0, self.landed(T_RIGHT, chunk), 0.0)
            value = value + jnp.where(z == 3, self.landed(T_NEXT, chunk), 0.0)
            value = value + jnp.where(z < 3, self.landed(T_LEFT, chunk), 0.0)
            self.sending[U_CORE, part] = value.astype(BF)

        self.send(U_CORE, chunk, self.sending.at[U_CORE], c == 0)

        def read(level, state):
            self.states[part, level * DH : (level + 1) * DH] = state.astype(BF)

        pl.when(z == 1)(lambda: read(0, self.factors[0] * self.landed(T_RIGHT, chunk)))
        pl.when(z == 3)(lambda: read(0, self.factors[0] * self.landed(T_NEXT, chunk)))
        pl.when(z >= 2)(lambda: read(1, self.factors[1] * self.landed(T_RIGHT, chunk)))

    def adjoint1(self, chunk):
        z = self.z
        part = self.part(chunk)
        self.wait(chunk, A_RIGHT, z == 1)
        self.wait(chunk, A_LEFT2)

        @pl.when(z == 3)
        def _():
            self.emit(A_LEFT, chunk, self.mine(1, chunk) + self.extra[part])

        pl.when(z == 1)(lambda: self.forward_right(chunk))

        @pl.when(z == 2)
        def _():
            value = self.mine(2, chunk) + self.extra[part] + self.landed(A_LEFT2, chunk)
            self.emit(A_LEFT, chunk, value)

    def adjoint2(self, chunk):
        z = self.z
        part = self.part(chunk)
        self.wait(chunk, A_RIGHT, z == 2)
        self.wait(chunk, A_LEFT, z == 1)
        pl.when(z == 2)(lambda: self.forward_right(chunk))

        @pl.when(z == 1)
        def _():
            value = self.mine(1, chunk) + self.extra[part] + self.landed(A_LEFT, chunk)
            self.emit(A_LEFT, chunk, value)

    def adjoint3(self, chunk):
        z = self.z
        part = self.part(chunk)
        self.wait(chunk, A_RIGHT, z == 3)
        self.wait(chunk, A_LEFT, z % 2 == 0)
        value = self.extra[part]
        value = value + jnp.where((z > 0) & self.both, self.landed(A_RIGHT, chunk), 0.0)
        value = value + jnp.where(z < 3, self.landed(A_LEFT, chunk), 0.0)
        self.adjoint[part] = value.astype(BF)

    def across(self, chunk):
        part = self.part(chunk)
        self.wait(chunk, U_CORE)

        @pl.when(self.c == 1)
        def _():
            state = self.factors[2] * self.landed(U_CORE, chunk)
            self.states[part, 2 * DH : 3 * DH] = state.astype(BF)

        @pl.when((self.x == 0) & (self.c == 1))
        def _():
            value = self.sending[U_CORE, part].astype(F32) + self.landed(U_CORE, chunk)
            self.sending[U_X0, part] = value.astype(BF)
            self.copy(U_X0, chunk, self.sending.at[U_X0]).start()
            self.copy(U_X1, chunk, self.sending.at[U_X0]).start()

    def arrive(self, chunk):
        part = self.part(chunk)
        self.wait(chunk, U_X0)
        self.wait(chunk, U_X1)
        for core, key in enumerate((U_X0, U_X1)):

            @pl.when((self.x == 1) & (self.c == core))
            def _(key=key):
                state = self.factors[3] * self.landed(key, chunk)
                self.states[part, 3 * DH : 4 * DH] = state.astype(BF)

    def advance(self, time):
        for stage, begin, pace in self.stages:
            late = time - begin
            chunk = jnp.right_shift(late * (8192 // pace + 1), 13)
            last = (self.chunks - 1) * pace

            @pl.when((late >= 0) & (late <= last) & (chunk * pace == late))
            def _(stage=stage, chunk=chunk):
                stage(chunk)

    def last(self):
        return max(begin + (self.chunks - 1) * pace for _, begin, pace in self.stages)

    def drain(self):
        whole = pl.ds(0, self.heads)
        for key, (_, sends, _) in self.table.items():
            pl.when(sends)(
                lambda k=key: self.copy(k, 0, self.landing.at[k], whole).wait_send()
            )


def rows_of_weights(w_ref, wt_ref):
    for start in range(0, w_ref.shape[0], C):
        here = slice(start, start + C)
        wt_ref[:, here] = w_ref[here, :].astype(F32).T


def level_rows(wt_ref, head):
    return wt_ref[pl.ds(pl.multiple_of(head * LEVELS, LEVELS), LEVELS), :]


def stage_kernel(stretches, heads, links, *refs):
    inputs, w_ref = refs[:4], refs[4]
    kept, outs, states_out, adjoint_out = refs[5:9], refs[9:14], refs[14], refs[15]
    natural, turned = refs[16:20], refs[20:24]
    wt, wq, load_sem, keep_sem = refs[24:28]
    links.bind(states_out, adjoint_out, refs[28:])
    keeps = [
        pltpu.make_async_copy(source, target, keep_sem.at[i])
        for i, (source, target) in enumerate(
            zip((turned[0], turned[3], natural[1], natural[2]), kept)
        )
    ]
    step = pl.program_id(0)
    head = lax.rem(step, heads)

    def load(i, h):
        return pltpu.make_async_copy(
            inputs[i].at[:, pl.ds(pl.multiple_of(h * DH, DH), DH)],
            natural[i].at[h],
            load_sem.at[i, h],
        )

    @pl.when(step == 0)
    def _():
        def start(h, carry):
            for i in range(4):
                load(i, h).start()
            return carry

        lax.fori_loop(0, heads, start, 0)
        rows_of_weights(w_ref, wt)
        states_out[...] = jnp.zeros_like(states_out)
        links.greet()

    weight = level_rows(wt, head)
    here = [ref.at[head] for ref in natural], [ref.at[head] for ref in turned]

    @pl.when(step < heads)
    def _():
        links.advance(step)
        for i in range(4):
            load(i, head).wait()
        sums_part(stretches, head, weight, *here, wq, links)

        @pl.when(head % links.count == links.count - 1)
        def _():
            links.first(head // links.count)

    @pl.when(step >= heads)
    def _():
        @pl.when(step == heads)
        def _():
            for keep in keeps:
                keep.start()

        slot = 2 * step - heads
        links.advance(slot)
        local_part(stretches, weight, *here, outs, lambda: links.advance(slot + 1))

    @pl.when(step == pl.num_programs(0) - 1)
    def _():
        def late(time, carry):
            links.advance(time)
            return carry

        for keep in keeps:
            keep.wait()
        lax.fori_loop(3 * heads, max(3 * heads, links.last() + 1), late, 0)
        links.drain()


def sums_part(stretches, head, weight, natural, turned, wq, links):
    local_bits = stretches.bit_length() - 1
    spans = [slice(start, start + 2 * C) for start in range(0, stretches * C, 2 * C)]
    for here in spans:
        flat = natural[0][here, :].T
        turned[0][:, here] = flat
        for j in range(4):
            row = weight[local_bits + 1 + j : local_bits + 2 + j, here]
            wq[j * DH : (j + 1) * DH, here] = (row * flat.astype(F32)).astype(BF)
        turned[3][:, here] = natural[3][here, :].T
    out = nt(turned[3][...], wq[...])
    for here in spans:
        turned[1][:, here] = natural[1][here, :].T
    links.own[0, head] = nn(turned[1][...], natural[2][...]).astype(BF)
    for j in range(4):
        links.own[1 + j, head] = (links.factors[j] * out[:, j * DH : (j + 1) * DH]).astype(BF)


def local_part(stretches, weight, natural, turned, outs, between):
    q_ref, k_ref, v_ref, g_ref = natural
    qt_ref, kt_ref, vt_ref, gt_ref = turned
    att_ref, dq_ref, dk_ref, dv_ref, gw_ref = outs
    local_bits = stretches.bit_length() - 1

    def here(n, count=1):
        return slice(n * C, (n + count) * C)

    def levels(n):
        return [b for b in range(local_bits) if n >> b & 1]

    sums = {}
    for n in range(stretches - 1):
        sums[0, n] = nn(kt_ref[:, here(n)], v_ref[here(n), :])
    for b in range(1, local_bits):
        for m in range(stretches >> b):
            if (b - 1, 2 * m + 1) in sums:
                sums[b, m] = sums[b - 1, 2 * m] + sums[b - 1, 2 * m + 1]
    states, flipped, adjoints, wq = {}, {}, {}, {}
    for b in range(local_bits):
        for group in range(stretches >> (b + 1)):
            state = (level_scale(b + 1) * sums[b, 2 * group]).astype(BF)
            states[b, group], flipped[b, group] = state, state.T
            first, count = (2 * group + 1) << b, 1 << b
            for n in range(first, first + count):
                row = weight[b + 1 : b + 2, here(n)]
                wq[b, n] = (row * qt_ref[:, here(n)].astype(F32)).astype(BF)
            across = cat([wq[b, n] for n in range(first, first + count)], 1)
            adjoints[b, group] = level_scale(b + 1) * nn(across, g_ref[here(first, count), :])

    row = lax.broadcasted_iota(jnp.int32, (C, C), 0)
    col = lax.broadcasted_iota(jnp.int32, (C, C), 1)
    mask = jnp.where(row <= col, level_scale(0), 0.0).astype(F32)
    ready = {}
    for n in range(stretches):
        bits = levels(n)
        scores = nn(k_ref[here(n), :], qt_ref[:, here(n)]) * mask
        vt_ref[:, here(n)] = v_ref[here(n), :].T
        rows = cat([v_ref[here(n), :]] + [states[b, n >> (b + 1)] for b in bits], 0)
        seen = nn(rows, gt_ref[:, here(n)])
        grads = seen[:C]
        w0 = weight[0:1, here(n)]
        gws = {0: jnp.sum(scores * grads, axis=0, keepdims=True)}
        extra = 0.0
        for i, b in enumerate(bits):
            back = seen[C + i * DH : C + (i + 1) * DH]
            extra = extra + weight[b + 1 : b + 2, here(n)] * back
            qt32 = qt_ref[:, here(n)].astype(F32)
            gws[b + 1] = jnp.sum(qt32 * back, axis=0, keepdims=True)
        zero = jnp.zeros((1, C), F32)
        gw_ref[0, :, here(n)] = jnp.concatenate([gws.get(l, zero) for l in range(LEVELS)], 0)
        ready[n] = (scores * w0).astype(BF), (grads * mask * w0).astype(BF), extra
    between()
    for n in range(stretches):
        bits = levels(n)
        q, k, v, g = (ref[here(n), :] for ref in natural)
        probs, gscores, extra = ready[n]
        left = [vt_ref[:, here(n)]] + [flipped[b, n >> (b + 1)] for b in bits]
        att = nn(cat(left, 1), cat([probs] + [wq[b, n] for b in bits], 0))
        dq = nn(kt_ref[:, here(n)], gscores) + extra
        terms = [adjoints[b, n >> (b + 1)] for b in range(local_bits) if b not in bits]
        if terms:
            adjoint = sum(terms[1:], terms[0]).astype(BF)
            dk = nn(cat([gscores, v], 1), cat([q, adjoint.T], 0))
            dv = nn(cat([probs, k], 1), cat([g, adjoint], 0))
        else:
            dk, dv = nn(gscores, q), nn(probs, g)
        att_ref[0, :, here(n)] = att.astype(BF)
        dq_ref[0, :, here(n)] = dq.astype(BF)
        dk_ref[0, here(n), :] = dk.astype(BF)
        dv_ref[0, here(n), :] = dv.astype(BF)


def stage_call(query, key, value, grad_out, weights):
    tokens = query.shape[0]
    stretches, heads = tokens // C, query.shape[1] // DH
    links = Links(heads, heads // 2, stretches.bit_length() - 1)

    def block(*shape):
        return pl.BlockSpec((1,) + shape, lambda s: (jnp.maximum(s - heads, 0), 0, 0))

    shapes = [(DH, tokens)] * 2 + [(tokens, DH)] * 2 + [(LEVELS, tokens)]
    types = [BF] * 4 + [F32]
    small = [(heads, 4 * DH, DH), (heads, DH, DH)]
    large = [(heads,) + shape for shape in shapes[:4]]
    return pl.pallas_call(
        functools.partial(stage_kernel, stretches, heads, links),
        grid=(2 * heads,),
        in_specs=[pl.BlockSpec(memory_space=pl.ANY)] * 4
        + [pl.BlockSpec(weights.shape, lambda s: (0, 0))],
        out_specs=[pl.BlockSpec(memory_space=pl.ANY)] * 4
        + [block(*shape) for shape in shapes]
        + [pl.BlockSpec(shape, lambda s: (0, 0, 0)) for shape in small],
        out_shape=[jax.ShapeDtypeStruct(shape, BF) for shape in large]
        + [jax.ShapeDtypeStruct((heads,) + shape, kind) for shape, kind in zip(shapes, types)]
        + [jax.ShapeDtypeStruct(shape, BF) for shape in small],
        scratch_shapes=[pltpu.VMEM((heads, tokens, DH), BF)] * 4
        + [pltpu.VMEM((heads, DH, tokens), BF)] * 4
        + [
            pltpu.VMEM(weights.shape[::-1], F32),
            pltpu.VMEM((4 * DH, tokens), BF),
            pltpu.SemaphoreType.DMA((4, heads)),
            pltpu.SemaphoreType.DMA((4,)),
        ]
        + links.scratch(),
        compiler_params=pltpu.CompilerParams(
            vmem_limit_bytes=VMEM_LIMIT, collective_id=1, has_side_effects=True
        ),
        name="stage",
    )(query, key, value, grad_out, weights)


def merge_kernel(pair, local_bits, *refs):
    near, gw_in, states_ref, adjoint_ref, w_ref = refs[:8], *refs[8:12]
    outs, gw_ref, wt, gwt = refs[12:16], *refs[16:]
    step = pl.program_id(0)

    @pl.when(step == 0)
    def _():
        rows_of_weights(w_ref, wt)

    for i in range(pair):
        head = step * pair + i
        rows = pl.ds(pl.multiple_of(head * LEVELS, LEVELS), LEVELS)
        merge_part(
            local_bits, level_rows(wt, head), [ref.at[i] for ref in near], gw_in[i],
            states_ref[i], adjoint_ref[i], outs, slice(i * DH, (i + 1) * DH), gwt.at[rows],
        )

    @pl.when(step == pl.num_programs(0) - 1)
    def _():
        for start in range(0, w_ref.shape[0], C):
            here = slice(start, start + C)
            gw_ref[here, :] = gwt[:, here].T.astype(BF)


def merge_part(local_bits, weight, near, gw_in, states, adjoint, outs, lanes, gwt):
    qt_ref, gt_ref, k_ref, v_ref, att_in, dq_in, dk_in, dv_in = near
    att_ref, dq_ref, dk_ref, dv_ref = outs
    flipped = cat([states[j * DH : (j + 1) * DH, :].T for j in range(4)], 1)
    back_adjoint = adjoint.T
    for start in range(0, k_ref.shape[0], 2 * C):
        here = slice(start, start + 2 * C)
        qt32 = qt_ref[:, here].astype(F32)
        levels = [weight[local_bits + 1 + j : local_bits + 2 + j, here] for j in range(4)]
        wq = cat([(row * qt32).astype(BF) for row in levels], 0)
        att = att_in[:, here].astype(F32) + nn(flipped, wq)
        back = nn(states, gt_ref[:, here])
        dq = dq_in[:, here].astype(F32)
        gws = [gw_in[0 : local_bits + 1, here]]
        for j, row in enumerate(levels):
            part = back[j * DH : (j + 1) * DH, :]
            dq = dq + row * part
            gws.append(jnp.sum(qt32 * part, axis=0, keepdims=True))
        gwt[:, here] = jnp.concatenate(gws, 0)
        att_ref[here, lanes] = att.astype(BF).T
        dq_ref[here, lanes] = dq.astype(BF).T
        dk = dk_in[here, :].astype(F32) + nn(v_ref[here, :], adjoint)
        dv = dv_in[here, :].astype(F32) + nn(k_ref[here, :], back_adjoint)
        dk_ref[here, lanes] = dk.astype(BF)
        dv_ref[here, lanes] = dv.astype(BF)


def merge_call(weights, outs, local_bits):
    heads, tokens = outs[0].shape[0], weights.shape[0]
    pair = 4
    column = pl.BlockSpec((tokens, pair * DH), lambda s: (0, s))
    whole = pl.BlockSpec(weights.shape, lambda s: (0, 0))

    def block(array):
        return pl.BlockSpec((pair,) + array.shape[1:], lambda s: (s, 0, 0))

    return pl.pallas_call(
        functools.partial(merge_kernel, pair, local_bits),
        grid=(heads // pair,),
        in_specs=[block(array) for array in outs] + [whole],
        out_specs=[column] * 4 + [whole],
        out_shape=[jax.ShapeDtypeStruct((tokens, heads * DH), BF)] * 4
        + [jax.ShapeDtypeStruct(weights.shape, BF)],
        scratch_shapes=[pltpu.VMEM(weights.shape[::-1], F32)] * 2,
        compiler_params=pltpu.CompilerParams(vmem_limit_bytes=VMEM_LIMIT),
        name="merge",
    )(*outs, weights)


def shards(query, key, value, grad_out, weights):
    local_bits = (query.shape[0] // C).bit_length() - 1
    square = lax.axis_size("head") == GRID and lax.axis_size("seq") == GRID
    if not square or local_bits != LEVELS - 5:
        return general(query, key, value, grad_out, weights)
    outs = stage_call(query, key, value, grad_out, weights)
    return tuple(merge_call(weights, outs, local_bits))


def solution(mesh):
    spec = P(("rep", "seq", "head"), None)
    return jax.shard_map(
        shards, mesh=mesh, in_specs=(spec,) * 5, out_specs=(spec,) * 5, check_vma=False
    )
```
